32 devices in a mesh: grp: 4 (over y, core), fsdp: 8 (over z, x).
Axes of the slice: x: 2, y: 2, z: 4, core: 2. Of those that a mesh axis runs over, the one named last changes fastest.
Arguments:
- tokens: bfloat16 [64, 512, 768], P('grp', 'fsdp'), may hold values from -6 to 6
- frames: bfloat16 [64, 1536, 768], P('grp', 'fsdp'), may hold values from -6 to 6
- lengths: int32 [64], P('grp'), may hold values from 1 to 448, as said below
- cotangent: bfloat16 [64, 512, 768], P('grp', 'fsdp'), may hold values from -6 to 6
- self_in: bfloat16 [768, 2304], P(('grp', 'fsdp')), may hold values from -0.21875 to 0.21875
- self_out: bfloat16 [768, 768], P(('grp', 'fsdp')), may hold values from -1.75 to 1.75
- cross_q: bfloat16 [768, 768], P(('grp', 'fsdp')), may hold values from -0.21875 to 0.21875
- cross_kv: bfloat16 [768, 1536], P(('grp', 'fsdp')), may hold values from -0.21875 to 0.21875
- cross_out: bfloat16 [768, 768], P(('grp', 'fsdp')), may hold values from -1.75 to 1.75
- fc_in: bfloat16 [768, 3072], P(('grp', 'fsdp')), may hold values from -0.21875 to 0.21875
- fc_out: bfloat16 [3072, 768], P(('grp', 'fsdp')), may hold values from -0.109375 to 0.109375
- norm_gain: bfloat16 [768, 4], P(('grp', 'fsdp')), may hold values from 0.25 to 1.75
- norm_bias: bfloat16 [768, 4], P(('grp', 'fsdp')), may hold values from -3 to 3
Outputs:
- output: bfloat16 [64, 512, 768], P('grp', 'fsdp')
- grad_tokens: bfloat16 [64, 512, 768], P('grp', 'fsdp')
- grad_frames: bfloat16 [64, 1536, 768], P('grp', 'fsdp')
- grad_self_in: float32 [768, 2304], P(('grp', 'fsdp'))
- grad_self_out: float32 [768, 768], P(('grp', 'fsdp'))
- grad_cross_q: float32 [768, 768], P(('grp', 'fsdp'))
- grad_cross_kv: float32 [768, 1536], P(('grp', 'fsdp'))
- grad_cross_out: float32 [768, 768], P(('grp', 'fsdp'))
- grad_fc_in: float32 [768, 3072], P(('grp', 'fsdp'))
- grad_fc_out: float32 [3072, 768], P(('grp', 'fsdp'))
- grad_norm_gain: float32 [768, 4], P(('grp', 'fsdp'))
- grad_norm_bias: float32 [768, 4], P(('grp', 'fsdp'))
The draws below stay inside these ranges and needn't reach their ends.
Inputs may be any that keep to these rules, and one draw needn't show every extreme that they name: `lengths`: each group of 16 sequences that one index of grp holds has one sequence of exactly 448 tokens; slots from a sequence's length on are padding.
All inputs are finite; a program needn't handle non-finite values.
Results may differ from the reference program's by a relative error of at most 0.02.
Values may be sent and summed in bfloat16 or wider, within the bound.
No kernel may reach another device: no remote copies, remote signals or barrier semaphores. Data moves between devices by JAX's collectives and lax.ppermute only.
A program may use at most 512 MiB of HBM per device.

```python
import jax
import jax.numpy as jnp
from jax import lax

D = 768
FF = 3072
HEAD_DIM = 64
FRAMES = 1500
MAXLEN = 448
LMAX = 512
FRAME_SLOTS = 1536
SEQ_GRP = 16
SEQS = 64


def draw_lengths(key, part):
    group_total = SEQS // SEQ_GRP
    drawn_len = jax.random.randint(jax.random.fold_in(key, 11), (group_total, SEQ_GRP), 1, MAXLEN + 1)
    longest = jax.random.randint(jax.random.fold_in(key, 12), (group_total, 1), 0, SEQ_GRP)
    positions = jnp.arange(SEQ_GRP, dtype=jnp.int32)[None, :]
    return jnp.where(positions == longest, MAXLEN, drawn_len).reshape(SEQS).astype(jnp.int32)


def block_scale(key, extent, shards, smallest, largest):
    level = 1.0
    for position, shards_of in shards:
        steps = jax.random.uniform(jax.random.fold_in(jax.random.fold_in(key, 6), position), (shards_of,), jnp.float32, smallest / len(shards), largest / len(shards))
        level = level * jnp.repeat(jnp.exp(steps), extent[position] // shards_of).reshape((-1,) + (1,) * (len(extent) - 1 - position))
    return level


def scatter_about(rng, shape, width, limit, shards=(), kind=jnp.bfloat16):
    values = jax.random.normal(rng, shape, jnp.float32) * width
    if len(shards) > 0:
        values = block_scale(rng, shape, shards, -0.22, 0.18) * values
    return jnp.clip(values, min=-limit, max=limit).astype(kind)


def setup_inputs(seed: int = 0) -> dict:
    key_of = jax.random.split(jax.random.key(seed), 14)
    return {
        "tokens": scatter_about(key_of[0], (SEQS, LMAX, D), 1.0, 6.0, ((0, 4), (1, 8))),
        "frames": scatter_about(key_of[1], (SEQS, FRAME_SLOTS, D), 1.0, 6.0, ((0, 4), (1, 8))),
        "lengths": draw_lengths(jax.random.fold_in(key_of[13], 71), 0),
        "cotangent": scatter_about(key_of[3], (SEQS, LMAX, D), 1.0, 6.0, ((0, 4), (1, 8))),
        "self_in": scatter_about(key_of[4], (D, 3 * D), D ** -0.5, 0.21875, ((0, 32),)),
        "self_out": scatter_about(key_of[5], (D, D), (D // 64) ** -0.5, 1.75, ((0, 32),)),
        "cross_q": scatter_about(key_of[6], (D, D), D ** -0.5, 0.21875, ((0, 32),)),
        "cross_kv": scatter_about(key_of[7], (D, 2 * D), D ** -0.5, 0.21875, ((0, 32),)),
        "cross_out": scatter_about(key_of[8], (D, D), (D // 64) ** -0.5, 1.75, ((0, 32),)),
        "fc_in": scatter_about(key_of[9], (D, FF), D ** -0.5, 0.21875, ((0, 32),)),
        "fc_out": scatter_about(key_of[10], (FF, D), FF ** -0.5, 0.109375, ((0, 32),)),
        "norm_gain": jnp.clip(1.0 + 0.15 * jax.random.normal(key_of[11], (D, 4), jnp.float32), 0.25, 1.75).astype(jnp.bfloat16),
        "norm_bias": scatter_about(key_of[12], (D, 4), 0.3, 3.0, ((0, 32),)),
    }


@jax.custom_vjp
def low(v):
    return lax.optimization_barrier(v.astype(jnp.bfloat16)).astype(jnp.float32)

@jax.custom_vjp
def low_back(v):
    return v

def low_keep(v):
    return (low(v), None)

def low_pass(kept, grad):
    return (grad,)

def back_keep(v):
    return (v, None)

def back_low(kept, grad):
    return (low(grad),)
low.defvjp(low_keep, low_pass)
low_back.defvjp(back_keep, back_low)
eps_norm = 1e-05
neg_big = -1e+30
head_scale = 0.125
highest = lax.Precision.HIGHEST

def matmul(left_side, right_side):
    return jnp.dot(left_side, right_side, precision=highest)

def layer_norm(inputs, gain_vec, shift_vec):
    average = lax.optimization_barrier(jnp.mean(inputs, axis=-1, keepdims=True))
    centered = inputs - average
    variance = lax.optimization_barrier(jnp.mean(centered * centered, axis=-1, keepdims=True))
    return centered * lax.rsqrt(variance + eps_norm) * gain_vec + shift_vec

def exact_gelu(inputs):
    return jax.nn.gelu(inputs, approximate=False)

def attend(queries, key_vecs, value_vecs, allowed):
    query_count = queries.shape[0]
    key_count = key_vecs.shape[0]
    head_count = queries.shape[1] // HEAD_DIM
    query_heads = queries.reshape(query_count, head_count, HEAD_DIM)
    key_heads = key_vecs.reshape(key_count, head_count, HEAD_DIM)
    value_heads = value_vecs.reshape(key_count, head_count, HEAD_DIM)
    scores = low_back(jnp.einsum('qhd,khd->hqk', query_heads, key_heads, precision=highest))
    scores = jnp.where(allowed[None], scores, neg_big)
    peak_score = lax.optimization_barrier(jnp.max(scores, axis=-1, keepdims=True))
    exp_scores = jnp.exp(scores - peak_score)
    softmaxed = low(exp_scores / lax.optimization_barrier(jnp.sum(exp_scores, axis=-1, keepdims=True)))
    mixture = jnp.einsum('hqk,khd->qhd', softmaxed, value_heads, precision=highest)
    return mixture.reshape(query_count, head_count * HEAD_DIM)

def decoder_layer(inputs, encoder, seq_len, params):
    self_in, self_out, cross_q, cross_kv, cross_out, fc_in, fc_out, norm_gain, norm_bias = params
    seq_rows = inputs.shape[0]
    slot_count = encoder.shape[0]
    model_width = inputs.shape[1]
    row_ids = lax.broadcasted_iota(jnp.int32, (seq_rows, seq_rows), 0)
    col_ids = lax.broadcasted_iota(jnp.int32, (seq_rows, seq_rows), 1)
    allowed = (col_ids <= row_ids) & (col_ids < seq_len)
    frame_allowed = lax.broadcasted_iota(jnp.int32, (seq_rows, slot_count), 1) < FRAMES
    valid_rows = (lax.broadcasted_iota(jnp.int32, (seq_rows, 1), 0) < seq_len).astype(inputs.dtype)
    normed_one = low(layer_norm(inputs, norm_gain[:, 0], norm_bias[:, 0]))
    projected = matmul(normed_one, self_in)
    queries = low(low_back(projected[:, :model_width] * head_scale))
    key_vecs = low(low_back(projected[:, model_width:2 * model_width]))
    value_vecs = low(low_back(projected[:, 2 * model_width:]))
    mixture = low(low_back(attend(queries, key_vecs, value_vecs, allowed)))
    after_self = inputs + low_back(matmul(mixture, self_out))
    normed_two = low(layer_norm(after_self, norm_gain[:, 1], norm_bias[:, 1]))
    queries_two = low(low_back(matmul(normed_two, cross_q) * head_scale))
    frame_proj = matmul(encoder, cross_kv)
    frame_keys = low(low_back(frame_proj[:, :model_width]))
    frame_values = low(low_back(frame_proj[:, model_width:]))
    mixture_two = low(low_back(attend(queries_two, frame_keys, frame_values, frame_allowed)))
    after_cross = after_self + low_back(matmul(mixture_two, cross_out))
    normed_three = low(layer_norm(after_cross, norm_gain[:, 2], norm_bias[:, 2]))
    hidden = low(exact_gelu(low_back(matmul(normed_three, fc_in))))
    after_mlp = after_cross + low_back(matmul(hidden, fc_out))
    return layer_norm(after_mlp, norm_gain[:, 3], norm_bias[:, 3]) * valid_rows

def reference(tokens, frames, lengths, cotangent, self_in, self_out, cross_q, cross_kv, cross_out, fc_in, fc_out, norm_gain, norm_bias):
    params = tuple((weight.astype(jnp.float32) for weight in (self_in, self_out, cross_q, cross_kv, cross_out, fc_in, fc_out, norm_gain, norm_bias)))

    def per_sequence(totals, stacked):
        seq_tokens, seq_frames, seq_len, seq_grad = stacked

        def layer_of(inputs, encoder, weights):
            return decoder_layer(inputs, encoder, seq_len, weights)
        result, pullback = jax.vjp(layer_of, seq_tokens.astype(jnp.float32), seq_frames.astype(jnp.float32), params)
        grad_inputs, grad_encoder, grad_params = pullback(seq_grad.astype(jnp.float32))
        totals = jax.tree.map(lambda summed, addend: summed + addend, totals, grad_params)
        return (totals, (result.astype(jnp.bfloat16), grad_inputs.astype(jnp.bfloat16), grad_encoder.astype(jnp.bfloat16)))
    start_grads = tuple((jnp.zeros_like(weight) for weight in params))
    totals, stacked_out = lax.scan(per_sequence, start_grads, (tokens, frames, lengths, cotangent))
    return (stacked_out[0], stacked_out[1], stacked_out[2], totals[0], totals[1], totals[2], totals[3], totals[4], totals[5], totals[6], totals[7], totals[8])
```

```python
import functools

import jax
import jax.numpy as jnp
import numpy as np
from jax import lax
from jax.experimental import pallas as pl
from jax.experimental.pallas import tpu as pltpu
from jax.sharding import PartitionSpec as P

D = 768
HEAD_DIM = 64
FRAMES = 1500
PAIR = 2 * HEAD_DIM
PAIRS = D // PAIR
TILE = 128
KEY_CHUNK = 256

eps_norm = 1e-05
neg_big = -1e30
head_scale = 0.125
bf16 = jnp.bfloat16
f32 = jnp.float32
VMEM_LIMIT = 56 * 1024 * 1024


def layer_norm(inputs, gain_vec, shift_vec):
    average = jnp.mean(inputs, axis=-1, keepdims=True)
    centered = inputs - average
    variance = jnp.mean(centered * centered, axis=-1, keepdims=True)
    return centered * lax.rsqrt(variance + eps_norm) * gain_vec + shift_vec


def exact_gelu(inputs):
    return jax.nn.gelu(inputs, approximate=False)


def nt(left, right):
    return lax.dot_general(left, right, (((1,), (1,)), ((), ())), preferred_element_type=f32)


def nn(left, right):
    return lax.dot_general(left, right, (((1,), (0,)), ((), ())), preferred_element_type=f32)


def split_heads(block):
    lanes = lax.broadcasted_iota(jnp.int32, block.shape, 1)
    zero = jnp.zeros_like(block)
    return jnp.concatenate(
        [jnp.where(lanes < HEAD_DIM, block, zero), jnp.where(lanes < HEAD_DIM, zero, block)], axis=0
    )


def join_heads(stacked):
    return jnp.concatenate([stacked[:HEAD_DIM, :TILE], stacked[HEAD_DIM:, TILE:]], axis=0).T


def row_dots(left, right):
    prod = (left.astype(f32) * right.astype(f32)).T
    return jnp.concatenate(
        [
            jnp.sum(prod[:HEAD_DIM], axis=0, keepdims=True),
            jnp.sum(prod[HEAD_DIM:], axis=0, keepdims=True),
        ],
        axis=1,
    )


def cross_forward_kernel(len_ref, q_ref, kv_ref, out_ref, lse_ref, vt_ref, s_ref):
    slots = kv_ref.shape[0]
    vt_ref[...] = kv_ref[:, PAIR:].T
    out_ref[...] = jnp.zeros_like(out_ref)
    lse_ref[...] = jnp.zeros_like(lse_ref)
    spans = [(k, min(KEY_CHUNK, slots - k)) for k in range(0, slots, KEY_CHUNK)]

    def per_tile(tile, carry):
        rows = pl.ds(pl.multiple_of(tile * TILE, TILE), TILE)
        queries = split_heads(q_ref[rows, :] * jnp.asarray(head_scale, bf16))
        peak = jnp.full((1, 2 * TILE), neg_big, f32)
        for start, size in spans:
            scores = nt(kv_ref[start : start + size, :PAIR], queries)
            if start + size > FRAMES:
                keys = start + lax.broadcasted_iota(jnp.int32, scores.shape, 0)
                scores = jnp.where(keys < FRAMES, scores, neg_big)
            s_ref[start : start + size, :] = scores
            peak = jnp.maximum(peak, jnp.max(scores, axis=0, keepdims=True))
        total = jnp.zeros((1, 2 * TILE), f32)
        mixed = jnp.zeros((PAIR, 2 * TILE), f32)
        for start, size in spans:
            probs = jnp.exp(s_ref[start : start + size, :] - peak)
            total = total + jnp.sum(probs, axis=0, keepdims=True)
            mixed = mixed + nn(vt_ref[:, start : start + size], probs.astype(bf16))
        out_ref[rows, :] = join_heads(mixed / total).astype(bf16)
        lse_ref[0, pl.ds(tile, 1), :] = peak + jnp.log(total)
        return carry

    lax.fori_loop(0, pl.cdiv(len_ref[0], TILE), per_tile, 0)


def cross_forward(queries, kv, seq_len):
    rows, slots = queries.shape[0], kv.shape[0]
    tiles = rows // TILE
    return pl.pallas_call(
        cross_forward_kernel,
        name="cross_forward",
        out_shape=(
            jax.ShapeDtypeStruct((rows, D), bf16),
            jax.ShapeDtypeStruct((PAIRS, tiles, 2 * TILE), f32),
        ),
        grid_spec=pltpu.PrefetchScalarGridSpec(
            num_scalar_prefetch=1,
            grid=(PAIRS,),
            in_specs=[
                pl.BlockSpec((rows, PAIR), lambda h, n: (0, h)),
                pl.BlockSpec((slots, 2 * PAIR), lambda h, n: (0, h)),
            ],
            out_specs=[
                pl.BlockSpec((rows, PAIR), lambda h, n: (0, h)),
                pl.BlockSpec((1, tiles, 2 * TILE), lambda h, n: (h, 0, 0)),
            ],
            scratch_shapes=[
                pltpu.VMEM((PAIR, slots), bf16),
                pltpu.VMEM((slots, 2 * TILE), f32),
            ],
        ),
        compiler_params=pltpu.CompilerParams(vmem_limit_bytes=VMEM_LIMIT),
        cost_estimate=pl.CostEstimate(
            flops=8 * rows * slots * D, bytes_accessed=2 * (2 * rows + 2 * slots) * D, transcendentals=rows * slots * 12
        ),
    )(seq_len, queries, kv)


def cross_backward_kernel(len_ref, q_ref, kv_ref, mix_ref, grad_ref, lse_ref, dq_ref, dkv_ref, kt_ref, dk_ref, dv_ref):
    slots = kv_ref.shape[0]
    kt_ref[...] = kv_ref[:, :PAIR].T
    dq_ref[...] = jnp.zeros_like(dq_ref)
    dk_ref[...] = jnp.zeros_like(dk_ref)
    dv_ref[...] = jnp.zeros_like(dv_ref)
    spans = [(k, min(KEY_CHUNK, slots - k)) for k in range(0, slots, KEY_CHUNK)]

    def per_tile(tile, carry):
        rows = pl.ds(pl.multiple_of(tile * TILE, TILE), TILE)
        queries = split_heads(q_ref[rows, :] * jnp.asarray(head_scale, bf16))
        grads = split_heads(grad_ref[rows, :])
        inner = row_dots(mix_ref[rows, :], grad_ref[rows, :])
        lse = lse_ref[0, pl.ds(tile, 1), :]
        dq = jnp.zeros((PAIR, 2 * TILE), f32)
        for start, size in spans:
            span = slice(start, start + size)
            probs = jnp.exp(nt(kv_ref[span, :PAIR], queries) - lse)
            if start + size > FRAMES:
                keys = start + lax.broadcasted_iota(jnp.int32, probs.shape, 0)
                probs = jnp.where(keys < FRAMES, probs, 0.0)
            dscores = (probs * (nt(kv_ref[span, PAIR:], grads) - inner)).astype(bf16)
            dv_ref[span, :] += nn(probs.astype(bf16), grads)
            dk_ref[span, :] += nn(dscores, queries)
            dq = dq + nn(kt_ref[:, span], dscores)
        dq_ref[rows, :] = join_heads(dq).astype(bf16) * jnp.asarray(head_scale, bf16)
        return carry

    lax.fori_loop(0, pl.cdiv(len_ref[0], TILE), per_tile, 0)
    dkv_ref[:, :PAIR] = dk_ref[...].astype(bf16)
    dkv_ref[:, PAIR:] = dv_ref[...].astype(bf16)


def cross_backward(queries, kv, mixture, grad_mixture, lse, seq_len):
    rows, slots = queries.shape[0], kv.shape[0]
    tiles = rows // TILE
    row_spec = pl.BlockSpec((rows, PAIR), lambda h, n: (0, h))
    kv_spec = pl.BlockSpec((slots, 2 * PAIR), lambda h, n: (0, h))
    return pl.pallas_call(
        cross_backward_kernel,
        name="cross_backward",
        out_shape=(
            jax.ShapeDtypeStruct((rows, D), bf16),
            jax.ShapeDtypeStruct((slots, 2 * D), bf16),
        ),
        grid_spec=pltpu.PrefetchScalarGridSpec(
            num_scalar_prefetch=1,
            grid=(PAIRS,),
            in_specs=[
                row_spec,
                kv_spec,
                row_spec,
                row_spec,
                pl.BlockSpec((1, tiles, 2 * TILE), lambda h, n: (h, 0, 0)),
            ],
            out_specs=[row_spec, kv_spec],
            scratch_shapes=[
                pltpu.VMEM((PAIR, slots), bf16),
                pltpu.VMEM((slots, PAIR), f32),
                pltpu.VMEM((slots, PAIR), f32),
            ],
        ),
        compiler_params=pltpu.CompilerParams(vmem_limit_bytes=VMEM_LIMIT),
        cost_estimate=pl.CostEstimate(
            flops=20 * rows * slots * D, bytes_accessed=2 * (4 * rows + 4 * slots) * D, transcendentals=rows * slots * 12
        ),
    )(seq_len, queries, kv, mixture, grad_mixture, lse)


def seen(shape, row_start, seq_len):
    keys = lax.broadcasted_iota(jnp.int32, shape, 0)
    rows = row_start + lax.rem(lax.broadcasted_iota(jnp.int32, shape, 1), TILE)
    return (keys <= rows) & (keys < seq_len)


def self_forward_kernel(len_ref, qkv_ref, out_ref, lse_ref, vt_ref):
    seq_len = len_ref[0]
    vt_ref[...] = qkv_ref[:, 2 * PAIR :].T
    out_ref[...] = jnp.zeros_like(out_ref)
    lse_ref[...] = jnp.zeros_like(lse_ref)
    for tile in range(qkv_ref.shape[0] // TILE):

        @pl.when(tile * TILE < seq_len)
        def _():
            rows = slice(tile * TILE, (tile + 1) * TILE)
            size = (tile + 1) * TILE
            queries = split_heads(qkv_ref[rows, :PAIR] * jnp.asarray(head_scale, bf16))
            scores = nt(qkv_ref[:size, PAIR : 2 * PAIR], queries)
            scores = jnp.where(seen(scores.shape, tile * TILE, seq_len), scores, neg_big)
            peak = jnp.max(scores, axis=0, keepdims=True)
            probs = jnp.exp(scores - peak)
            total = jnp.sum(probs, axis=0, keepdims=True)
            mixed = nn(vt_ref[:, :size], probs.astype(bf16))
            out_ref[rows, :] = join_heads(mixed / total).astype(bf16)
            lse_ref[0, tile : tile + 1, :] = peak + jnp.log(total)


def self_forward(qkv, seq_len):
    rows = qkv.shape[0]
    tiles = rows // TILE
    return pl.pallas_call(
        self_forward_kernel,
        name="self_forward",
        out_shape=(
            jax.ShapeDtypeStruct((rows, D), bf16),
            jax.ShapeDtypeStruct((PAIRS, tiles, 2 * TILE), f32),
        ),
        grid_spec=pltpu.PrefetchScalarGridSpec(
            num_scalar_prefetch=1,
            grid=(PAIRS,),
            in_specs=[pl.BlockSpec((rows, 3 * PAIR), lambda h, n: (0, h))],
            out_specs=[
                pl.BlockSpec((rows, PAIR), lambda h, n: (0, h)),
                pl.BlockSpec((1, tiles, 2 * TILE), lambda h, n: (h, 0, 0)),
            ],
            scratch_shapes=[pltpu.VMEM((PAIR, rows), bf16)],
        ),
        compiler_params=pltpu.CompilerParams(vmem_limit_bytes=VMEM_LIMIT),
        cost_estimate=pl.CostEstimate(
            flops=5 * rows * rows * D, bytes_accessed=8 * rows * D, transcendentals=rows * rows * 8
        ),
    )(seq_len, qkv)


def self_backward_kernel(len_ref, qkv_ref, mix_ref, grad_ref, lse_ref, dqkv_ref, kt_ref, dk_ref, dv_ref):
    seq_len = len_ref[0]
    kt_ref[...] = qkv_ref[:, PAIR : 2 * PAIR].T
    dqkv_ref[...] = jnp.zeros_like(dqkv_ref)
    dk_ref[...] = jnp.zeros_like(dk_ref)
    dv_ref[...] = jnp.zeros_like(dv_ref)
    for tile in range(qkv_ref.shape[0] // TILE):

        @pl.when(tile * TILE < seq_len)
        def _():
            rows = slice(tile * TILE, (tile + 1) * TILE)
            size = (tile + 1) * TILE
            queries = split_heads(qkv_ref[rows, :PAIR] * jnp.asarray(head_scale, bf16))
            grads = split_heads(grad_ref[rows, :])
            inner = row_dots(mix_ref[rows, :], grad_ref[rows, :])
            lse = lse_ref[0, tile : tile + 1, :]
            scores = nt(qkv_ref[:size, PAIR : 2 * PAIR], queries)
            scores = jnp.where(seen(scores.shape, tile * TILE, seq_len), scores, neg_big)
            probs = jnp.exp(scores - lse)
            dscores = (probs * (nt(qkv_ref[:size, 2 * PAIR :], grads) - inner)).astype(bf16)
            dv_ref[:size, :] += nn(probs.astype(bf16), grads)
            dk_ref[:size, :] += nn(dscores, queries)
            dq = nn(kt_ref[:, :size], dscores)
            dqkv_ref[rows, :PAIR] = join_heads(dq).astype(bf16) * jnp.asarray(head_scale, bf16)

    dqkv_ref[:, PAIR : 2 * PAIR] = dk_ref[...].astype(bf16)
    dqkv_ref[:, 2 * PAIR :] = dv_ref[...].astype(bf16)


def self_backward(qkv, mixture, grad_mixture, lse, seq_len):
    rows = qkv.shape[0]
    tiles = rows // TILE
    row_spec = pl.BlockSpec((rows, PAIR), lambda h, n: (0, h))
    qkv_spec = pl.BlockSpec((rows, 3 * PAIR), lambda h, n: (0, h))
    return pl.pallas_call(
        self_backward_kernel,
        name="self_backward",
        out_shape=jax.ShapeDtypeStruct((rows, 3 * D), bf16),
        grid_spec=pltpu.PrefetchScalarGridSpec(
            num_scalar_prefetch=1,
            grid=(PAIRS,),
            in_specs=[
                qkv_spec,
                row_spec,
                row_spec,
                pl.BlockSpec((1, tiles, 2 * TILE), lambda h, n: (h, 0, 0)),
            ],
            out_specs=qkv_spec,
            scratch_shapes=[
                pltpu.VMEM((PAIR, rows), bf16),
                pltpu.VMEM((rows, PAIR), f32),
                pltpu.VMEM((rows, PAIR), f32),
            ],
        ),
        compiler_params=pltpu.CompilerParams(vmem_limit_bytes=VMEM_LIMIT),
        cost_estimate=pl.CostEstimate(
            flops=12 * rows * rows * D, bytes_accessed=16 * rows * D, transcendentals=rows * rows * 8
        ),
    )(seq_len, qkv, mixture, grad_mixture, lse)


def dot(left, right):
    return jnp.dot(left, right, preferred_element_type=f32)


def dot_t(left, right):
    return jnp.einsum("re,de->rd", left, right, preferred_element_type=f32)


def by_pair(weight, parts):
    rows = weight.shape[0]
    return weight.reshape(rows, parts, PAIRS, PAIR).swapaxes(1, 2).reshape(rows, parts * D)


def by_part(weight, parts):
    rows = weight.shape[0]
    return weight.reshape(rows, PAIRS, parts, PAIR).swapaxes(1, 2).reshape(rows, parts * D)


def gather_rows(shard):
    half = lax.all_gather(shard, "fsdp", axis=0, tiled=True)
    half = lax.optimization_barrier(half)
    return lax.all_gather(half, "grp", axis=0, tiled=True)


def scatter_sum(grad):
    n_grp, n_fsdp = lax.axis_size("grp"), lax.axis_size("fsdp")
    bits = [("grp", b) for b in range(n_grp.bit_length() - 1)]
    bits += [("fsdp", b) for b in range(n_fsdp.bit_length() - 1)]
    rows = grad.shape[0] // (n_grp * n_fsdp)
    total = len(bits)
    current = grad.reshape((2,) * total + (rows,) + grad.shape[1:])
    dims = [("grp", b) for b in reversed(range(n_grp.bit_length() - 1))]
    dims += [("fsdp", b) for b in reversed(range(n_fsdp.bit_length() - 1))]
    for step, (axis, b) in enumerate(bits):
        dim = dims.index((axis, b))
        dims.pop(dim)
        mine = (lax.axis_index(axis) >> b) & 1
        sent = lax.dynamic_index_in_dim(current, 1 - mine, dim, keepdims=False)
        kept = lax.dynamic_index_in_dim(current, mine, dim, keepdims=False)
        count = lax.axis_size(axis)
        got = lax.ppermute(sent, axis, [(i, i ^ (1 << b)) for i in range(count)])
        current = kept.astype(f32) + got.astype(f32)
        if step + 1 < total:
            current = current.astype(grad.dtype)
    return current


def shards(
    tokens,
    frames,
    lengths,
    cotangent,
    self_in,
    self_out,
    cross_q,
    cross_kv,
    cross_out,
    fc_in,
    fc_out,
    norm_gain,
    norm_bias,
):
    fsdp_count = lax.axis_size("fsdp")
    group_seqs = lengths.shape[0]
    per_device = group_seqs // fsdp_count
    seq_ids = jnp.arange(group_seqs, dtype=jnp.int32)
    rank_order = jnp.argsort(-(lengths * group_seqs + (group_seqs - 1 - seq_ids)))
    rank_ids = np.arange(group_seqs)
    rounds = rank_ids // fsdp_count
    places = rank_ids % fsdp_count
    rank_of = np.where(rounds % 2 == 0, rank_ids, rounds * fsdp_count + fsdp_count - 1 - places)
    sender = rank_order[jnp.asarray(rank_of, dtype=jnp.int32)]
    slot_of_seq = jnp.argsort(sender)
    device = lax.axis_index("fsdp")

    def bring(array, slot):
        picked = array[sender[slot * fsdp_count : (slot + 1) * fsdp_count]]
        moved = lax.all_to_all(picked, "fsdp", split_axis=0, concat_axis=0, tiled=True)
        return moved.reshape(-1, array.shape[-1])

    def send_back(array):
        parts = array.reshape(fsdp_count, -1, array.shape[-1])
        return lax.all_to_all(parts, "fsdp", split_axis=0, concat_axis=0, tiled=True)

    norms = jnp.concatenate(
        [norm_gain, norm_bias, jnp.zeros((norm_gain.shape[0], 120), bf16)], axis=1
    )
    group_one = gather_rows(jnp.concatenate([by_pair(self_in, 3), self_out, norms], axis=1))
    group_two = gather_rows(jnp.concatenate([by_pair(cross_kv, 2), cross_q, cross_out], axis=1))
    w_fc_in = gather_rows(fc_in)
    n_all = lax.axis_size("grp") * fsdp_count
    w_fc_out = gather_rows(fc_out)
    w_self_in = group_one[:, : 3 * D]
    w_self_out = group_one[:, 3 * D : 4 * D]
    gains = group_one[:, 4 * D : 4 * D + 4].astype(f32)
    biases = group_one[:, 4 * D + 4 : 4 * D + 8].astype(f32)
    w_cross_kv = group_two[:, : 2 * D]
    w_cross_q = group_two[:, 2 * D : 3 * D]
    w_cross_out = group_two[:, 3 * D :]

    tok = [bring(tokens, s) for s in range(per_device)]
    frm = [bring(frames, s) for s in range(per_device)]
    cot = [bring(cotangent, s) for s in range(per_device)]
    lens = [
        lax.dynamic_slice_in_dim(lengths[sender], s * fsdp_count + device, 1)
        for s in range(per_device)
    ]

    results = []
    for slot in range(per_device):
        seq_len = lens[slot]
        stream = tok[slot].astype(f32)
        valid = (lax.broadcasted_iota(jnp.int32, (stream.shape[0], 1), 0) < seq_len[0]).astype(f32)
        normed_one, pull_one = jax.vjp(layer_norm, stream, gains[:, 0], biases[:, 0])
        normed_one = normed_one.astype(bf16)
        qkv = dot(normed_one, w_self_in).astype(bf16)
        mixture, lse = self_forward(qkv, seq_len)
        after_self = stream + dot(mixture, w_self_out)
        normed_two, pull_two = jax.vjp(layer_norm, after_self, gains[:, 1], biases[:, 1])
        normed_two = normed_two.astype(bf16)
        queries_two = dot(normed_two, w_cross_q).astype(bf16)
        kv = dot(frm[slot], w_cross_kv).astype(bf16)
        mixture_two, lse_two = cross_forward(queries_two, kv, seq_len)
        after_cross = after_self + dot(mixture_two, w_cross_out)
        normed_three, pull_three = jax.vjp(layer_norm, after_cross, gains[:, 2], biases[:, 2])
        normed_three = normed_three.astype(bf16)
        pre_act = dot(normed_three, w_fc_in)
        activated, pull_gelu = jax.vjp(exact_gelu, pre_act)
        hidden = activated.astype(bf16)
        after_mlp = after_cross + dot(hidden, w_fc_out)
        final_norm, pull_four = jax.vjp(layer_norm, after_mlp, gains[:, 3], biases[:, 3])
        output = (final_norm * valid).astype(bf16)

        grad_mlp, gain_four, shift_four = pull_four(cot[slot].astype(f32) * valid)
        branch_three = grad_mlp.astype(bf16)
        grad_pre = pull_gelu(dot_t(branch_three, w_fc_out))[0].astype(bf16)
        norm_three_in, gain_three, shift_three = pull_three(dot_t(grad_pre, w_fc_in))
        grad_cross = grad_mlp + norm_three_in
        branch_two = grad_cross.astype(bf16)
        grad_mixture_two = dot_t(branch_two, w_cross_out).astype(bf16)
        grad_q_two, grad_kv = cross_backward(
            queries_two, kv, mixture_two, grad_mixture_two, lse_two, seq_len
        )
        grad_frames = dot_t(grad_kv, w_cross_kv).astype(bf16)
        norm_two_in, gain_two, shift_two = pull_two(dot_t(grad_q_two, w_cross_q))
        grad_attn = grad_cross + norm_two_in
        branch_one = grad_attn.astype(bf16)
        grad_mixture = dot_t(branch_one, w_self_out).astype(bf16)
        grad_qkv = self_backward(qkv, mixture, grad_mixture, lse, seq_len)
        norm_one_in, gain_one, shift_one = pull_one(dot_t(grad_qkv, w_self_in))
        grad_tokens = (grad_attn + norm_one_in).astype(bf16)
        norm_grads = jnp.stack(
            [gain_one, gain_two, gain_three, gain_four, shift_one, shift_two, shift_three, shift_four],
            axis=1,
        )
        results.append(
            dict(
                output=output,
                grad_tokens=grad_tokens,
                grad_frames=grad_frames,
                norm=norm_grads,
                fc_out=(hidden, branch_three),
                fc_in=(normed_three, grad_pre),
                cross_out=(mixture_two, branch_two),
                cross_q=(normed_two, grad_q_two),
                cross_kv=(frm[slot], grad_kv),
                self_out=(mixture, branch_one),
                self_in=(normed_one, grad_qkv),
            )
        )

    def weight_grad(name):
        total = None
        for res in results:
            left, right = res[name]
            part = jnp.einsum("rd,re->de", left, right, preferred_element_type=f32)
            total = part if total is None else total + part
        return total.astype(bf16)

    def finish(name):
        back = jnp.concatenate([send_back(res[name]) for res in results], axis=0)
        return back[slot_of_seq]

    g_fc_out = scatter_sum(weight_grad("fc_out"))
    g_fc_in = scatter_sum(weight_grad("fc_in"))
    g_two = scatter_sum(
        jnp.concatenate([weight_grad(n) for n in ("cross_kv", "cross_q", "cross_out")], axis=1)
    )
    g_one = scatter_sum(jnp.concatenate([weight_grad(n) for n in ("self_in", "self_out")], axis=1))
    norm_sum = results[0]["norm"]
    for res in results[1:]:
        norm_sum = norm_sum + res["norm"]
    g_norm = scatter_sum(norm_sum.reshape(n_all, 1, -1)).reshape(-1, 8)
    grad_frames_final = finish("grad_frames")
    output_final = finish("output")
    grad_tokens_final = finish("grad_tokens")
    return (
        output_final,
        grad_tokens_final,
        grad_frames_final,
        by_part(g_one[:, : 3 * D], 3),
        g_one[:, 3 * D :],
        g_two[:, 2 * D : 3 * D],
        by_part(g_two[:, : 2 * D], 2),
        g_two[:, 3 * D :],
        g_fc_in,
        g_fc_out,
        g_norm[:, :4],
        g_norm[:, 4:],
    )


def solution(mesh):
    rows = P(("grp", "fsdp"), None)
    seqs = P("grp", "fsdp", None)
    return jax.shard_map(
        shards,
        mesh=mesh,
        in_specs=(seqs, seqs, P("grp"), seqs) + (rows,) * 9,
        out_specs=(seqs,) * 3 + (rows,) * 9,
        check_vma=False,
    )
```

```python
import functools

import jax
import jax.numpy as jnp
import numpy as np
from jax import lax
from jax.experimental import pallas as pl
from jax.experimental.pallas import tpu as pltpu
from jax.sharding import PartitionSpec as P

D = 768
FF = 3072
HEAD_DIM = 64
FRAMES = 1500
PAIR = 2 * HEAD_DIM
PAIRS = D // PAIR
TILE = 128
ROWS = 256
KEY_CHUNK = 256
FF_PARTS = FF // D

eps_norm = 1e-05
neg_big = -1e30
head_scale = 0.125
bf16 = jnp.bfloat16
f32 = jnp.float32
MIB = 1024 * 1024
COST = pl.CostEstimate(flops=1000000, bytes_accessed=1000000, transcendentals=0)

ONE_OUT = 3 * D
ONE_Q = 4 * D
ONE_NORM = 5 * D
ONE_COLS = 5 * D + 128
TWO_OUT = 2 * D


def nt(left, right):
    return lax.dot_general(left, right, (((1,), (1,)), ((), ())), preferred_element_type=f32)


def nn(left, right):
    return lax.dot_general(left, right, (((1,), (0,)), ((), ())), preferred_element_type=f32)


def normalize(stream):
    centered = stream - jnp.mean(stream, axis=-1, keepdims=True)
    scale = lax.rsqrt(jnp.mean(centered * centered, axis=-1, keepdims=True) + eps_norm)
    return centered * scale, scale


def norm_backward(normed, scale, gain, grad):
    scaled = grad * gain
    mean_scaled = jnp.mean(scaled, axis=-1, keepdims=True)
    mean_along = jnp.mean(scaled * normed, axis=-1, keepdims=True)
    return scale * (scaled - mean_scaled - normed * mean_along)


def col_sum(values):
    return jnp.sum(values, axis=0, keepdims=True)


def split_heads(block):
    lanes = lax.broadcasted_iota(jnp.int32, block.shape, 1)
    zero = jnp.zeros_like(block)
    return jnp.concatenate(
        [jnp.where(lanes < HEAD_DIM, block, zero), jnp.where(lanes < HEAD_DIM, zero, block)], axis=0
    )


def join_heads(stacked):
    return jnp.concatenate([stacked[:HEAD_DIM, :TILE], stacked[HEAD_DIM:, TILE:]], axis=0).T


def row_dots(left, right):
    prod = (left.astype(f32) * right.astype(f32)).T
    return jnp.concatenate([col_sum(prod[:HEAD_DIM]), col_sum(prod[HEAD_DIM:])], axis=1)


def seen(shape, row_start, seq_len):
    keys = lax.broadcasted_iota(jnp.int32, shape, 0)
    rows = row_start + lax.rem(lax.broadcasted_iota(jnp.int32, shape, 1), TILE)
    return (keys <= rows) & (keys < seq_len)


def each_tile(count, size, body):
    def step(i, carry):
        body(pl.ds(pl.multiple_of(i * size, size), size), i)
        return carry

    lax.fori_loop(0, count, step, 0)


def lane_block(index):
    return pl.ds(pl.multiple_of(index * PAIR, PAIR), PAIR)


def token_rows(ref, tile):
    count = ROWS // ref.shape[1]
    return ref[pl.ds(tile * count, count)].reshape(ROWS, D).astype(f32)


def clear(*refs):
    for ref in refs:
        ref[...] = jnp.zeros_like(ref)


scale_of_heads = functools.partial(jnp.asarray, head_scale, bf16)


def self_part_forward(
    len_ref, tok_ref, one_ref, norm_ref,
    qkv_ref, normed_one_ref, mix_ref, lse_ref, after_ref, normed_two_ref, q_two_ref,
    vt_ref,
):
    seq_len = len_ref[0]
    row_tiles = pl.cdiv(seq_len, ROWS)
    clear(normed_one_ref, mix_ref, lse_ref, normed_two_ref)

    def project(rows, i):
        normed, _ = normalize(token_rows(tok_ref, i))
        normed = (normed * norm_ref[0:1, :] + norm_ref[4:5, :]).astype(bf16)
        normed_one_ref[rows, :] = normed
        qkv_ref[rows, :] = nn(normed, one_ref[:, :ONE_OUT]).astype(bf16)

    each_tile(row_tiles, ROWS, project)

    def per_pair(pair, carry):
        q_lanes, k_lanes, v_lanes = (lane_block(3 * pair + i) for i in range(3))
        for tile in range(qkv_ref.shape[0] // TILE):

            @pl.when(tile * TILE < seq_len)
            def _():
                rows = slice(tile * TILE, (tile + 1) * TILE)
                size = (tile + 1) * TILE
                vt_ref[:, rows] = qkv_ref[rows, v_lanes].T
                queries = split_heads(qkv_ref[rows, q_lanes] * scale_of_heads())
                scores = nt(qkv_ref[:size, k_lanes], queries)
                scores = jnp.where(seen(scores.shape, tile * TILE, seq_len), scores, neg_big)
                peak = jnp.max(scores, axis=0, keepdims=True)
                probs = jnp.exp(scores - peak)
                total = col_sum(probs)
                mixed = nn(vt_ref[:, :size], probs.astype(bf16))
                mix_ref[rows, lane_block(pair)] = join_heads(mixed / total).astype(bf16)
                lse_ref[pair, tile : tile + 1, :] = peak + jnp.log(total)

        return carry

    lax.fori_loop(0, PAIRS, per_pair, 0)

    def finish(rows, i):
        after = token_rows(tok_ref, i) + nn(mix_ref[rows, :], one_ref[:, ONE_OUT:ONE_Q])
        after_ref[rows, :] = after
        normed, _ = normalize(after)
        normed = (normed * norm_ref[1:2, :] + norm_ref[5:6, :]).astype(bf16)
        normed_two_ref[rows, :] = normed
        q_two_ref[rows, :] = nn(normed, one_ref[:, ONE_Q:ONE_NORM]).astype(bf16)

    each_tile(row_tiles, ROWS, finish)


PARTS = {"frames": 4, "tokens": 4, "first": 2, "second": 2}


def part_at(part):
    return {"frames": 0, "tokens": 3, "first": 0, "second": 1}[part]


def whole():
    return pl.BlockSpec(memory_space=pltpu.VMEM)


def in_smem():
    return pl.BlockSpec(memory_space=pltpu.SMEM)


def shape_of(*dims, dtype=bf16):
    return jax.ShapeDtypeStruct(dims, dtype)


def in_hbm(*dims, dtype=bf16):
    return pltpu.HBM(dims, dtype)


def run_self_forward(seq_len, arrived, part, one, norm_rows):
    blocks, size = arrived.shape[0], arrived.shape[1] // PARTS[part]
    at = part_at(part)
    rows = blocks * size
    fixed = lambda *dims: pl.BlockSpec(dims, lambda i: (0,) * len(dims), pipeline_mode=pl.Buffered(1))
    shapes = [
        in_hbm(rows, 3 * D),
        in_hbm(rows, D),
        in_hbm(rows, D),
        in_hbm(PAIRS, rows // TILE, 2 * TILE, dtype=f32),
        in_hbm(rows, D, dtype=f32),
        in_hbm(rows, D),
        in_hbm(rows, D),
    ]
    return pl.pallas_call(
        self_part_forward,
        name="self_part_forward",
        grid=(1,),
        in_specs=[
            in_smem(),
            pl.BlockSpec((blocks, size, D), lambda i: (0, at, 0), pipeline_mode=pl.Buffered(1)),
            fixed(*one.shape),
            fixed(8, D),
        ],
        out_specs=[fixed(*s.shape) for s in shapes],
        out_shape=shapes,
        scratch_shapes=[pltpu.VMEM((PAIR, rows), bf16)],
        compiler_params=pltpu.CompilerParams(vmem_limit_bytes=36 * MIB),
        cost_estimate=COST,
    )(seq_len, arrived, one, norm_rows)


def cross_forward_kernel(len_ref, frm_ref, w_ref, q_ref, out_ref, lse_ref, kv_ref, vt_ref, s_ref):
    slots = kv_ref.shape[0]
    clear(out_ref, lse_ref)
    kv_ref[...] = nn(frm_ref[...].reshape(slots, D), w_ref[...]).astype(bf16)
    vt_ref[...] = kv_ref[:, PAIR:].T
    spans = [(k, min(KEY_CHUNK, slots - k)) for k in range(0, slots, KEY_CHUNK)]

    def per_tile(rows, tile):
        queries = split_heads(q_ref[rows, :] * scale_of_heads())
        peak = jnp.full((1, 2 * TILE), neg_big, f32)
        for start, size in spans:
            scores = nt(kv_ref[start : start + size, :PAIR], queries)
            if start + size > FRAMES:
                keys = start + lax.broadcasted_iota(jnp.int32, scores.shape, 0)
                scores = jnp.where(keys < FRAMES, scores, neg_big)
            s_ref[start : start + size, :] = scores
            peak = jnp.maximum(peak, jnp.max(scores, axis=0, keepdims=True))
        total = jnp.zeros((1, 2 * TILE), f32)
        mixed = jnp.zeros((PAIR, 2 * TILE), f32)
        for start, size in spans:
            probs = jnp.exp(s_ref[start : start + size, :] - peak)
            total = total + col_sum(probs)
            mixed = mixed + nn(vt_ref[:, start : start + size], probs.astype(bf16))
        out_ref[rows, :] = join_heads(mixed / total).astype(bf16)
        lse_ref[0, pl.ds(tile, 1), :] = peak + jnp.log(total)

    each_tile(pl.cdiv(len_ref[0], TILE), TILE, per_tile)


def run_cross_forward(seq_len, arrived, two, q_two):
    blocks, size = arrived.shape[0], 3 * arrived.shape[1] // 4
    rows, slots = q_two.shape[0], blocks * size
    tiles = rows // TILE
    return pl.pallas_call(
        cross_forward_kernel,
        name="cross_forward",
        grid=(PAIRS,),
        in_specs=[
            in_smem(),
            pl.BlockSpec((blocks, size, D), lambda h: (0, 0, 0), pipeline_mode=pl.Buffered(1)),
            pl.BlockSpec((D, 2 * PAIR), lambda h: (0, h)),
            pl.BlockSpec((rows, PAIR), lambda h: (0, h)),
        ],
        out_specs=[
            pl.BlockSpec((rows, PAIR), lambda h: (0, h)),
            pl.BlockSpec((1, tiles, 2 * TILE), lambda h: (h, 0, 0)),
            pl.BlockSpec((slots, 2 * PAIR), lambda h: (0, h)),
        ],
        out_shape=[
            in_hbm(rows, D),
            in_hbm(PAIRS, tiles, 2 * TILE, dtype=f32),
            in_hbm(slots, 2 * D),
        ],
        scratch_shapes=[pltpu.VMEM((PAIR, slots), bf16), pltpu.VMEM((slots, 2 * TILE), f32)],
        compiler_params=pltpu.CompilerParams(vmem_limit_bytes=24 * MIB),
        cost_estimate=COST,
    )(seq_len, arrived, two, q_two)


def cross_backward_kernel(
    len_ref, q_ref, kv_ref, mix_ref, grad_ref, lse_ref, w_ref, _,
    dq_ref, dkv_ref, dfrm_ref,
    kt_ref, dk_ref, dv_ref, acc_ref,
):
    slots = kv_ref.shape[0]
    pair = pl.program_id(0)
    kt_ref[...] = kv_ref[:, :PAIR].T
    clear(dq_ref, dk_ref, dv_ref)
    spans = [(k, min(KEY_CHUNK, slots - k)) for k in range(0, slots, KEY_CHUNK)]

    def per_tile(rows, tile):
        queries = split_heads(q_ref[rows, :] * scale_of_heads())
        grads = split_heads(grad_ref[rows, :])
        inner = row_dots(mix_ref[rows, :], grad_ref[rows, :])
        lse = lse_ref[0, pl.ds(tile, 1), :]
        dq = jnp.zeros((PAIR, 2 * TILE), f32)
        for start, size in spans:
            span = slice(start, start + size)
            probs = jnp.exp(nt(kv_ref[span, :PAIR], queries) - lse)
            if start + size > FRAMES:
                keys = start + lax.broadcasted_iota(jnp.int32, probs.shape, 0)
                probs = jnp.where(keys < FRAMES, probs, 0.0)
            dscores = (probs * (nt(kv_ref[span, PAIR:], grads) - inner)).astype(bf16)
            dv_ref[span, :] += nn(probs.astype(bf16), grads)
            dk_ref[span, :] += nn(dscores, queries)
            dq = dq + nn(kt_ref[:, span], dscores)
        dq_ref[rows, :] = join_heads(dq).astype(bf16) * scale_of_heads()

    each_tile(pl.cdiv(len_ref[0], TILE), TILE, per_tile)
    dkv_ref[:, :PAIR] = dk_ref[...].astype(bf16)
    dkv_ref[:, PAIR:] = dv_ref[...].astype(bf16)
    part = nt(dkv_ref[...], w_ref[...])

    @pl.when(pair == 0)
    def _():
        acc_ref[...] = part

    @pl.when((pair > 0) & (pair < PAIRS - 1))
    def _():
        acc_ref[...] += part

    @pl.when(pair == PAIRS - 1)
    def _():
        dfrm_ref[...] = (acc_ref[...] + part).astype(bf16).reshape(dfrm_ref.shape)


def run_cross_backward(seq_len, q_two, kv, mix, grad_mix, lse, two, leaving):
    rows, slots, blocks = q_two.shape[0], kv.shape[0], leaving.shape[0]
    tiles = rows // TILE
    row_spec = pl.BlockSpec((rows, PAIR), lambda h: (0, h))
    kv_spec = pl.BlockSpec((slots, 2 * PAIR), lambda h: (0, h))
    return pl.pallas_call(
        cross_backward_kernel,
        name="cross_backward",
        grid=(PAIRS,),
        in_specs=[
            in_smem(),
            row_spec,
            kv_spec,
            row_spec,
            row_spec,
            pl.BlockSpec((1, tiles, 2 * TILE), lambda h: (h, 0, 0)),
            pl.BlockSpec((D, 2 * PAIR), lambda h: (0, h)),
            pl.BlockSpec(memory_space=pl.ANY),
        ],
        out_specs=[
            row_spec,
            kv_spec,
            pl.BlockSpec((blocks, slots // blocks, D), lambda h: (0, 0, 0), pipeline_mode=pl.Buffered(1)),
        ],
        out_shape=[in_hbm(rows, D), in_hbm(slots, 2 * D), in_hbm(*leaving.shape)],
        input_output_aliases={7: 2},
        scratch_shapes=[
            pltpu.VMEM((PAIR, slots), bf16),
            pltpu.VMEM((slots, PAIR), f32),
            pltpu.VMEM((slots, PAIR), f32),
            pltpu.VMEM((slots, D), f32),
        ],
        compiler_params=pltpu.CompilerParams(vmem_limit_bytes=36 * MIB),
        cost_estimate=COST,
    )(seq_len, q_two, kv, mix, grad_mix, lse, two, leaving)


def middle_kernel(
    len_ref, mix_ref, after_ref, cot_ref, two_ref, fc_ref, norm_ref,
    out_ref, normed_ref, hidden_ref, grad_pre_ref, branch_three_ref, branch_two_ref,
    grad_cross_ref, grad_mix_ref, norm_grad_ref,
    slope_ref,
):
    seq_len = len_ref[0]
    step = pl.program_id(0)
    parts = [(slice(k, k + D), slice(FF + k, FF + k + D)) for k in range(0, FF, D)]

    @pl.when(step == 0)
    def _():
        clear(norm_grad_ref)

    @pl.when(step * ROWS >= seq_len)
    def _():
        clear(out_ref, normed_ref, hidden_ref, grad_pre_ref, branch_three_ref, branch_two_ref)
        clear(grad_cross_ref, grad_mix_ref)

    @pl.when(step * ROWS < seq_len)
    def _():
        w_out = two_ref[:, TWO_OUT:]
        after_cross = after_ref[...] + nn(mix_ref[...], w_out)
        n_three, scale_three = normalize(after_cross)
        normed = (n_three * norm_ref[2:3, :] + norm_ref[6:7, :]).astype(bf16)
        normed_ref[...] = normed
        mlp = jnp.zeros((ROWS, D), f32)
        for span, rows_out in parts:
            pre = nn(normed, fc_ref[:, span])
            below = 0.5 * (1.0 + lax.erf(pre * np.float32(np.sqrt(0.5))))
            density = jnp.exp(-0.5 * pre * pre) * np.float32(1.0 / np.sqrt(2.0 * np.pi))
            slope_ref[:, span] = below + pre * density
            hidden = (pre * below).astype(bf16)
            hidden_ref[:, span] = hidden
            mlp = mlp + nn(hidden, fc_ref[:, rows_out])
        n_four, scale_four = normalize(after_cross + mlp)
        row_ids = step * ROWS + lax.broadcasted_iota(jnp.int32, (ROWS, 1), 0)
        valid = (row_ids < seq_len).astype(f32)
        output = ((n_four * norm_ref[3:4, :] + norm_ref[7:8, :]) * valid).astype(bf16)
        out_ref[...] = output.reshape(out_ref.shape)

        grad = cot_ref[...].reshape(ROWS, D).astype(f32) * valid
        norm_grad_ref[1:2, :] += col_sum(grad * n_four)
        norm_grad_ref[3:4, :] += col_sum(grad)
        grad_mlp = norm_backward(n_four, scale_four, norm_ref[3:4, :], grad)
        branch_three = grad_mlp.astype(bf16)
        branch_three_ref[...] = branch_three
        back = jnp.zeros((ROWS, D), f32)
        for span, rows_out in parts:
            grad_pre = (nt(branch_three, fc_ref[:, rows_out]) * slope_ref[:, span]).astype(bf16)
            grad_pre_ref[:, span] = grad_pre
            back = back + nt(grad_pre, fc_ref[:, span])
        norm_grad_ref[0:1, :] += col_sum(back * n_three)
        norm_grad_ref[2:3, :] += col_sum(back)
        grad_cross = grad_mlp + norm_backward(n_three, scale_three, norm_ref[2:3, :], back)
        grad_cross_ref[...] = grad_cross
        branch_two = grad_cross.astype(bf16)
        branch_two_ref[...] = branch_two
        grad_mix_ref[...] = nt(branch_two, w_out).astype(bf16)


def run_middle(seq_len, mix, after, arrived, part, two, fc, norm_rows):
    rows, blocks = mix.shape[0], arrived.shape[0]
    size = rows // blocks
    at = part_at(part)
    count = ROWS // size
    row_spec = pl.BlockSpec((ROWS, D), lambda i: (i, 0))
    wide_spec = pl.BlockSpec((ROWS, FF), lambda i: (i, 0))

    def fixed(*dims):
        return pl.BlockSpec(dims, lambda i: (0, 0), pipeline_mode=pl.Buffered(1))

    return pl.pallas_call(
        middle_kernel,
        name="mlp_and_back",
        grid=(rows // ROWS,),
        in_specs=[
            in_smem(), row_spec, row_spec, pl.BlockSpec((count, size, D), lambda i: (i, at, 0)),
            fixed(D, 3 * D), fixed(D, 2 * FF), fixed(8, D),
        ],
        out_specs=[pl.BlockSpec((count, size, D), lambda i: (i, 3, 0)), row_spec, wide_spec, wide_spec, row_spec, row_spec, row_spec, row_spec,
                   pl.BlockSpec((8, D), lambda i: (0, 0))],
        out_shape=[
            in_hbm(blocks, 4 * size, D), in_hbm(rows, D), in_hbm(rows, FF), in_hbm(rows, FF),
            in_hbm(rows, D), in_hbm(rows, D), in_hbm(rows, D, dtype=f32), in_hbm(rows, D),
            in_hbm(8, D, dtype=f32),
        ],
        scratch_shapes=[pltpu.VMEM((ROWS, FF), f32)],
        compiler_params=pltpu.CompilerParams(vmem_limit_bytes=48 * MIB),
        cost_estimate=COST,
    )(seq_len, mix, after, arrived, two, fc, norm_rows)


def self_part_backward(
    len_ref, dq_ref, grad_cross_ref, after_ref, qkv_ref, mix_ref, lse_ref, tok_ref, one_ref, norm_ref, _,
    branch_ref, dqkv_ref, grad_tok_ref, norm_grad_ref,
    attn_ref, grad_mix_ref, kt_ref, dk_ref, dv_ref,
):
    seq_len = len_ref[0]
    row_tiles = pl.cdiv(seq_len, ROWS)
    clear(branch_ref, dqkv_ref, grad_tok_ref, norm_grad_ref)

    def enter(rows, _):
        normed, scale = normalize(after_ref[rows, :])
        grad = nt(dq_ref[rows, :], one_ref[:, ONE_Q:ONE_NORM])
        norm_grad_ref[1:2, :] += col_sum(grad * normed)
        norm_grad_ref[3:4, :] += col_sum(grad)
        attn = grad_cross_ref[rows, :] + norm_backward(normed, scale, norm_ref[1:2, :], grad)
        attn_ref[rows, :] = attn
        branch = attn.astype(bf16)
        branch_ref[rows, :] = branch
        grad_mix_ref[rows, :] = nt(branch, one_ref[:, ONE_OUT:ONE_Q]).astype(bf16)

    each_tile(row_tiles, ROWS, enter)

    def per_pair(pair, carry):
        q_lanes, k_lanes, v_lanes = (lane_block(3 * pair + i) for i in range(3))
        clear(dk_ref, dv_ref)
        for tile in range(qkv_ref.shape[0] // TILE):

            @pl.when(tile * TILE < seq_len)
            def _():
                rows = slice(tile * TILE, (tile + 1) * TILE)
                size = (tile + 1) * TILE
                kt_ref[:, rows] = qkv_ref[rows, k_lanes].T
                queries = split_heads(qkv_ref[rows, q_lanes] * scale_of_heads())
                grad_mix = grad_mix_ref[rows, lane_block(pair)]
                grads = split_heads(grad_mix)
                inner = row_dots(mix_ref[rows, lane_block(pair)], grad_mix)
                scores = nt(qkv_ref[:size, k_lanes], queries)
                scores = jnp.where(seen(scores.shape, tile * TILE, seq_len), scores, neg_big)
                probs = jnp.exp(scores - lse_ref[pair, tile : tile + 1, :])
                dscores = (probs * (nt(qkv_ref[:size, v_lanes], grads) - inner)).astype(bf16)
                dv_ref[:size, :] += nn(probs.astype(bf16), grads)
                dk_ref[:size, :] += nn(dscores, queries)
                dq = nn(kt_ref[:, :size], dscores)
                dqkv_ref[rows, q_lanes] = join_heads(dq).astype(bf16) * scale_of_heads()

        dqkv_ref[:, k_lanes] = dk_ref[...].astype(bf16)
        dqkv_ref[:, v_lanes] = dv_ref[...].astype(bf16)
        return carry

    lax.fori_loop(0, PAIRS, per_pair, 0)

    def leave(rows, i):
        normed, scale = normalize(token_rows(tok_ref, i))
        grad = nt(dqkv_ref[rows, :], one_ref[:, :ONE_OUT])
        norm_grad_ref[0:1, :] += col_sum(grad * normed)
        norm_grad_ref[2:3, :] += col_sum(grad)
        total = attn_ref[rows, :] + norm_backward(normed, scale, norm_ref[0:1, :], grad)
        count = ROWS // grad_tok_ref.shape[1]
        grad_tok_ref[pl.ds(i * count, count)] = total.astype(bf16).reshape(count, -1, D)

    each_tile(row_tiles, ROWS, leave)


def run_self_backward(seq_len, dq, grad_cross, after, qkv, mix, lse, arrived, part, one, norm_rows, leaving, slot):
    blocks, size = arrived.shape[0], arrived.shape[1] // PARTS[part]
    at = part_at(part)
    rows = blocks * size
    fixed = lambda *dims: pl.BlockSpec(dims, lambda i: (0,) * len(dims), pipeline_mode=pl.Buffered(1))
    spec = lambda block: pl.BlockSpec(
        (blocks, size, D), lambda i: (0, block, 0), pipeline_mode=pl.Buffered(1)
    )
    before = [] if leaving is None else [leaving]
    body = self_part_backward
    if leaving is None:
        body = lambda *refs: self_part_backward(*refs[:10], None, *refs[10:])
    return pl.pallas_call(
        body,
        name="self_part_backward",
        grid=(1,),
        in_specs=[in_smem()]
        + [fixed(*a.shape) for a in (dq, grad_cross, after, qkv, mix, lse)]
        + [spec(at), fixed(*one.shape), fixed(8, D)]
        + [anywhere()] * len(before),
        out_specs=[fixed(rows, D), fixed(rows, 3 * D), spec(slot), fixed(8, D)],
        out_shape=[
            in_hbm(rows, D),
            in_hbm(rows, 3 * D),
            in_hbm(blocks, 2 * size, D),
            in_hbm(8, D, dtype=f32),
        ],
        input_output_aliases={10: 2} if before else {},
        scratch_shapes=[
            pltpu.VMEM((rows, D), f32),
            pltpu.VMEM((rows, D), bf16),
            pltpu.VMEM((PAIR, rows), bf16),
            pltpu.VMEM((rows, PAIR), f32),
            pltpu.VMEM((rows, PAIR), f32),
        ],
        compiler_params=pltpu.CompilerParams(vmem_limit_bytes=40 * MIB),
        cost_estimate=COST,
    )(seq_len, dq, grad_cross, after, qkv, mix, lse, arrived, one, norm_rows, *before)


def anywhere():
    return pl.BlockSpec(memory_space=pl.ANY)


def copy_kernel(plan, n_in, n_out, scalar_ref, *refs):
    ins, outs, sem = refs[:n_in], refs[n_in : n_in + n_out], refs[-1]
    for which, src, dst in plan(scalar_ref, ins, outs):
        pltpu.make_async_copy(src, dst, sem.at[which]).start()
    for which, out in enumerate(outs):
        pltpu.make_async_copy(out, out, sem.at[which]).wait()


def run_copies(name, plan, scalars, ins, out_shapes, stage="in"):
    vmem = pl.BlockSpec(memory_space=pltpu.VMEM)
    return pl.pallas_call(
        functools.partial(copy_kernel, plan, len(ins), len(out_shapes)),
        name=name,
        in_specs=[in_smem()] + [vmem if stage == "in" else anywhere()] * len(ins),
        out_specs=[vmem if stage == "out" else anywhere()] * len(out_shapes),
        out_shape=out_shapes,
        scratch_shapes=[pltpu.SemaphoreType.DMA((len(out_shapes),))],
        compiler_params=pltpu.CompilerParams(vmem_limit_bytes=16 * MIB),
        cost_estimate=pl.CostEstimate(flops=0, bytes_accessed=1000, transcendentals=0),
    )(scalars, *ins)


def device_bits():
    return [
        (axis, b)
        for axis in ("grp", "fsdp")
        for b in reversed(range(lax.axis_size(axis).bit_length() - 1))
    ]


def swap(array, axis, b):
    return lax.ppermute(array, axis, [(i, i ^ (1 << b)) for i in range(lax.axis_size(axis))])


def bit_mask(axis, b):
    return (1 << b) if axis == "fsdp" else lax.axis_size("fsdp") << b


def my_bit(axis, b):
    return (lax.axis_index(axis) >> b) & 1


class Gather:
    def __init__(self, name, shard, me, outs, pieces):
        self.name = name
        bits = device_bits()
        self.left = [p for p in bits if p[0] == "fsdp"] + [p for p in bits if p[0] == "grp"]
        self.masks = [0]
        self.value = shard[None]
        self.me = me
        self.outs = outs
        self.pieces = pieces
        self.got = None

    def send(self):
        self.got = swap(self.value, *self.left[0])

    def take(self):
        mask = bit_mask(*self.left.pop(0))
        masks = self.masks
        self.masks = masks + [mask ^ m for m in masks]
        k = len(masks)
        if self.left:

            def plan(_, ins, outs):
                return [(0, ins[0], outs[0].at[:k]), (0, ins[1], outs[0].at[k:])]

            shape = (2 * k,) + self.value.shape[1:]
            (self.value,) = run_copies(
                self.name + "_join", plan, self.me, [self.value, self.got], [in_hbm(*shape)]
            )
            return self.value

        def plan(me_ref, ins, outs):
            me = me_ref[0]
            return [
                (which, src, dst)
                for i in range(k)
                for half, src_ref in ((0, ins[0]), (k, ins[1]))
                for which, src, dst in self.pieces(src_ref.at[i], outs, me ^ self.masks[half + i])
            ]

        self.value = run_copies(
            self.name + "_order", plan, self.me, [self.value, self.got], self.outs
        )
        return self.value

    def step(self):
        self.send()
        return self.take()


def pack_shards(me, self_in, self_out, cross_q, norms, cross_kv, cross_out):
    rows = self_in.shape[0]

    def plan(_, ins, outs):
        w_in, w_out, w_q, w_norm, w_kv, w_cross = ins
        one, two = outs
        copies = []
        for pair in range(PAIRS):
            for o, w, parts in ((0, w_in, 3), (1, w_kv, 2)):
                for part in range(parts):
                    src = w.at[:, part * D + pair * PAIR : part * D + (pair + 1) * PAIR]
                    at = (parts * pair + part) * PAIR
                    copies.append((o, src, outs[o].at[:, at : at + PAIR]))
        copies.append((0, w_out, one.at[:, ONE_OUT:ONE_Q]))
        copies.append((0, w_q, one.at[:, ONE_Q:ONE_NORM]))
        copies.append((0, w_norm, one.at[:, ONE_NORM:]))
        copies.append((1, w_cross, two.at[:, TWO_OUT:]))
        return copies

    ins = [self_in, self_out, cross_q, norms, cross_kv, cross_out]
    shapes = [in_hbm(rows, ONE_COLS), in_hbm(rows, 3 * D)]
    return run_copies("pack_shards", plan, me, ins, shapes, "out")


def gather_rows(shard):
    return lax.all_gather(shard, ("grp", "fsdp"), axis=0, tiled=True)


def grad_kernel(
    full, len0_ref, len1_ref, bit_ref, left0_ref, right0_ref, left1_ref, right1_ref, *refs
):
    keep_ref, send_ref, flip_ref, acc_ref = refs[-4:]
    chunk, half, count = acc_ref.shape[0], acc_ref.shape[0] // 2, right0_ref.shape[0]
    sides = (
        (len0_ref[0], left0_ref, right0_ref, 0),
        (len1_ref[0], left1_ref, right1_ref, count),
    )
    tiles = [slice(k, k + ROWS) for k in range(0, count, ROWS)]

    @pl.when((pl.program_id(0) == 0) & (pl.program_id(1) == 0))
    def _():
        for seq_len, left_ref, _, at in sides:
            for tile in tiles:

                @pl.when(jnp.logical_or(full or tile.start == 0, tile.start < seq_len))
                def _():
                    if len(left_ref.shape) == 3:
                        size = left_ref.shape[1]
                        left = left_ref[tile.start // size : (tile.stop + size - 1) // size]
                        skip = tile.start % size
                        left = left.reshape(-1, D)[skip : skip + ROWS]
                    else:
                        left = left_ref[tile, :]
                    flip_ref[:, at + tile.start : at + tile.stop] = left.T

    mine = pl.ds(pl.multiple_of(pl.program_id(0) * chunk, chunk), chunk)
    if full:
        acc_ref[...] = nn(flip_ref[mine, :count], right0_ref[...]) + nn(
            flip_ref[mine, count:], right1_ref[...]
        )
    else:
        acc_ref[...] = nn(flip_ref[mine, :ROWS], right0_ref[:ROWS, :]) + nn(
            flip_ref[mine, count : count + ROWS], right1_ref[:ROWS, :]
        )
        for seq_len, _, right_ref, at in sides:
            for tile in tiles[1:]:

                @pl.when(tile.start < seq_len)
                def _():
                    acc_ref[...] += nn(flip_ref[mine, at + tile.start : at + tile.stop], right_ref[tile, :])

    bit = bit_ref[0]
    keep_ref[0] = acc_ref[pl.ds(pl.multiple_of(bit * half, half), half), :].astype(bf16)
    send_ref[0] = acc_ref[pl.ds(pl.multiple_of((1 - bit) * half, half), half), :].astype(bf16)


def run_grad(name, lens, pairs, cols, at, before=(), full=False, left_at=0):
    (left0, right0), (left1, right1) = pairs
    count, wide = right0.shape
    tall = D
    n_grp = lax.axis_size("grp")
    chunk = 2 * tall // n_grp
    if left0.ndim == 3:
        left_spec = pl.BlockSpec(
            (left0.shape[0], 3 * left0.shape[1] // 4, D), lambda m, n: (0, 0, 0), pipeline_mode=pl.Buffered(1)
        )
    else:
        left_spec = pl.BlockSpec((count, tall), lambda m, n: (0, left_at), pipeline_mode=pl.Buffered(1))
    right_spec = pl.BlockSpec((count, D), lambda m, n: (0, n))
    out_spec = pl.BlockSpec((1, chunk // 2, D), lambda m, n: (m, 0, n + at))
    shape = in_hbm(n_grp // 2, chunk // 2, cols)
    bit = my_bit("grp", 0).reshape(1)
    return pl.pallas_call(
        functools.partial(grad_kernel, full),
        name=name,
        grid=(n_grp // 2, wide // D),
        in_specs=[in_smem()] * 3
        + [left_spec, right_spec, left_spec, right_spec]
        + [anywhere()] * len(before),
        out_specs=[out_spec, out_spec],
        out_shape=[shape, shape],
        input_output_aliases={7: 0, 8: 1} if before else {},
        scratch_shapes=[pltpu.VMEM((tall, 2 * count), bf16), pltpu.VMEM((chunk, D), f32)],
        compiler_params=pltpu.CompilerParams(vmem_limit_bytes=48 * MIB),
        cost_estimate=COST,
    )(*lens, bit, left0, right0, left1, right1, *before)


def add_split_kernel(me_ref, kept_ref, got_ref, keep_ref, send_ref):
    for out_ref, half in ((keep_ref, me_ref[0]), (send_ref, 1 - me_ref[0])):
        total = kept_ref[0, half].astype(f32) + got_ref[0, half].astype(f32)
        out_ref[0] = total.astype(out_ref.dtype)


def add_kernel(kept_ref, got_ref, out_ref):
    out_ref[...] = kept_ref[...].astype(f32) + got_ref[...].astype(f32)


class Scatter:
    def __init__(self, name, keep, send):
        self.name = name
        self.held = device_bits()
        self.order = [p for p in reversed(self.held) if p[0] == "grp"]
        self.order += [p for p in reversed(self.held) if p[0] == "fsdp"]
        self.split()
        blocks = 1 << len(self.held)
        self.keep, self.send = (a.reshape(blocks, -1, a.shape[-1]) for a in (keep, send))
        self.block = self.keep.shape[1:]

    def split(self):
        self.bit = self.order.pop(0)
        dim = self.held.index(self.bit)
        self.held.remove(self.bit)
        return 1 << dim, 1 << (len(self.held) - dim)

    def step(self):
        got = swap(self.send, *self.bit)
        if not self.order:
            spec = pl.BlockSpec((1,) + self.block, lambda i: (0, 0, 0))
            return pl.pallas_call(
                add_kernel,
                name=self.name + "_sum",
                grid=(1,),
                in_specs=[spec, spec],
                out_specs=spec,
                out_shape=shape_of(1, *self.block, dtype=f32),
                compiler_params=pltpu.CompilerParams(vmem_limit_bytes=8 * MIB),
                cost_estimate=COST,
            )(self.keep, got).reshape(self.block)
        before, after = self.split()
        half = self.keep.shape[0] // 2
        view = (before, 2, after) + self.block
        some = min(after, 4)
        in_spec = pl.BlockSpec((1, 2, some) + self.block, lambda i, j, _: (i, 0, j, 0, 0))
        out_spec = pl.BlockSpec((1, some) + self.block, lambda i, j, _: (i, j, 0, 0))
        shape = shape_of(before, after, *self.block, dtype=self.keep.dtype)
        keep, send = pl.pallas_call(
            add_split_kernel,
            name=self.name + "_add",
            grid_spec=pltpu.PrefetchScalarGridSpec(
                num_scalar_prefetch=1,
                grid=(before, after // some),
                in_specs=[in_spec, in_spec],
                out_specs=[out_spec, out_spec],
            ),
            out_shape=[shape, shape],
            compiler_params=pltpu.CompilerParams(vmem_limit_bytes=16 * MIB),
            cost_estimate=COST,
        )(my_bit(*self.bit).reshape(1), self.keep.reshape(view), got.reshape(view))
        self.keep, self.send = (a.reshape((half,) + self.block) for a in (keep, send))

    def finish(self):
        while True:
            done = self.step()
            if done is not None:
                return done


def fence(*values):
    return lax.optimization_barrier(values)


def by_part(weight, parts):
    rows = weight.shape[0]
    return weight.reshape(rows, PAIRS, parts, PAIR).swapaxes(1, 2).reshape(rows, parts * D)


def rows_of(array):
    return array.reshape(-1, array.shape[-1])


def exchange(array):
    return lax.all_to_all(array, "fsdp", split_axis=0, concat_axis=0, tiled=True)


def shards(
    tokens,
    frames,
    lengths,
    cotangent,
    self_in,
    self_out,
    cross_q,
    cross_kv,
    cross_out,
    fc_in,
    fc_out,
    norm_gain,
    norm_bias,
):
    fsdp_count = lax.axis_size("fsdp")
    n_all = lax.axis_size("grp") * fsdp_count
    group_seqs, size = tokens.shape[:2]
    seq_ids = jnp.arange(group_seqs, dtype=jnp.int32)
    rank_order = jnp.argsort(-(lengths * group_seqs + (group_seqs - 1 - seq_ids)))
    sender = jnp.concatenate([rank_order[:fsdp_count], rank_order[fsdp_count:][::-1]])
    device = lax.axis_index("fsdp")
    len0, len1 = (
        lax.dynamic_slice_in_dim(lengths[sender], s * fsdp_count + device, 1) for s in range(2)
    )
    rows = self_in.shape[0]
    me = (lax.axis_index("grp") * fsdp_count + device).reshape(1)

    def pick(name, *parts):
        total = sum(array.shape[1] for array, _ in parts)

        def plan(seq_ref, ins, outs):
            copies, at = [], 0
            for src, (array, slot) in zip(ins, parts):
                span = slice(at, at + array.shape[1])
                at += array.shape[1]
                for j in range(fsdp_count):
                    seq = seq_ref[slot * fsdp_count + j]
                    copies.append((0, src.at[seq], outs[0].at[j, span]))
            return copies

        shape = in_hbm(fsdp_count, total, D)
        return run_copies(name, plan, sender, [array for array, _ in parts], [shape], "out")[0]

    def put_back(name, *parts):
        ins = []
        for first, _, second, _ in parts:
            ins += [a for a in (first, second) if not any(a is b for b in ins)]
        where = [[next(i for i, a in enumerate(ins) if a is p[k]) for k in (0, 2)] for p in parts]

        def plan(seq_ref, in_refs, outs):
            return [
                (o, in_refs[where[o][slot]].at[j, part[2 * slot + 1]], outs[o].at[seq_ref[slot * fsdp_count + j]])
                for o, part in enumerate(parts)
                for slot in range(2)
                for j in range(fsdp_count)
            ]

        shapes = [in_hbm(group_seqs, p[1].stop - p[1].start, D) for p in parts]
        return run_copies(name, plan, sender, ins, shapes)

    norms = jnp.pad(jnp.concatenate([norm_gain, norm_bias], axis=1), ((0, 0), (0, 120)))
    shard_one, shard_two = pack_shards(me, self_in, self_out, cross_q, norms, cross_kv, cross_out)
    w_two = gather_rows(shard_two)
    fc_up = fc_in.reshape(rows, n_all, FF_PARTS, rows).swapaxes(1, 2).reshape(rows, FF)
    fc_down = fc_out.reshape(FF_PARTS, rows, D).swapaxes(0, 1).reshape(rows, FF)
    w_fc = gather_rows(jnp.concatenate([fc_up, fc_down], axis=1))
    one = Gather(
        "one", shard_one, me, [in_hbm(n_all, rows, ONE_COLS)],
        lambda src, outs, b: [(0, src, outs[0].at[b])],
    )

    pick_a = pick("pick_first", (frames, 0), (tokens, 0))
    for _ in range(sum(1 for axis, _ in device_bits() if axis == "fsdp") - 1):
        one.step()
    (one.value, pick_a) = fence(one.value, pick_a)
    in_a = exchange(pick_a)
    pick_b = pick("pick_second", (tokens, 1), (cotangent, 0))
    pick_c = pick("pick_third", (frames, 1), (cotangent, 1))
    while len(one.left) > 1:
        one.step()
    (w_one,) = one.step()
    (in_a, w_one, pick_b, pick_c) = fence(in_a, w_one, pick_b, pick_c)
    w_one = rows_of(w_one)
    norm_rows = w_one[:, ONE_NORM : ONE_NORM + 8].T.astype(f32)

    in_b = exchange(pick_b)
    fwd0 = run_self_forward(len0, in_a, "tokens", w_one, norm_rows)
    crs0 = run_cross_forward(len0, in_a, w_two, fwd0[6])
    (in_b, fwd0, crs0, pick_c) = fence(in_b, fwd0, crs0, pick_c)

    in_c = exchange(pick_c)
    fwd1 = run_self_forward(len1, in_b, "first", w_one, norm_rows)
    mid0 = run_middle(len0, crs0[0], fwd0[4], in_b, "second", w_two, w_fc, norm_rows)
    cb0 = run_cross_backward(len0, fwd0[6], crs0[2], crs0[0], mid0[7], crs0[1], w_two, mid0[0])
    (in_c, crs0, cb0, fwd1, mid0) = fence(in_c, crs0, cb0, fwd1, mid0)

    lens = (len0, len1)

    back_a = exchange(cb0[2])
    crs1 = run_cross_forward(len1, in_c, w_two, fwd1[6])
    mid1 = run_middle(len1, crs1[0], fwd1[4], in_c, "tokens", w_two, w_fc, norm_rows)
    (crs1, mid1, mid0) = fence(crs1, mid1, mid0)
    g_up = Scatter(
        "up", *run_grad("grad_fc_in", lens, ((mid0[1], mid0[3]), (mid1[1], mid1[3])), FF, 0)
    )
    halves = ()
    for j in range(FF_PARTS):
        halves = run_grad("grad_fc_out", lens, ((mid0[2], mid0[4]), (mid1[2], mid1[4])), FF, j, halves, left_at=j)
    g_down = Scatter("down", *halves)
    g_up.step()
    g_down.step()
    (crs1, mid1, g_down.keep, g_down.send, g_up.keep, g_up.send) = fence(
        crs1, mid1, g_down.keep, g_down.send, g_up.keep, g_up.send
    )
    cb1 = run_cross_backward(len1, fwd1[6], crs1[2], crs1[0], mid1[7], crs1[1], w_two, mid1[0])
    g_down.step()
    g_up.step()
    (back_a, cb0, cb1, mid0, mid1, g_down.keep, g_down.send, g_up.keep, g_up.send) = fence(
        back_a, cb0, cb1, mid0, mid1, g_down.keep, g_down.send, g_up.keep, g_up.send
    )

    back_b = exchange(cb1[2])
    halves = run_grad("grad_cross_kv", lens, ((in_a, cb0[1]), (in_c, cb1[1])), 3 * D, 0, full=True)
    halves = run_grad(
        "grad_cross_out", lens, ((crs0[0], mid0[5]), (crs1[0], mid1[5])), 3 * D, 2, halves
    )
    g_two = Scatter("two", *halves)
    g_two.step()
    sb0 = run_self_backward(
        len0, cb0[0], mid0[6], fwd0[4], fwd0[0], fwd0[2], fwd0[3], in_a, "tokens", w_one, norm_rows, None, 0
    )
    sb1 = run_self_backward(
        len1, cb1[0], mid1[6], fwd1[4], fwd1[0], fwd1[2], fwd1[3], in_b, "first", w_one, norm_rows, sb0[2], 1
    )
    halves = run_grad("grad_self_in", lens, ((fwd0[1], sb0[1]), (fwd1[1], sb1[1])), 5 * D, 0)
    halves = run_grad("grad_self_out", lens, ((fwd0[2], sb0[0]), (fwd1[2], sb1[0])), 5 * D, 3, halves)
    halves = run_grad("grad_cross_q", lens, ((fwd0[5], cb0[0]), (fwd1[5], cb1[0])), 5 * D, 4, halves)
    g_one = Scatter("one", *halves)
    g_one.step()
    g_down.step()
    g_up.step()
    every = (back_b, sb0, sb1, g_one.keep, g_one.send, g_two.keep, g_two.send)
    every += (g_down.keep, g_down.send, g_up.keep, g_up.send)
    (back_b, sb0, sb1, g_one.keep, g_one.send, g_two.keep, g_two.send, *rest) = fence(*every)
    (g_down.keep, g_down.send, g_up.keep, g_up.send) = rest

    back_c = exchange(sb1[2])
    ng_self = sb0[3] + sb1[3]
    ng_mid = mid0[8] + mid1[8]
    norm_sum = jnp.concatenate([ng_self[:2], ng_mid[:2], ng_self[2:4], ng_mid[2:4]], axis=0)
    by_device = norm_sum.reshape(8, n_all, rows).swapaxes(0, 1).reshape(-1, 2, fsdp_count, 8 * rows)
    core = my_bit("grp", 0)
    g_norm = Scatter(
        "norms",
        *(
            lax.dynamic_index_in_dim(by_device, c, 1, keepdims=False).reshape(-1, 1, 8 * rows)
            for c in (core, 1 - core)
        ),
    )
    grad_frames, output = put_back(
        "put_frames",
        (back_a, slice(0, 3 * size), back_b, slice(0, 3 * size)),
        (back_a, slice(3 * size, 4 * size), back_b, slice(3 * size, 4 * size)),
    )
    g_one = g_one.finish()
    g_two = g_two.finish()
    g_down = g_down.finish()
    g_up = g_up.finish()
    g_norm = g_norm.finish().reshape(8, rows).T
    (grad_tokens,) = put_back("put_tokens", (back_c, slice(0, size), back_c, slice(size, 2 * size)))
    return (
        output,
        grad_tokens,
        grad_frames,
        by_part(g_one[:, :ONE_OUT], 3),
        g_one[:, ONE_OUT:ONE_Q],
        g_one[:, ONE_Q:],
        by_part(g_two[:, :TWO_OUT], 2),
        g_two[:, TWO_OUT:],
        g_up.reshape(rows, FF_PARTS, n_all, rows).swapaxes(1, 2).reshape(rows, FF),
        g_down.reshape(rows, FF_PARTS, D).swapaxes(0, 1).reshape(FF_PARTS * rows, D),
        g_norm[:, :4],
        g_norm[:, 4:],
    )


def solution(mesh):
    rows = P(("grp", "fsdp"), None)
    seqs = P("grp", "fsdp", None)
    return jax.shard_map(
        shards,
        mesh=mesh,
        in_specs=(seqs, seqs, P("grp"), seqs) + (rows,) * 9,
        out_specs=(seqs,) * 3 + (rows,) * 9,
        check_vma=False,
    )
```

```python
import functools

import jax
import jax.numpy as jnp
import numpy as np
from jax import lax
from jax.experimental import pallas as pl
from jax.experimental.pallas import tpu as pltpu
from jax.sharding import PartitionSpec as P

D = 768
FF = 3072
HEAD_DIM = 64
FRAMES = 1500
FRAME_SLOTS = 1536
PAIR = 2 * HEAD_DIM
PAIRS = D // PAIR
TILE = 128
ROWS = 256
KEY_CHUNK = 256
FF_PARTS = FF // D

eps_norm = 1e-05
neg_big = -1e30
head_scale = 0.125
bf16 = jnp.bfloat16
f32 = jnp.float32
MIB = 1024 * 1024
COST = pl.CostEstimate(flops=1000000, bytes_accessed=1000000, transcendentals=0)

ONE_OUT = 3 * D
ONE_Q = 4 * D
ONE_NORM = 5 * D
ONE_COLS = 5 * D + 128
TWO_OUT = 2 * D


def nt(left, right):
    return lax.dot_general(left, right, (((1,), (1,)), ((), ())), preferred_element_type=f32)


def nn(left, right):
    return lax.dot_general(left, right, (((1,), (0,)), ((), ())), preferred_element_type=f32)


def normalize(stream):
    centered = stream - jnp.mean(stream, axis=-1, keepdims=True)
    scale = lax.rsqrt(jnp.mean(centered * centered, axis=-1, keepdims=True) + eps_norm)
    return centered * scale, scale


def norm_backward(normed, scale, gain, grad):
    scaled = grad * gain
    mean_scaled = jnp.mean(scaled, axis=-1, keepdims=True)
    mean_along = jnp.mean(scaled * normed, axis=-1, keepdims=True)
    return scale * (scaled - mean_scaled - normed * mean_along)


def col_sum(values):
    return jnp.sum(values, axis=0, keepdims=True)


def split_heads(block):
    lanes = lax.broadcasted_iota(jnp.int32, block.shape, 1)
    zero = jnp.zeros_like(block)
    return jnp.concatenate(
        [jnp.where(lanes < HEAD_DIM, block, zero), jnp.where(lanes < HEAD_DIM, zero, block)], axis=0
    )


def join_heads(stacked):
    return jnp.concatenate([stacked[:HEAD_DIM, :TILE], stacked[HEAD_DIM:, TILE:]], axis=0).T


def row_dots(left, right):
    prod = (left.astype(f32) * right.astype(f32)).T
    return jnp.concatenate([col_sum(prod[:HEAD_DIM]), col_sum(prod[HEAD_DIM:])], axis=1)


def seen(shape, row_start, seq_len):
    keys = lax.broadcasted_iota(jnp.int32, shape, 0)
    rows = row_start + lax.rem(lax.broadcasted_iota(jnp.int32, shape, 1), TILE)
    return (keys <= rows) & (keys < seq_len)


def each_tile(count, size, body):
    def step(i, carry):
        body(pl.ds(pl.multiple_of(i * size, size), size), i)
        return carry

    lax.fori_loop(0, count, step, 0)


def lane_block(index):
    return pl.ds(pl.multiple_of(index * PAIR, PAIR), PAIR)


def token_rows(ref, tile):
    count = ROWS // ref.shape[1]
    return ref[pl.ds(tile * count, count)].reshape(ROWS, D).astype(f32)


def clear(*refs):
    for ref in refs:
        ref[...] = jnp.zeros_like(ref)


scale_of_heads = functools.partial(jnp.asarray, head_scale, bf16)


def self_part_forward(
    len_ref, tok_ref, one_ref, norm_ref,
    qkv_ref, normed_one_ref, mix_ref, lse_ref, after_ref, normed_two_ref, q_two_ref,
    vt_ref,
):
    seq_len = len_ref[0]
    row_tiles = pl.cdiv(seq_len, ROWS)
    clear(normed_one_ref, mix_ref, lse_ref, normed_two_ref)

    def project(rows, i):
        normed, _ = normalize(token_rows(tok_ref, i))
        normed = (normed * norm_ref[0:1, :] + norm_ref[4:5, :]).astype(bf16)
        normed_one_ref[rows, :] = normed
        qkv_ref[rows, :] = nn(normed, one_ref[:, :ONE_OUT]).astype(bf16)

    each_tile(row_tiles, ROWS, project)

    def per_pair(pair, carry):
        q_lanes, k_lanes, v_lanes = (lane_block(3 * pair + i) for i in range(3))
        for tile in range(qkv_ref.shape[0] // TILE):

            @pl.when(tile * TILE < seq_len)
            def _():
                rows = slice(tile * TILE, (tile + 1) * TILE)
                size = (tile + 1) * TILE
                vt_ref[:, rows] = qkv_ref[rows, v_lanes].T
                queries = split_heads(qkv_ref[rows, q_lanes] * scale_of_heads())
                scores = nt(qkv_ref[:size, k_lanes], queries)
                scores = jnp.where(seen(scores.shape, tile * TILE, seq_len), scores, neg_big)
                peak = jnp.max(scores, axis=0, keepdims=True)
                probs = jnp.exp(scores - peak)
                total = col_sum(probs)
                mixed = nn(vt_ref[:, :size], probs.astype(bf16))
                mix_ref[rows, lane_block(pair)] = join_heads(mixed / total).astype(bf16)
                lse_ref[pair, tile : tile + 1, :] = peak + jnp.log(total)

        return carry

    lax.fori_loop(0, PAIRS, per_pair, 0)

    def finish(rows, i):
        after = token_rows(tok_ref, i) + nn(mix_ref[rows, :], one_ref[:, ONE_OUT:ONE_Q])
        after_ref[rows, :] = after
        normed, _ = normalize(after)
        normed = (normed * norm_ref[1:2, :] + norm_ref[5:6, :]).astype(bf16)
        normed_two_ref[rows, :] = normed
        q_two_ref[rows, :] = nn(normed, one_ref[:, ONE_Q:ONE_NORM]).astype(bf16)

    each_tile(row_tiles, ROWS, finish)


PARTS = {"frames": 4, "tokens": 4, "first": 2, "second": 2, "all": 1}


def part_at(part):
    return {"frames": 0, "tokens": 3, "first": 0, "second": 1, "all": 0}[part]


def whole():
    return pl.BlockSpec(memory_space=pltpu.VMEM)


def in_smem():
    return pl.BlockSpec(memory_space=pltpu.SMEM)


def shape_of(*dims, dtype=bf16):
    return jax.ShapeDtypeStruct(dims, dtype)


def in_hbm(*dims, dtype=bf16):
    return pltpu.HBM(dims, dtype)


def run_self_forward(seq_len, arrived, part, one, norm_rows):
    blocks, size = arrived.shape[0], arrived.shape[1] // PARTS[part]
    at = part_at(part)
    rows = blocks * size
    fixed = lambda *dims: pl.BlockSpec(dims, lambda i: (0,) * len(dims), pipeline_mode=pl.Buffered(1))
    shapes = [
        in_hbm(rows, 3 * D),
        in_hbm(rows, D),
        in_hbm(rows, D),
        in_hbm(PAIRS, rows // TILE, 2 * TILE, dtype=f32),
        in_hbm(rows, D, dtype=f32),
        in_hbm(rows, D),
        in_hbm(rows, D),
    ]
    return pl.pallas_call(
        self_part_forward,
        name="self_part_forward",
        grid=(1,),
        in_specs=[
            in_smem(),
            pl.BlockSpec((blocks, size, D), lambda i: (0, at, 0), pipeline_mode=pl.Buffered(1)),
            fixed(*one.shape),
            fixed(8, D),
        ],
        out_specs=[fixed(*s.shape) for s in shapes],
        out_shape=shapes,
        scratch_shapes=[pltpu.VMEM((PAIR, rows), bf16)],
        compiler_params=pltpu.CompilerParams(vmem_limit_bytes=36 * MIB),
        cost_estimate=COST,
    )(seq_len, arrived, one, norm_rows)


def cross_forward_kernel(len_ref, frm_ref, w_ref, q_ref, out_ref, lse_ref, kv_ref, vt_ref, s_ref):
    slots = kv_ref.shape[0]
    clear(out_ref, lse_ref)
    kv_ref[...] = nn(frm_ref[...].reshape(slots, D), w_ref[...]).astype(bf16)
    vt_ref[...] = kv_ref[:, PAIR:].T
    spans = [(k, min(KEY_CHUNK, slots - k)) for k in range(0, slots, KEY_CHUNK)]

    def per_tile(rows, tile):
        queries = split_heads(q_ref[rows, :] * scale_of_heads())
        peak = jnp.full((1, 2 * TILE), neg_big, f32)
        for start, size in spans:
            scores = nt(kv_ref[start : start + size, :PAIR], queries)
            if start + size > FRAMES:
                keys = start + lax.broadcasted_iota(jnp.int32, scores.shape, 0)
                scores = jnp.where(keys < FRAMES, scores, neg_big)
            s_ref[start : start + size, :] = scores
            peak = jnp.maximum(peak, jnp.max(scores, axis=0, keepdims=True))
        total = jnp.zeros((1, 2 * TILE), f32)
        mixed = jnp.zeros((PAIR, 2 * TILE), f32)
        for start, size in spans:
            probs = jnp.exp(s_ref[start : start + size, :] - peak)
            total = total + col_sum(probs)
            mixed = mixed + nn(vt_ref[:, start : start + size], probs.astype(bf16))
        out_ref[rows, :] = join_heads(mixed / total).astype(bf16)
        lse_ref[0, pl.ds(tile, 1), :] = peak + jnp.log(total)

    each_tile(pl.cdiv(len_ref[0], TILE), TILE, per_tile)


def frame_rows(arrived):
    return FRAME_SLOTS // arrived.shape[0]


def run_cross_forward(seq_len, arrived, two, q_two):
    blocks, size = arrived.shape[0], frame_rows(arrived)
    rows, slots = q_two.shape[0], blocks * size
    tiles = rows // TILE
    return pl.pallas_call(
        cross_forward_kernel,
        name="cross_forward",
        grid=(PAIRS,),
        in_specs=[
            in_smem(),
            pl.BlockSpec((blocks, size, D), lambda h: (0, 0, 0), pipeline_mode=pl.Buffered(1)),
            pl.BlockSpec((D, 2 * PAIR), lambda h: (0, h)),
            pl.BlockSpec((rows, PAIR), lambda h: (0, h)),
        ],
        out_specs=[
            pl.BlockSpec((rows, PAIR), lambda h: (0, h)),
            pl.BlockSpec((1, tiles, 2 * TILE), lambda h: (h, 0, 0)),
            pl.BlockSpec((slots, 2 * PAIR), lambda h: (0, h)),
        ],
        out_shape=[
            in_hbm(rows, D),
            in_hbm(PAIRS, tiles, 2 * TILE, dtype=f32),
            in_hbm(slots, 2 * D),
        ],
        scratch_shapes=[pltpu.VMEM((PAIR, slots), bf16), pltpu.VMEM((slots, 2 * TILE), f32)],
        compiler_params=pltpu.CompilerParams(vmem_limit_bytes=24 * MIB),
        cost_estimate=COST,
    )(seq_len, arrived, two, q_two)


def cross_backward_kernel(
    len_ref, q_ref, kv_ref, mix_ref, grad_ref, lse_ref, w_ref, _,
    dq_ref, dkv_ref, dfrm_ref,
    kt_ref, dk_ref, dv_ref, acc_ref,
):
    slots = kv_ref.shape[0]
    pair = pl.program_id(0)
    kt_ref[...] = kv_ref[:, :PAIR].T
    clear(dq_ref, dk_ref, dv_ref)
    spans = [(k, min(KEY_CHUNK, slots - k)) for k in range(0, slots, KEY_CHUNK)]

    def per_tile(rows, tile):
        queries = split_heads(q_ref[rows, :] * scale_of_heads())
        grads = split_heads(grad_ref[rows, :])
        inner = row_dots(mix_ref[rows, :], grad_ref[rows, :])
        lse = lse_ref[0, pl.ds(tile, 1), :]
        dq = jnp.zeros((PAIR, 2 * TILE), f32)
        for start, size in spans:
            span = slice(start, start + size)
            probs = jnp.exp(nt(kv_ref[span, :PAIR], queries) - lse)
            if start + size > FRAMES:
                keys = start + lax.broadcasted_iota(jnp.int32, probs.shape, 0)
                probs = jnp.where(keys < FRAMES, probs, 0.0)
            dscores = (probs * (nt(kv_ref[span, PAIR:], grads) - inner)).astype(bf16)
            dv_ref[span, :] += nn(probs.astype(bf16), grads)
            dk_ref[span, :] += nn(dscores, queries)
            dq = dq + nn(kt_ref[:, span], dscores)
        dq_ref[rows, :] = join_heads(dq).astype(bf16) * scale_of_heads()

    each_tile(pl.cdiv(len_ref[0], TILE), TILE, per_tile)
    dkv_ref[:, :PAIR] = dk_ref[...].astype(bf16)
    dkv_ref[:, PAIR:] = dv_ref[...].astype(bf16)
    part = nt(dkv_ref[...], w_ref[...])

    @pl.when(pair == 0)
    def _():
        acc_ref[...] = part

    @pl.when((pair > 0) & (pair < PAIRS - 1))
    def _():
        acc_ref[...] += part

    @pl.when(pair == PAIRS - 1)
    def _():
        dfrm_ref[...] = (acc_ref[...] + part).astype(bf16).reshape(dfrm_ref.shape)


def run_cross_backward(seq_len, q_two, kv, mix, grad_mix, lse, two, leaving):
    rows, slots, blocks = q_two.shape[0], kv.shape[0], leaving.shape[0]
    tiles = rows // TILE
    row_spec = pl.BlockSpec((rows, PAIR), lambda h: (0, h))
    kv_spec = pl.BlockSpec((slots, 2 * PAIR), lambda h: (0, h))
    return pl.pallas_call(
        cross_backward_kernel,
        name="cross_backward",
        grid=(PAIRS,),
        in_specs=[
            in_smem(),
            row_spec,
            kv_spec,
            row_spec,
            row_spec,
            pl.BlockSpec((1, tiles, 2 * TILE), lambda h: (h, 0, 0)),
            pl.BlockSpec((D, 2 * PAIR), lambda h: (0, h)),
            pl.BlockSpec(memory_space=pl.ANY),
        ],
        out_specs=[
            row_spec,
            kv_spec,
            pl.BlockSpec((blocks, slots // blocks, D), lambda h: (0, 0, 0), pipeline_mode=pl.Buffered(1)),
        ],
        out_shape=[in_hbm(rows, D), in_hbm(slots, 2 * D), in_hbm(*leaving.shape)],
        input_output_aliases={7: 2},
        scratch_shapes=[
            pltpu.VMEM((PAIR, slots), bf16),
            pltpu.VMEM((slots, PAIR), f32),
            pltpu.VMEM((slots, PAIR), f32),
            pltpu.VMEM((slots, D), f32),
        ],
        compiler_params=pltpu.CompilerParams(vmem_limit_bytes=36 * MIB),
        cost_estimate=COST,
    )(seq_len, q_two, kv, mix, grad_mix, lse, two, leaving)


def middle_kernel(
    len_ref, mix_ref, after_ref, cot_ref, two_ref, fc_ref, norm_ref,
    out_ref, normed_ref, hidden_ref, grad_pre_ref, branch_three_ref, branch_two_ref,
    grad_cross_ref, grad_mix_ref, norm_grad_ref,
    slope_ref,
):
    seq_len = len_ref[0]
    step = pl.program_id(0)
    parts = [(slice(k, k + D), slice(FF + k, FF + k + D)) for k in range(0, FF, D)]

    @pl.when(step == 0)
    def _():
        clear(norm_grad_ref)

    @pl.when(step * ROWS >= seq_len)
    def _():
        clear(out_ref, normed_ref, hidden_ref, grad_pre_ref, branch_three_ref, branch_two_ref)
        clear(grad_cross_ref, grad_mix_ref)

    @pl.when(step * ROWS < seq_len)
    def _():
        w_out = two_ref[:, TWO_OUT:]
        after_cross = after_ref[...] + nn(mix_ref[...], w_out)
        n_three, scale_three = normalize(after_cross)
        normed = (n_three * norm_ref[2:3, :] + norm_ref[6:7, :]).astype(bf16)
        normed_ref[...] = normed
        mlp = jnp.zeros((ROWS, D), f32)
        for span, rows_out in parts:
            pre = nn(normed, fc_ref[:, span])
            below = 0.5 * (1.0 + lax.erf(pre * np.float32(np.sqrt(0.5))))
            density = jnp.exp(-0.5 * pre * pre) * np.float32(1.0 / np.sqrt(2.0 * np.pi))
            slope_ref[:, span] = below + pre * density
            hidden = (pre * below).astype(bf16)
            hidden_ref[:, span] = hidden
            mlp = mlp + nn(hidden, fc_ref[:, rows_out])
        n_four, scale_four = normalize(after_cross + mlp)
        row_ids = step * ROWS + lax.broadcasted_iota(jnp.int32, (ROWS, 1), 0)
        valid = (row_ids < seq_len).astype(f32)
        output = ((n_four * norm_ref[3:4, :] + norm_ref[7:8, :]) * valid).astype(bf16)
        out_ref[...] = output.reshape(out_ref.shape)

        grad = cot_ref[...].reshape(ROWS, D).astype(f32) * valid
        norm_grad_ref[1:2, :] += col_sum(grad * n_four)
        norm_grad_ref[3:4, :] += col_sum(grad)
        grad_mlp = norm_backward(n_four, scale_four, norm_ref[3:4, :], grad)
        branch_three = grad_mlp.astype(bf16)
        branch_three_ref[...] = branch_three
        back = jnp.zeros((ROWS, D), f32)
        for span, rows_out in parts:
            grad_pre = (nt(branch_three, fc_ref[:, rows_out]) * slope_ref[:, span]).astype(bf16)
            grad_pre_ref[:, span] = grad_pre
            back = back + nt(grad_pre, fc_ref[:, span])
        norm_grad_ref[0:1, :] += col_sum(back * n_three)
        norm_grad_ref[2:3, :] += col_sum(back)
        grad_cross = grad_mlp + norm_backward(n_three, scale_three, norm_ref[2:3, :], back)
        grad_cross_ref[...] = grad_cross
        branch_two = grad_cross.astype(bf16)
        branch_two_ref[...] = branch_two
        grad_mix_ref[...] = nt(branch_two, w_out).astype(bf16)


def run_middle(seq_len, mix, after, arrived, part, two, fc, norm_rows):
    rows, blocks = mix.shape[0], arrived.shape[0]
    size = rows // blocks
    at = part_at(part)
    count = ROWS // size
    row_spec = pl.BlockSpec((ROWS, D), lambda i: (i, 0))
    wide_spec = pl.BlockSpec((ROWS, FF), lambda i: (i, 0))

    def fixed(*dims):
        return pl.BlockSpec(dims, lambda i: (0, 0), pipeline_mode=pl.Buffered(1))

    return pl.pallas_call(
        middle_kernel,
        name="mlp_and_back",
        grid=(rows // ROWS,),
        in_specs=[
            in_smem(), row_spec, row_spec, pl.BlockSpec((count, size, D), lambda i: (i, at, 0)),
            fixed(D, 3 * D), fixed(D, 2 * FF), fixed(8, D),
        ],
        out_specs=[pl.BlockSpec((count, size, D), lambda i: (i, 3, 0)), row_spec, wide_spec, wide_spec, row_spec, row_spec, row_spec, row_spec,
                   pl.BlockSpec((8, D), lambda i: (0, 0))],
        out_shape=[
            in_hbm(blocks, 4 * size, D), in_hbm(rows, D), in_hbm(rows, FF), in_hbm(rows, FF),
            in_hbm(rows, D), in_hbm(rows, D), in_hbm(rows, D, dtype=f32), in_hbm(rows, D),
            in_hbm(8, D, dtype=f32),
        ],
        scratch_shapes=[pltpu.VMEM((ROWS, FF), f32)],
        compiler_params=pltpu.CompilerParams(vmem_limit_bytes=48 * MIB),
        cost_estimate=COST,
    )(seq_len, mix, after, arrived, two, fc, norm_rows)


def self_part_backward(
    len_ref, dq_ref, grad_cross_ref, after_ref, qkv_ref, mix_ref, lse_ref, tok_ref, one_ref, norm_ref, _,
    branch_ref, dqkv_ref, grad_tok_ref, norm_grad_ref,
    attn_ref, grad_mix_ref, kt_ref, dk_ref, dv_ref,
):
    seq_len = len_ref[0]
    row_tiles = pl.cdiv(seq_len, ROWS)
    clear(branch_ref, dqkv_ref, grad_tok_ref, norm_grad_ref)

    def enter(rows, _):
        normed, scale = normalize(after_ref[rows, :])
        grad = nt(dq_ref[rows, :], one_ref[:, ONE_Q:ONE_NORM])
        norm_grad_ref[1:2, :] += col_sum(grad * normed)
        norm_grad_ref[3:4, :] += col_sum(grad)
        attn = grad_cross_ref[rows, :] + norm_backward(normed, scale, norm_ref[1:2, :], grad)
        attn_ref[rows, :] = attn
        branch = attn.astype(bf16)
        branch_ref[rows, :] = branch
        grad_mix_ref[rows, :] = nt(branch, one_ref[:, ONE_OUT:ONE_Q]).astype(bf16)

    each_tile(row_tiles, ROWS, enter)

    def per_pair(pair, carry):
        q_lanes, k_lanes, v_lanes = (lane_block(3 * pair + i) for i in range(3))
        clear(dk_ref, dv_ref)
        for tile in range(qkv_ref.shape[0] // TILE):

            @pl.when(tile * TILE < seq_len)
            def _():
                rows = slice(tile * TILE, (tile + 1) * TILE)
                size = (tile + 1) * TILE
                kt_ref[:, rows] = qkv_ref[rows, k_lanes].T
                queries = split_heads(qkv_ref[rows, q_lanes] * scale_of_heads())
                grad_mix = grad_mix_ref[rows, lane_block(pair)]
                grads = split_heads(grad_mix)
                inner = row_dots(mix_ref[rows, lane_block(pair)], grad_mix)
                scores = nt(qkv_ref[:size, k_lanes], queries)
                scores = jnp.where(seen(scores.shape, tile * TILE, seq_len), scores, neg_big)
                probs = jnp.exp(scores - lse_ref[pair, tile : tile + 1, :])
                dscores = (probs * (nt(qkv_ref[:size, v_lanes], grads) - inner)).astype(bf16)
                dv_ref[:size, :] += nn(probs.astype(bf16), grads)
                dk_ref[:size, :] += nn(dscores, queries)
                dq = nn(kt_ref[:, :size], dscores)
                dqkv_ref[rows, q_lanes] = join_heads(dq).astype(bf16) * scale_of_heads()

        dqkv_ref[:, k_lanes] = dk_ref[...].astype(bf16)
        dqkv_ref[:, v_lanes] = dv_ref[...].astype(bf16)
        return carry

    lax.fori_loop(0, PAIRS, per_pair, 0)

    def leave(rows, i):
        normed, scale = normalize(token_rows(tok_ref, i))
        grad = nt(dqkv_ref[rows, :], one_ref[:, :ONE_OUT])
        norm_grad_ref[0:1, :] += col_sum(grad * normed)
        norm_grad_ref[2:3, :] += col_sum(grad)
        total = attn_ref[rows, :] + norm_backward(normed, scale, norm_ref[0:1, :], grad)
        count = ROWS // grad_tok_ref.shape[1]
        grad_tok_ref[pl.ds(i * count, count)] = total.astype(bf16).reshape(count, -1, D)

    each_tile(row_tiles, ROWS, leave)


def run_self_backward(seq_len, dq, grad_cross, after, qkv, mix, lse, arrived, part, one, norm_rows, leaving, slot):
    blocks, size = arrived.shape[0], arrived.shape[1] // PARTS[part]
    at = part_at(part)
    rows = blocks * size
    fixed = lambda *dims: pl.BlockSpec(dims, lambda i: (0,) * len(dims), pipeline_mode=pl.Buffered(1))
    spec = lambda block: pl.BlockSpec(
        (blocks, size, D), lambda i: (0, block, 0), pipeline_mode=pl.Buffered(1)
    )
    before = [] if leaving is None else [leaving]
    body = self_part_backward
    if leaving is None:
        body = lambda *refs: self_part_backward(*refs[:10], None, *refs[10:])
    return pl.pallas_call(
        body,
        name="self_part_backward",
        grid=(1,),
        in_specs=[in_smem()]
        + [fixed(*a.shape) for a in (dq, grad_cross, after, qkv, mix, lse)]
        + [spec(at), fixed(*one.shape), fixed(8, D)]
        + [anywhere()] * len(before),
        out_specs=[fixed(rows, D), fixed(rows, 3 * D), spec(slot), fixed(8, D)],
        out_shape=[
            in_hbm(rows, D),
            in_hbm(rows, 3 * D),
            in_hbm(blocks, 2 * size, D),
            in_hbm(8, D, dtype=f32),
        ],
        input_output_aliases={10: 2} if before else {},
        scratch_shapes=[
            pltpu.VMEM((rows, D), f32),
            pltpu.VMEM((rows, D), bf16),
            pltpu.VMEM((PAIR, rows), bf16),
            pltpu.VMEM((rows, PAIR), f32),
            pltpu.VMEM((rows, PAIR), f32),
        ],
        compiler_params=pltpu.CompilerParams(vmem_limit_bytes=40 * MIB),
        cost_estimate=COST,
    )(seq_len, dq, grad_cross, after, qkv, mix, lse, arrived, one, norm_rows, *before)


def anywhere():
    return pl.BlockSpec(memory_space=pl.ANY)


def copy_kernel(plan, n_in, n_out, scalar_ref, *refs):
    ins, outs, sem = refs[:n_in], refs[n_in : n_in + n_out], refs[-1]
    for which, src, dst in plan(scalar_ref, ins, outs):
        pltpu.make_async_copy(src, dst, sem.at[which]).start()
    for which, out in enumerate(outs):
        pltpu.make_async_copy(out, out, sem.at[which]).wait()


def run_copies(name, plan, scalars, ins, out_shapes, stage="in"):
    vmem = pl.BlockSpec(memory_space=pltpu.VMEM)
    return pl.pallas_call(
        functools.partial(copy_kernel, plan, len(ins), len(out_shapes)),
        name=name,
        in_specs=[in_smem()] + [vmem if stage == "in" else pl.BlockSpec(memory_space=pltpu.HBM)] * len(ins),
        out_specs=[vmem if stage == "out" else anywhere()] * len(out_shapes),
        out_shape=out_shapes,
        scratch_shapes=[pltpu.SemaphoreType.DMA((len(out_shapes),))],
        compiler_params=pltpu.CompilerParams(vmem_limit_bytes=16 * MIB),
        cost_estimate=pl.CostEstimate(flops=0, bytes_accessed=1000, transcendentals=0),
    )(scalars, *ins)


def device_bits():
    return [
        (axis, b)
        for axis in ("grp", "fsdp")
        for b in reversed(range(lax.axis_size(axis).bit_length() - 1))
    ]


def swap(array, axis, b):
    return lax.ppermute(array, axis, [(i, i ^ (1 << b)) for i in range(lax.axis_size(axis))])


def bit_mask(axis, b):
    return (1 << b) if axis == "fsdp" else lax.axis_size("fsdp") << b


def my_bit(axis, b):
    return (lax.axis_index(axis) >> b) & 1


class Gather:
    def __init__(self, name, shard, me, outs, pieces):
        self.name = name
        bits = device_bits()
        self.left = [p for p in bits if p[0] == "fsdp"] + [p for p in bits if p[0] == "grp"]
        self.masks = [0]
        self.value = shard[None]
        self.me = me
        self.outs = outs
        self.pieces = pieces
        self.got = None

    def send(self):
        self.got = swap(self.value, *self.left[0])

    def take(self):
        mask = bit_mask(*self.left.pop(0))
        masks = self.masks
        self.masks = masks + [mask ^ m for m in masks]
        k = len(masks)
        if self.left:

            def plan(_, ins, outs):
                return [(0, ins[0], outs[0].at[:k]), (0, ins[1], outs[0].at[k:])]

            shape = (2 * k,) + self.value.shape[1:]
            (self.value,) = run_copies(
                self.name + "_join", plan, self.me, [self.value, self.got], [in_hbm(*shape)]
            )
            return self.value

        def plan(me_ref, ins, outs):
            me = me_ref[0]
            return [
                (which, src, dst)
                for i in range(k)
                for half, src_ref in ((0, ins[0]), (k, ins[1]))
                for which, src, dst in self.pieces(src_ref.at[i], outs, me ^ self.masks[half + i])
            ]

        self.value = run_copies(
            self.name + "_order", plan, self.me, [self.value, self.got], self.outs
        )
        return self.value

    def step(self):
        self.send()
        return self.take()


def pack_shards(me, self_in, self_out, cross_q, norms, cross_kv, cross_out):
    rows = self_in.shape[0]

    def plan(_, ins, outs):
        w_in, w_out, w_q, w_norm, w_kv, w_cross = ins
        one, two = outs
        copies = []
        for pair in range(PAIRS):
            for o, w, parts in ((0, w_in, 3), (1, w_kv, 2)):
                for part in range(parts):
                    src = w.at[:, part * D + pair * PAIR : part * D + (pair + 1) * PAIR]
                    at = (parts * pair + part) * PAIR
                    copies.append((o, src, outs[o].at[:, at : at + PAIR]))
        copies.append((0, w_out, one.at[:, ONE_OUT:ONE_Q]))
        copies.append((0, w_q, one.at[:, ONE_Q:ONE_NORM]))
        copies.append((0, w_norm, one.at[:, ONE_NORM:]))
        copies.append((1, w_cross, two.at[:, TWO_OUT:]))
        return copies

    ins = [self_in, self_out, cross_q, norms, cross_kv, cross_out]
    shapes = [in_hbm(rows, ONE_COLS), in_hbm(rows, 3 * D)]
    return run_copies("pack_shards", plan, me, ins, shapes, "out")


def gather_rows(shard):
    return lax.all_gather(shard, ("grp", "fsdp"), axis=0, tiled=True)


def grad_kernel(
    full, len0_ref, len1_ref, bit_ref, left0_ref, right0_ref, left1_ref, right1_ref, *refs
):
    keep_ref, send_ref, flip_ref, acc_ref = refs[-4:]
    chunk, half, count = acc_ref.shape[0], acc_ref.shape[0] // 2, right0_ref.shape[0]
    sides = (
        (len0_ref[0], left0_ref, right0_ref, 0),
        (len1_ref[0], left1_ref, right1_ref, count),
    )
    tiles = [slice(k, k + ROWS) for k in range(0, count, ROWS)]

    @pl.when((pl.program_id(0) == 0) & (pl.program_id(1) == 0))
    def _():
        for seq_len, left_ref, _, at in sides:
            for tile in tiles:

                @pl.when(jnp.logical_or(full or tile.start == 0, tile.start < seq_len))
                def _():
                    if len(left_ref.shape) == 3:
                        size = left_ref.shape[1]
                        left = left_ref[tile.start // size : (tile.stop + size - 1) // size]
                        skip = tile.start % size
                        left = left.reshape(-1, D)[skip : skip + ROWS]
                    else:
                        left = left_ref[tile, :]
                    flip_ref[:, at + tile.start : at + tile.stop] = left.T

    mine = pl.ds(pl.multiple_of(pl.program_id(0) * chunk, chunk), chunk)
    if full:
        acc_ref[...] = nn(flip_ref[mine, :count], right0_ref[...]) + nn(
            flip_ref[mine, count:], right1_ref[...]
        )
    else:
        acc_ref[...] = nn(flip_ref[mine, :ROWS], right0_ref[:ROWS, :]) + nn(
            flip_ref[mine, count : count + ROWS], right1_ref[:ROWS, :]
        )
        for seq_len, _, right_ref, at in sides:
            for tile in tiles[1:]:

                @pl.when(tile.start < seq_len)
                def _():
                    acc_ref[...] += nn(flip_ref[mine, at + tile.start : at + tile.stop], right_ref[tile, :])

    bit = bit_ref[0]
    keep_ref[0] = acc_ref[pl.ds(pl.multiple_of(bit * half, half), half), :].astype(bf16)
    send_ref[0] = acc_ref[pl.ds(pl.multiple_of((1 - bit) * half, half), half), :].astype(bf16)


def fc_grad_kernel(
    len0_ref, len1_ref, normed0_ref, pre0_ref, hid0_ref, branch0_ref, normed1_ref, pre1_ref, hid1_ref, branch1_ref,
    out_ref, flip_ref, acc_ref,
):
    step = pl.program_id(0)
    count = normed0_ref.shape[0]
    tiles = [slice(k, k + ROWS) for k in range(0, count, ROWS)]
    sides = (
        (len0_ref[0], normed0_ref, pre0_ref, hid0_ref, branch0_ref, 0),
        (len1_ref[0], normed1_ref, pre1_ref, hid1_ref, branch1_ref, count),
    )

    def flip(pick):
        for side in sides:
            for tile in tiles:

                @pl.when(jnp.logical_or(tile.start == 0, tile.start < side[0]))
                def _():
                    flip_ref[:, side[5] + tile.start : side[5] + tile.stop] = side[pick][tile, :].T

    def multiply(pick):
        acc_ref[...] = nn(flip_ref[:, :ROWS], sides[0][pick][:ROWS, :]) + nn(
            flip_ref[:, count : count + ROWS], sides[1][pick][:ROWS, :]
        )
        for side in sides:
            for tile in tiles[1:]:

                @pl.when(tile.start < side[0])
                def _():
                    at = side[5]
                    acc_ref[...] += nn(flip_ref[:, at + tile.start : at + tile.stop], side[pick][tile, :])

        out_ref[...] = acc_ref[...].astype(bf16)

    @pl.when(step == 0)
    def _():
        flip(1)

    @pl.when(step < FF_PARTS)
    def _():
        multiply(2)

    @pl.when(step >= FF_PARTS)
    def _():
        flip(3)
        multiply(4)


def norm_grad_kernel(bit_ref, norm_ref, _, __, keep_ref, send_ref, flip_ref):
    flip_ref[...] = jnp.concatenate([norm_ref[...], jnp.zeros((PAIR - 8, D), f32)], axis=0).T
    size = keep_ref.shape[1]
    for i in range(keep_ref.shape[0]):
        for out_ref, bit in ((keep_ref, bit_ref[0]), (send_ref, 1 - bit_ref[0])):
            at = pl.multiple_of((2 * i + bit) * size, size)
            out_ref[i] = flip_ref[pl.ds(at, size), :].astype(bf16)


def put_norm_grad(norm_sum, halves):
    count, size, cols = halves[0].shape
    spec = pl.BlockSpec((count, size, PAIR), lambda i: (0, 0, cols // PAIR - 1))
    return pl.pallas_call(
        norm_grad_kernel,
        name="put_norm_grad",
        grid=(1,),
        in_specs=[in_smem(), pl.BlockSpec((8, D), lambda i: (0, 0)), anywhere(), anywhere()],
        out_specs=[spec, spec],
        out_shape=[in_hbm(*h.shape) for h in halves],
        input_output_aliases={2: 0, 3: 1},
        scratch_shapes=[pltpu.VMEM((D, PAIR), f32)],
        compiler_params=pltpu.CompilerParams(vmem_limit_bytes=8 * MIB),
        cost_estimate=COST,
    )(my_bit("grp", 0).reshape(1), norm_sum, *halves)


def run_fc_grad(lens, side0, side1):
    count = side0[0].shape[0]
    whole_spec = pl.BlockSpec((count, D), lambda i: (0, 0), pipeline_mode=pl.Buffered(1))
    pre_spec = pl.BlockSpec((count, D), lambda i: (0, jnp.minimum(i, FF_PARTS - 1)))
    hid_spec = pl.BlockSpec((count, D), lambda i: (0, jnp.maximum(i - FF_PARTS, 0)))
    return pl.pallas_call(
        fc_grad_kernel,
        name="grad_fc",
        grid=(2 * FF_PARTS,),
        in_specs=[in_smem()] * 2 + [whole_spec, pre_spec, hid_spec, whole_spec] * 2,
        out_specs=pl.BlockSpec((D, D), lambda i: (0, i)),
        out_shape=in_hbm(D, 2 * FF),
        scratch_shapes=[pltpu.VMEM((D, 2 * count), bf16), pltpu.VMEM((D, D), f32)],
        compiler_params=pltpu.CompilerParams(vmem_limit_bytes=32 * MIB),
        cost_estimate=COST,
    )(*lens, *side0, *side1)


def run_grad(name, lens, pairs, cols, at, before=(), full=False):
    (left0, right0), (left1, right1) = pairs
    count, wide = right0.shape
    tall = D
    n_grp = lax.axis_size("grp")
    chunk = 2 * tall // n_grp
    def left_spec(left):
        if left.ndim == 3:
            block = (left.shape[0], frame_rows(left), D)
            return pl.BlockSpec(block, lambda m, n: (0, 0, 0), pipeline_mode=pl.Buffered(1))
        return pl.BlockSpec((count, tall), lambda m, n: (0, 0), pipeline_mode=pl.Buffered(1))

    right_spec = pl.BlockSpec((count, D), lambda m, n: (0, n))
    out_spec = pl.BlockSpec((1, chunk // 2, D), lambda m, n: (m, 0, n + at))
    shape = in_hbm(n_grp // 2, chunk // 2, cols)
    bit = my_bit("grp", 0).reshape(1)
    return pl.pallas_call(
        functools.partial(grad_kernel, full),
        name=name,
        grid=(n_grp // 2, wide // D),
        in_specs=[in_smem()] * 3
        + [left_spec(left0), right_spec, left_spec(left1), right_spec]
        + [anywhere()] * len(before),
        out_specs=[out_spec, out_spec],
        out_shape=[shape, shape],
        input_output_aliases={7: 0, 8: 1} if before else {},
        scratch_shapes=[pltpu.VMEM((tall, 2 * count), bf16), pltpu.VMEM((chunk, D), f32)],
        compiler_params=pltpu.CompilerParams(vmem_limit_bytes=48 * MIB),
        cost_estimate=COST,
    )(*lens, bit, left0, right0, left1, right1, *before)


def add_split_kernel(me_ref, kept_ref, got_ref, keep_ref, send_ref):
    for out_ref, half in ((keep_ref, me_ref[0]), (send_ref, 1 - me_ref[0])):
        total = kept_ref[0, half].astype(f32) + got_ref[0, half].astype(f32)
        out_ref[0] = total.astype(out_ref.dtype)


def add_kernel(kept_ref, got_ref, out_ref):
    out_ref[...] = kept_ref[...].astype(f32) + got_ref[...].astype(f32)


class Scatter:
    def __init__(self, name, keep, send):
        self.name = name
        self.held = device_bits()
        self.order = [p for p in reversed(self.held) if p[0] == "grp"]
        self.order += [p for p in reversed(self.held) if p[0] == "fsdp"]
        self.split()
        blocks = 1 << len(self.held)
        self.keep, self.send = (a.reshape(blocks, -1, a.shape[-1]) for a in (keep, send))
        self.block = self.keep.shape[1:]

    def split(self):
        self.bit = self.order.pop(0)
        dim = self.held.index(self.bit)
        self.held.remove(self.bit)
        return 1 << dim, 1 << (len(self.held) - dim)

    def move(self):
        self.got = swap(self.send, *self.bit)

    def step(self):
        self.move()
        return self.take()

    def take(self):
        got = self.got
        if not self.order:
            spec = pl.BlockSpec((1,) + self.block, lambda i: (0, 0, 0))
            return pl.pallas_call(
                add_kernel,
                name=self.name + "_sum",
                grid=(1,),
                in_specs=[spec, spec],
                out_specs=spec,
                out_shape=shape_of(1, *self.block, dtype=f32),
                compiler_params=pltpu.CompilerParams(vmem_limit_bytes=8 * MIB),
                cost_estimate=COST,
            )(self.keep, got).reshape(self.block)
        before, after = self.split()
        half = self.keep.shape[0] // 2
        view = (before, 2, after) + self.block
        some = min(after, 4)
        in_spec = pl.BlockSpec((1, 2, some) + self.block, lambda i, j, _: (i, 0, j, 0, 0))
        out_spec = pl.BlockSpec((1, some) + self.block, lambda i, j, _: (i, j, 0, 0))
        shape = shape_of(before, after, *self.block, dtype=self.keep.dtype)
        keep, send = pl.pallas_call(
            add_split_kernel,
            name=self.name + "_add",
            grid_spec=pltpu.PrefetchScalarGridSpec(
                num_scalar_prefetch=1,
                grid=(before, after // some),
                in_specs=[in_spec, in_spec],
                out_specs=[out_spec, out_spec],
            ),
            out_shape=[shape, shape],
            compiler_params=pltpu.CompilerParams(vmem_limit_bytes=16 * MIB),
            cost_estimate=COST,
        )(my_bit(*self.bit).reshape(1), self.keep.reshape(view), got.reshape(view))
        self.keep, self.send = (a.reshape((half,) + self.block) for a in (keep, send))

    def finish(self):
        while True:
            done = self.take()
            if done is not None:
                return done
            self.move()


def fence(*values):
    return lax.optimization_barrier(values)


def by_part(weight, parts):
    rows = weight.shape[0]
    return weight.reshape(rows, PAIRS, parts, PAIR).swapaxes(1, 2).reshape(rows, parts * D)


def rows_of(array):
    return array.reshape(-1, array.shape[-1])


def exchange(array):
    return lax.all_to_all(array, "fsdp", split_axis=0, concat_axis=0, tiled=True)


def shards(
    tokens,
    frames,
    lengths,
    cotangent,
    self_in,
    self_out,
    cross_q,
    cross_kv,
    cross_out,
    fc_in,
    fc_out,
    norm_gain,
    norm_bias,
):
    fsdp_count = lax.axis_size("fsdp")
    n_all = lax.axis_size("grp") * fsdp_count
    group_seqs, size = tokens.shape[:2]
    seq_ids = jnp.arange(group_seqs, dtype=jnp.int32)
    rank_order = jnp.argsort(-(lengths * group_seqs + (group_seqs - 1 - seq_ids)))
    sender = jnp.concatenate([rank_order[:fsdp_count], rank_order[fsdp_count:][::-1]])
    device = lax.axis_index("fsdp")
    len0, len1 = (
        lax.dynamic_slice_in_dim(lengths[sender], s * fsdp_count + device, 1) for s in range(2)
    )
    rows = self_in.shape[0]
    me = (lax.axis_index("grp") * fsdp_count + device).reshape(1)

    def pick(name, *parts):
        total = sum(array.shape[1] for array, _ in parts)

        def plan(seq_ref, ins, outs):
            copies, at = [], 0
            for src, (array, slot) in zip(ins, parts):
                span = slice(at, at + array.shape[1])
                at += array.shape[1]
                for j in range(fsdp_count):
                    seq = seq_ref[slot * fsdp_count + j]
                    copies.append((0, src.at[seq], outs[0].at[j, span]))
            return copies

        shape = in_hbm(fsdp_count, total, D)
        return run_copies(name, plan, sender, [array for array, _ in parts], [shape], "out")[0]

    def put_back(name, *parts):
        ins = []
        for first, _, second, _ in parts:
            ins += [a for a in (first, second) if not any(a is b for b in ins)]
        where = [[next(i for i, a in enumerate(ins) if a is p[k]) for k in (0, 2)] for p in parts]

        def plan(seq_ref, in_refs, outs):
            return [
                (o, in_refs[where[o][slot]].at[j, part[2 * slot + 1]], outs[o].at[seq_ref[slot * fsdp_count + j]])
                for o, part in enumerate(parts)
                for slot in range(2)
                for j in range(fsdp_count)
            ]

        shapes = [in_hbm(group_seqs, p[1].stop - p[1].start, D) for p in parts]
        return run_copies(name, plan, sender, ins, shapes)

    norms = jnp.pad(jnp.concatenate([norm_gain, norm_bias], axis=1), ((0, 0), (0, 120)))
    shard_one, shard_two = pack_shards(me, self_in, self_out, cross_q, norms, cross_kv, cross_out)
    w_two = gather_rows(shard_two)
    one = Gather(
        "one", shard_one, me, [in_hbm(n_all, rows, ONE_COLS)],
        lambda src, outs, b: [(0, src, outs[0].at[b])],
    )

    pick_t = pick("pick_tokens", (tokens, 0))
    far = sum(1 for axis, _ in device_bits() if axis == "fsdp")
    one.step()
    (one.value, pick_t, fc_in, fc_out) = fence(one.value, pick_t, fc_in, fc_out)
    fc_up = fc_in.reshape(rows, n_all, FF_PARTS, rows).swapaxes(1, 2).reshape(rows, FF)
    fc_down = fc_out.reshape(FF_PARTS, rows, D).swapaxes(0, 1).reshape(rows, FF)
    w_fc = gather_rows(jnp.concatenate([fc_up, fc_down], axis=1))
    for _ in range(far - 2):
        one.step()
        (one.value, pick_t) = fence(one.value, pick_t)
    in_t = exchange(pick_t)
    pick_a = pick("pick_frames", (frames, 0))
    one.step()
    (one.value, in_t, pick_a) = fence(one.value, in_t, pick_a)
    in_a = exchange(pick_a)
    while len(one.left) > 1:
        one.send()
        pick_b = pick("pick_second", (tokens, 1), (cotangent, 0))
        pick_c = pick("pick_third", (frames, 1), (cotangent, 1))
        (one.value, one.got, pick_b, pick_c) = fence(one.value, one.got, pick_b, pick_c)
        one.take()
    (w_one,) = one.step()
    (w_one, in_t) = fence(w_one, in_t)
    w_one = rows_of(w_one)
    norm_rows = w_one[:, ONE_NORM : ONE_NORM + 8].T.astype(f32)

    fwd0 = run_self_forward(len0, in_t, "all", w_one, norm_rows)
    (in_a, fwd0, pick_b) = fence(in_a, fwd0, pick_b)
    in_b = exchange(pick_b)
    crs0 = run_cross_forward(len0, in_a, w_two, fwd0[6])
    (in_b, fwd0, crs0, pick_c) = fence(in_b, fwd0, crs0, pick_c)

    in_c = exchange(pick_c)
    fwd1 = run_self_forward(len1, in_b, "first", w_one, norm_rows)
    mid0 = run_middle(len0, crs0[0], fwd0[4], in_b, "second", w_two, w_fc, norm_rows)
    cb0 = run_cross_backward(len0, fwd0[6], crs0[2], crs0[0], mid0[7], crs0[1], w_two, mid0[0])
    mid0 = mid0[1:]
    (in_c, crs0, cb0, fwd1, mid0) = fence(in_c, crs0, cb0, fwd1, mid0)

    lens = (len0, len1)

    back_a = exchange(cb0[2])
    crs1 = run_cross_forward(len1, in_c, w_two, fwd1[6])
    mid1 = run_middle(len1, crs1[0], fwd1[4], in_c, "tokens", w_two, w_fc, norm_rows)
    leaving, mid1 = mid1[0], mid1[1:]
    fc_sides = [(mid[0], mid[2], mid[1], mid[3]) for mid in (mid0, mid1)]
    g_fc = run_fc_grad(lens, *fc_sides)
    (crs1, mid1, g_fc, leaving) = fence(crs1, mid1, g_fc, leaving)
    g_fc = lax.psum_scatter(g_fc, ("grp", "fsdp"), scatter_dimension=0, tiled=True)
    cb1 = run_cross_backward(len1, fwd1[6], crs1[2], crs1[0], mid1[6], crs1[1], w_two, leaving)
    (back_a, cb0, cb1, mid0, mid1) = fence(back_a, cb0, cb1, mid0, mid1)

    back_b = exchange(cb1[2])
    sb0 = run_self_backward(
        len0, cb0[0], mid0[5], fwd0[4], fwd0[0], fwd0[2], fwd0[3], in_t, "all", w_one, norm_rows, None, 0
    )
    sb1 = run_self_backward(
        len1, cb1[0], mid1[5], fwd1[4], fwd1[0], fwd1[2], fwd1[3], in_b, "first", w_one, norm_rows, sb0[2], 1
    )
    halves = run_grad("grad_self_in", lens, ((fwd0[1], sb0[1]), (fwd1[1], sb1[1])), 5 * D, 0)
    halves = run_grad("grad_self_out", lens, ((fwd0[2], sb0[0]), (fwd1[2], sb1[0])), 5 * D, 3, halves)
    halves = run_grad("grad_cross_q", lens, ((fwd0[5], cb0[0]), (fwd1[5], cb1[0])), 5 * D, 4, halves)
    g_one = Scatter("one", *halves)
    gtok, sb0, sb1 = sb1[2], (sb0[0], sb0[1], sb0[3]), (sb1[0], sb1[1], sb1[3])
    (sb0, sb1, g_one.keep, g_one.send, cb0, cb1, mid0, mid1) = fence(
        sb0, sb1, g_one.keep, g_one.send, cb0, cb1, mid0, mid1
    )
    g_one.step()
    halves = run_grad("grad_cross_kv", lens, ((in_a, cb0[1]), (in_c, cb1[1])), 3 * D + PAIR, 0, full=True)
    (g_one.keep, g_one.send, halves, cb0, cb1) = fence(g_one.keep, g_one.send, halves, cb0, cb1)
    g_one.move()
    halves = run_grad(
        "grad_cross_out", lens, ((crs0[0], mid0[4]), (crs1[0], mid1[4])), 3 * D + PAIR, 2, halves
    )
    ng_self = sb0[2] + sb1[2]
    ng_mid = mid0[7] + mid1[7]
    norm_sum = jnp.concatenate([ng_self[:2], ng_mid[:2], ng_self[2:4], ng_mid[2:4]], axis=0)
    g_two = Scatter("two", *put_norm_grad(norm_sum, halves))
    g_two.move()
    (back_b, g_two.got, gtok) = fence(back_b, g_two.got, gtok)

    back_c = exchange(gtok)
    grad_frames, output = put_back(
        "put_frames",
        (back_a, slice(0, 3 * size), back_b, slice(0, 3 * size)),
        (back_a, slice(3 * size, 4 * size), back_b, slice(3 * size, 4 * size)),
    )
    g_one = g_one.finish()
    g_two = g_two.finish()
    g_norm = g_two[:, 3 * D : 3 * D + 8]
    (grad_tokens,) = put_back("put_tokens", (back_c, slice(0, size), back_c, slice(size, 2 * size)))
    return (
        output,
        grad_tokens,
        grad_frames,
        by_part(g_one[:, :ONE_OUT], 3),
        g_one[:, ONE_OUT:ONE_Q],
        g_one[:, ONE_Q:],
        by_part(g_two[:, :TWO_OUT], 2),
        g_two[:, TWO_OUT : 3 * D],
        g_fc[:, :FF].astype(f32).reshape(rows, FF_PARTS, n_all, rows).swapaxes(1, 2).reshape(rows, FF),
        g_fc[:, FF:].astype(f32).reshape(rows, FF_PARTS, D).swapaxes(0, 1).reshape(FF_PARTS * rows, D),
        g_norm[:, :4],
        g_norm[:, 4:],
    )


def solution(mesh):
    rows = P(("grp", "fsdp"), None)
    seqs = P("grp", "fsdp", None)
    return jax.shard_map(
        shards,
        mesh=mesh,
        in_specs=(seqs, seqs, P("grp"), seqs) + (rows,) * 9,
        out_specs=(seqs,) * 3 + (rows,) * 9,
        check_vma=False,
    )
```

```python
import functools

import jax
import jax.numpy as jnp
import numpy as np
from jax import lax
from jax.experimental import pallas as pl
from jax.experimental.pallas import tpu as pltpu
from jax.sharding import PartitionSpec as P

D = 768
FF = 3072
HEAD_DIM = 64
FRAMES = 1500
FRAME_SLOTS = 1536
PAIR = 2 * HEAD_DIM
PAIRS = D // PAIR
TILE = 128
ROWS = 256
KEY_CHUNK = 256
SOME = 3
FF_PARTS = FF // D

eps_norm = 1e-05
neg_big = -1e30
head_scale = 0.125
bf16 = jnp.bfloat16
f32 = jnp.float32
MIB = 1024 * 1024
COST = pl.CostEstimate(flops=1000000, bytes_accessed=1000000, transcendentals=0)

ONE_OUT = 3 * D
ONE_Q = 4 * D
ONE_NORM = 5 * D
ONE_COLS = 5 * D + 128
TWO_OUT = 2 * D


def nt(left, right):
    return lax.dot_general(left, right, (((1,), (1,)), ((), ())), preferred_element_type=f32)


def nn(left, right):
    return lax.dot_general(left, right, (((1,), (0,)), ((), ())), preferred_element_type=f32)


def normalize(stream):
    centered = stream - jnp.mean(stream, axis=-1, keepdims=True)
    scale = lax.rsqrt(jnp.mean(centered * centered, axis=-1, keepdims=True) + eps_norm)
    return centered * scale, scale


def norm_backward(normed, scale, gain, grad):
    scaled = grad * gain
    mean_scaled = jnp.mean(scaled, axis=-1, keepdims=True)
    mean_along = jnp.mean(scaled * normed, axis=-1, keepdims=True)
    return scale * (scaled - mean_scaled - normed * mean_along)


def col_sum(values):
    return jnp.sum(values, axis=0, keepdims=True)


def split_heads(block):
    lanes = lax.broadcasted_iota(jnp.int32, block.shape, 1)
    zero = jnp.zeros_like(block)
    return jnp.concatenate(
        [jnp.where(lanes < HEAD_DIM, block, zero), jnp.where(lanes < HEAD_DIM, zero, block)], axis=0
    )


def join_heads(stacked):
    width = stacked.shape[1] // 2
    return jnp.concatenate([stacked[:HEAD_DIM, :width], stacked[HEAD_DIM:, width:]], axis=0).T


def row_dots(left, right):
    prod = (left.astype(f32) * right.astype(f32)).T
    return jnp.concatenate([col_sum(prod[:HEAD_DIM]), col_sum(prod[HEAD_DIM:])], axis=1)


def seen(shape, row_start, seq_len):
    keys = lax.broadcasted_iota(jnp.int32, shape, 0)
    rows = row_start + lax.rem(lax.broadcasted_iota(jnp.int32, shape, 1), TILE)
    return (keys <= rows) & (keys < seq_len)


def each_tile(count, size, body):
    def step(i, carry):
        body(pl.ds(pl.multiple_of(i * size, size), size), i)
        return carry

    lax.fori_loop(0, count, step, 0)


def each_wide_tile(seq_len, body):
    count = pl.cdiv(seq_len, TILE)
    each_tile(count // 4, 4 * TILE, lambda rows, i: body(rows, 4 * TILE))
    for some in (2, 1):

        @pl.when(count // some % 2 == 1)
        def _():
            start = count // (2 * some) * (2 * some) * TILE
            body(pl.ds(pl.multiple_of(start, TILE), some * TILE), some * TILE)


def lane_block(index):
    return pl.ds(pl.multiple_of(index * PAIR, PAIR), PAIR)


def token_rows(ref, tile):
    count = ROWS // ref.shape[1]
    return ref[pl.ds(tile * count, count)].reshape(ROWS, D).astype(f32)


def clear(*refs):
    for ref in refs:
        ref[...] = jnp.zeros_like(ref)


scale_of_heads = functools.partial(jnp.asarray, head_scale, bf16)


def self_part_forward(
    len_ref, tok_ref, one_ref, norm_ref,
    qkv_ref, normed_one_ref, mix_ref, lse_ref, after_ref, normed_two_ref, q_two_ref,
    vt_ref,
):
    seq_len = len_ref[0]
    row_tiles = pl.cdiv(seq_len, ROWS)
    clear(normed_one_ref, mix_ref, lse_ref, normed_two_ref)

    def project(rows, i):
        normed, _ = normalize(token_rows(tok_ref, i))
        normed = (normed * norm_ref[0:1, :] + norm_ref[4:5, :]).astype(bf16)
        normed_one_ref[rows, :] = normed
        qkv_ref[rows, :] = nn(normed, one_ref[:, :ONE_OUT]).astype(bf16)

    each_tile(row_tiles, ROWS, project)

    def per_pair(pair, vt_ref, rows, tile):
        q_lanes, k_lanes, v_lanes = (lane_block(3 * pair + i) for i in range(3))
        size = (tile + 1) * TILE
        vt_ref[:, rows] = qkv_ref[rows, v_lanes].T
        queries = split_heads(qkv_ref[rows, q_lanes] * scale_of_heads())
        scores = nt(qkv_ref[:size, k_lanes], queries)
        scores = jnp.where(seen(scores.shape, tile * TILE, seq_len), scores, neg_big)
        peak = jnp.max(scores, axis=0, keepdims=True)
        probs = jnp.exp(scores - peak)
        total = col_sum(probs)
        mixed = nn(vt_ref[:, :size], probs.astype(bf16))
        mix_ref[rows, lane_block(pair)] = join_heads(mixed / total).astype(bf16)
        lse_ref[pair, tile : tile + 1, :] = peak + jnp.log(total)

    def some_pairs(step, carry):
        for tile in range(qkv_ref.shape[0] // TILE):

            @pl.when(tile * TILE < seq_len)
            def _():
                for i in range(SOME):
                    per_pair(step * SOME + i, vt_ref.at[i], slice(tile * TILE, (tile + 1) * TILE), tile)

        return carry

    lax.fori_loop(0, PAIRS // SOME, some_pairs, 0)

    def finish(rows, i):
        after = token_rows(tok_ref, i) + nn(mix_ref[rows, :], one_ref[:, ONE_OUT:ONE_Q])
        after_ref[rows, :] = after
        normed, _ = normalize(after)
        normed = (normed * norm_ref[1:2, :] + norm_ref[5:6, :]).astype(bf16)
        normed_two_ref[rows, :] = normed
        q_two_ref[rows, :] = nn(normed, one_ref[:, ONE_Q:ONE_NORM]).astype(bf16)

    each_tile(row_tiles, ROWS, finish)


PARTS = {"frames": 4, "tokens": 4, "first": 2, "second": 2, "all": 1}


def part_at(part):
    return {"frames": 0, "tokens": 3, "first": 0, "second": 1, "all": 0}[part]


def whole():
    return pl.BlockSpec(memory_space=pltpu.VMEM)


def in_smem():
    return pl.BlockSpec(memory_space=pltpu.SMEM)


def shape_of(*dims, dtype=bf16):
    return jax.ShapeDtypeStruct(dims, dtype)


def in_hbm(*dims, dtype=bf16):
    return pltpu.HBM(dims, dtype)


def run_self_forward(seq_len, arrived, part, one, norm_rows):
    blocks, size = arrived.shape[0], arrived.shape[1] // PARTS[part]
    at = part_at(part)
    rows = blocks * size
    fixed = lambda *dims: pl.BlockSpec(dims, lambda i: (0,) * len(dims), pipeline_mode=pl.Buffered(1))
    shapes = [
        in_hbm(rows, 3 * D),
        in_hbm(rows, D),
        in_hbm(rows, D),
        in_hbm(PAIRS, rows // TILE, 2 * TILE, dtype=f32),
        in_hbm(rows, D, dtype=f32),
        in_hbm(rows, D),
        in_hbm(rows, D),
    ]
    return pl.pallas_call(
        self_part_forward,
        name="self_part_forward",
        grid=(1,),
        in_specs=[
            in_smem(),
            pl.BlockSpec((blocks, size, D), lambda i: (0, at, 0), pipeline_mode=pl.Buffered(1)),
            fixed(*one.shape),
            fixed(8, D),
        ],
        out_specs=[fixed(*s.shape) for s in shapes],
        out_shape=shapes,
        scratch_shapes=[pltpu.VMEM((SOME, PAIR, rows), bf16)],
        compiler_params=pltpu.CompilerParams(vmem_limit_bytes=36 * MIB),
        cost_estimate=COST,
    )(seq_len, arrived, one, norm_rows)


def cross_forward_kernel(len_ref, frm_ref, w_ref, q_ref, out_ref, lse_ref, kv_ref, vt_ref, s_ref):
    slots = kv_ref.shape[0]
    clear(out_ref, lse_ref)
    kv_ref[...] = nn(frm_ref[...].reshape(slots, D), w_ref[...]).astype(bf16)
    vt_ref[...] = kv_ref[:, PAIR:].T
    spans = [(k, min(KEY_CHUNK, slots - k)) for k in range(0, slots, KEY_CHUNK)]

    def per_tile(rows, width):
        queries = split_heads(q_ref[rows, :] * scale_of_heads())
        peak = jnp.full((1, 2 * width), neg_big, f32)
        for start, size in spans:
            scores = nt(kv_ref[start : start + size, :PAIR], queries)
            if start + size > FRAMES:
                keys = start + lax.broadcasted_iota(jnp.int32, scores.shape, 0)
                scores = jnp.where(keys < FRAMES, scores, neg_big)
            s_ref[start : start + size, : 2 * width] = scores
            peak = jnp.maximum(peak, jnp.max(scores, axis=0, keepdims=True))
        total = jnp.zeros((1, 2 * width), f32)
        mixed = jnp.zeros((PAIR, 2 * width), f32)
        for start, size in spans:
            probs = jnp.exp(s_ref[start : start + size, : 2 * width] - peak)
            total = total + col_sum(probs)
            mixed = mixed + nn(vt_ref[:, start : start + size], probs.astype(bf16))
        out_ref[rows, :] = join_heads(mixed / total).astype(bf16)
        log_sum = peak + jnp.log(total)
        lse_ref[0, 0:1, rows] = log_sum[:, :width]
        lse_ref[0, 1:2, rows] = log_sum[:, width:]

    each_wide_tile(len_ref[0], per_tile)


def frame_rows(arrived):
    return FRAME_SLOTS // arrived.shape[0]


def run_cross_forward(seq_len, arrived, two, q_two):
    blocks, size = arrived.shape[0], frame_rows(arrived)
    rows, slots = q_two.shape[0], blocks * size
    return pl.pallas_call(
        cross_forward_kernel,
        name="cross_forward",
        grid=(PAIRS,),
        in_specs=[
            in_smem(),
            pl.BlockSpec((blocks, size, D), lambda h: (0, 0, 0), pipeline_mode=pl.Buffered(1)),
            pl.BlockSpec((D, 2 * PAIR), lambda h: (0, h)),
            pl.BlockSpec((rows, PAIR), lambda h: (0, h)),
        ],
        out_specs=[
            pl.BlockSpec((rows, PAIR), lambda h: (0, h)),
            pl.BlockSpec((1, 2, rows), lambda h: (h, 0, 0)),
            pl.BlockSpec((slots, 2 * PAIR), lambda h: (0, h)),
        ],
        out_shape=[
            in_hbm(rows, D),
            in_hbm(PAIRS, 2, rows, dtype=f32),
            in_hbm(slots, 2 * D),
        ],
        scratch_shapes=[pltpu.VMEM((PAIR, slots), bf16), pltpu.VMEM((slots, 8 * TILE), f32)],
        compiler_params=pltpu.CompilerParams(vmem_limit_bytes=24 * MIB),
        cost_estimate=COST,
    )(seq_len, arrived, two, q_two)


def cross_backward_kernel(
    len_ref, q_ref, kv_ref, mix_ref, grad_ref, lse_ref, w_ref, _,
    dq_ref, dkv_ref, dfrm_ref,
    kt_ref, dk_ref, dv_ref, acc_ref,
):
    slots = kv_ref.shape[0]
    pair = pl.program_id(0)
    kt_ref[...] = kv_ref[:, :PAIR].T
    clear(dq_ref, dk_ref, dv_ref)
    spans = [(k, min(KEY_CHUNK, slots - k)) for k in range(0, slots, KEY_CHUNK)]

    def per_tile(rows, width):
        queries = split_heads(q_ref[rows, :] * scale_of_heads())
        grads = split_heads(grad_ref[rows, :])
        inner = row_dots(mix_ref[rows, :], grad_ref[rows, :])
        lse = jnp.concatenate([lse_ref[0, 0:1, rows], lse_ref[0, 1:2, rows]], axis=1)
        dq = jnp.zeros((PAIR, 2 * width), f32)
        for start, size in spans:
            span = slice(start, start + size)
            probs = jnp.exp(nt(kv_ref[span, :PAIR], queries) - lse)
            if start + size > FRAMES:
                keys = start + lax.broadcasted_iota(jnp.int32, probs.shape, 0)
                probs = jnp.where(keys < FRAMES, probs, 0.0)
            dscores = (probs * (nt(kv_ref[span, PAIR:], grads) - inner)).astype(bf16)
            dv_ref[span, :] += nn(probs.astype(bf16), grads)
            dk_ref[span, :] += nn(dscores, queries)
            dq = dq + nn(kt_ref[:, span], dscores)
        dq_ref[rows, :] = join_heads(dq).astype(bf16) * scale_of_heads()

    each_wide_tile(len_ref[0], per_tile)
    dkv_ref[:, :PAIR] = dk_ref[...].astype(bf16)
    dkv_ref[:, PAIR:] = dv_ref[...].astype(bf16)
    part = nt(dkv_ref[...], w_ref[...])

    @pl.when(pair == 0)
    def _():
        acc_ref[...] = part

    @pl.when((pair > 0) & (pair < PAIRS - 1))
    def _():
        acc_ref[...] += part

    @pl.when(pair == PAIRS - 1)
    def _():
        dfrm_ref[...] = (acc_ref[...] + part).astype(bf16).reshape(dfrm_ref.shape)


def run_cross_backward(seq_len, q_two, kv, mix, grad_mix, lse, two, leaving):
    rows, slots, blocks = q_two.shape[0], kv.shape[0], leaving.shape[0]
    row_spec = pl.BlockSpec((rows, PAIR), lambda h: (0, h))
    kv_spec = pl.BlockSpec((slots, 2 * PAIR), lambda h: (0, h))
    return pl.pallas_call(
        cross_backward_kernel,
        name="cross_backward",
        grid=(PAIRS,),
        in_specs=[
            in_smem(),
            row_spec,
            kv_spec,
            row_spec,
            row_spec,
            pl.BlockSpec((1, 2, rows), lambda h: (h, 0, 0)),
            pl.BlockSpec((D, 2 * PAIR), lambda h: (0, h)),
            pl.BlockSpec(memory_space=pl.ANY),
        ],
        out_specs=[
            row_spec,
            kv_spec,
            pl.BlockSpec((blocks, slots // blocks, D), lambda h: (0, 0, 0), pipeline_mode=pl.Buffered(1)),
        ],
        out_shape=[in_hbm(rows, D), in_hbm(slots, 2 * D), in_hbm(*leaving.shape)],
        input_output_aliases={7: 2},
        scratch_shapes=[
            pltpu.VMEM((PAIR, slots), bf16),
            pltpu.VMEM((slots, PAIR), f32),
            pltpu.VMEM((slots, PAIR), f32),
            pltpu.VMEM((slots, D), f32),
        ],
        compiler_params=pltpu.CompilerParams(vmem_limit_bytes=36 * MIB),
        cost_estimate=COST,
    )(seq_len, q_two, kv, mix, grad_mix, lse, two, leaving)


def middle_kernel(
    len_ref, mix_ref, after_ref, cot_ref, two_ref, fc_ref, norm_ref,
    out_ref, normed_ref, hidden_ref, grad_pre_ref, branch_three_ref, branch_two_ref,
    grad_cross_ref, grad_mix_ref, norm_grad_ref,
    slope_ref,
):
    seq_len = len_ref[0]
    step = pl.program_id(0)
    parts = [(slice(k, k + D), slice(FF + k, FF + k + D)) for k in range(0, FF, D)]

    @pl.when(step == 0)
    def _():
        clear(norm_grad_ref)

    @pl.when(step * ROWS >= seq_len)
    def _():
        clear(out_ref)

    @pl.when(step * ROWS < seq_len)
    def _():
        w_out = two_ref[:, TWO_OUT:]
        after_cross = after_ref[...] + nn(mix_ref[...], w_out)
        n_three, scale_three = normalize(after_cross)
        normed = (n_three * norm_ref[2:3, :] + norm_ref[6:7, :]).astype(bf16)
        normed_ref[...] = normed
        mlp = jnp.zeros((ROWS, D), f32)
        for span, rows_out in parts:
            pre = nn(normed, fc_ref[:, span])
            below = 0.5 * (1.0 + lax.erf(pre * np.float32(np.sqrt(0.5))))
            density = jnp.exp(-0.5 * pre * pre) * np.float32(1.0 / np.sqrt(2.0 * np.pi))
            slope_ref[:, span] = below + pre * density
            hidden = (pre * below).astype(bf16)
            hidden_ref[:, span] = hidden
            mlp = mlp + nn(hidden, fc_ref[:, rows_out])
        n_four, scale_four = normalize(after_cross + mlp)
        row_ids = step * ROWS + lax.broadcasted_iota(jnp.int32, (ROWS, 1), 0)
        valid = (row_ids < seq_len).astype(f32)
        output = ((n_four * norm_ref[3:4, :] + norm_ref[7:8, :]) * valid).astype(bf16)
        out_ref[...] = output.reshape(out_ref.shape)

        grad = cot_ref[...].reshape(ROWS, D).astype(f32) * valid
        norm_grad_ref[1:2, :] += col_sum(grad * n_four)
        norm_grad_ref[3:4, :] += col_sum(grad)
        grad_mlp = norm_backward(n_four, scale_four, norm_ref[3:4, :], grad)
        branch_three = grad_mlp.astype(bf16)
        branch_three_ref[...] = branch_three
        back = jnp.zeros((ROWS, D), f32)
        for span, rows_out in parts:
            grad_pre = (nt(branch_three, fc_ref[:, rows_out]) * slope_ref[:, span]).astype(bf16)
            grad_pre_ref[:, span] = grad_pre
            back = back + nt(grad_pre, fc_ref[:, span])
        norm_grad_ref[0:1, :] += col_sum(back * n_three)
        norm_grad_ref[2:3, :] += col_sum(back)
        grad_cross = grad_mlp + norm_backward(n_three, scale_three, norm_ref[2:3, :], back)
        grad_cross_ref[...] = grad_cross
        branch_two = grad_cross.astype(bf16)
        branch_two_ref[...] = branch_two
        grad_mix_ref[...] = nt(branch_two, w_out).astype(bf16)


def run_middle(seq_len, mix, after, arrived, part, two, fc, norm_rows):
    rows, blocks = mix.shape[0], arrived.shape[0]
    size = rows // blocks
    at = part_at(part)
    count = ROWS // size
    last = lambda i, n: jnp.minimum(i, (n[0] - 1) // ROWS)
    row_spec = pl.BlockSpec((ROWS, D), lambda i, n: (last(i, n), 0))
    wide_spec = pl.BlockSpec((ROWS, FF), lambda i, n: (last(i, n), 0))

    def fixed(*dims):
        return pl.BlockSpec(dims, lambda i, n: (0, 0), pipeline_mode=pl.Buffered(1))

    return pl.pallas_call(
        middle_kernel,
        name="mlp_and_back",
        grid_spec=pltpu.PrefetchScalarGridSpec(
            num_scalar_prefetch=1,
            grid=(rows // ROWS,),
            in_specs=[
                row_spec, row_spec, pl.BlockSpec((count, size, D), lambda i, n: (last(i, n), at, 0)),
                fixed(D, 3 * D), fixed(D, 2 * FF), fixed(8, D),
            ],
            out_specs=[pl.BlockSpec((count, size, D), lambda i, n: (i, 3, 0)), row_spec, wide_spec, wide_spec, row_spec, row_spec, row_spec, row_spec,
                   pl.BlockSpec((8, D), lambda i, n: (0, 0))],
            scratch_shapes=[pltpu.VMEM((ROWS, FF), f32)],
        ),
        out_shape=[
            in_hbm(blocks, 4 * size, D), in_hbm(rows, D), in_hbm(rows, FF), in_hbm(rows, FF),
            in_hbm(rows, D), in_hbm(rows, D), in_hbm(rows, D, dtype=f32), in_hbm(rows, D),
            in_hbm(8, D, dtype=f32),
        ],
        compiler_params=pltpu.CompilerParams(vmem_limit_bytes=48 * MIB),
        cost_estimate=COST,
    )(seq_len, mix, after, arrived, two, fc, norm_rows)


def self_part_backward(
    len_ref, dq_ref, grad_cross_ref, after_ref, qkv_ref, mix_ref, lse_ref, tok_ref, one_ref, norm_ref, _,
    branch_ref, dqkv_ref, grad_tok_ref, norm_grad_ref,
    attn_ref, grad_mix_ref, kt_ref, dk_ref, dv_ref,
):
    seq_len = len_ref[0]
    row_tiles = pl.cdiv(seq_len, ROWS)
    clear(branch_ref, dqkv_ref, grad_tok_ref, norm_grad_ref)

    def enter(rows, _):
        normed, scale = normalize(after_ref[rows, :])
        grad = nt(dq_ref[rows, :], one_ref[:, ONE_Q:ONE_NORM])
        norm_grad_ref[1:2, :] += col_sum(grad * normed)
        norm_grad_ref[3:4, :] += col_sum(grad)
        attn = grad_cross_ref[rows, :] + norm_backward(normed, scale, norm_ref[1:2, :], grad)
        attn_ref[rows, :] = attn
        branch = attn.astype(bf16)
        branch_ref[rows, :] = branch
        grad_mix_ref[rows, :] = nt(branch, one_ref[:, ONE_OUT:ONE_Q]).astype(bf16)

    each_tile(row_tiles, ROWS, enter)

    def per_pair(pair, kt_ref, dk_ref, dv_ref, rows, tile):
        q_lanes, k_lanes, v_lanes = (lane_block(3 * pair + i) for i in range(3))
        size = (tile + 1) * TILE
        kt_ref[:, rows] = qkv_ref[rows, k_lanes].T
        queries = split_heads(qkv_ref[rows, q_lanes] * scale_of_heads())
        grad_mix = grad_mix_ref[rows, lane_block(pair)]
        grads = split_heads(grad_mix)
        inner = row_dots(mix_ref[rows, lane_block(pair)], grad_mix)
        scores = nt(qkv_ref[:size, k_lanes], queries)
        scores = jnp.where(seen(scores.shape, tile * TILE, seq_len), scores, neg_big)
        probs = jnp.exp(scores - lse_ref[pair, tile : tile + 1, :])
        dscores = (probs * (nt(qkv_ref[:size, v_lanes], grads) - inner)).astype(bf16)
        dv_ref[:size, :] += nn(probs.astype(bf16), grads)
        dk_ref[:size, :] += nn(dscores, queries)
        dq = nn(kt_ref[:, :size], dscores)
        dqkv_ref[rows, q_lanes] = join_heads(dq).astype(bf16) * scale_of_heads()

    def some_pairs(step, carry):
        clear(dk_ref, dv_ref)
        for tile in range(qkv_ref.shape[0] // TILE):

            @pl.when(tile * TILE < seq_len)
            def _():
                for i in range(SOME):
                    rows = slice(tile * TILE, (tile + 1) * TILE)
                    per_pair(step * SOME + i, kt_ref.at[i], dk_ref.at[i], dv_ref.at[i], rows, tile)

        for i in range(SOME):
            pair = step * SOME + i
            dqkv_ref[:, lane_block(3 * pair + 1)] = dk_ref[i].astype(bf16)
            dqkv_ref[:, lane_block(3 * pair + 2)] = dv_ref[i].astype(bf16)
        return carry

    lax.fori_loop(0, PAIRS // SOME, some_pairs, 0)

    def leave(rows, i):
        normed, scale = normalize(token_rows(tok_ref, i))
        grad = nt(dqkv_ref[rows, :], one_ref[:, :ONE_OUT])
        norm_grad_ref[0:1, :] += col_sum(grad * normed)
        norm_grad_ref[2:3, :] += col_sum(grad)
        total = attn_ref[rows, :] + norm_backward(normed, scale, norm_ref[0:1, :], grad)
        count = ROWS // grad_tok_ref.shape[1]
        grad_tok_ref[pl.ds(i * count, count)] = total.astype(bf16).reshape(count, -1, D)

    each_tile(row_tiles, ROWS, leave)


def run_self_backward(seq_len, dq, grad_cross, after, qkv, mix, lse, arrived, part, one, norm_rows, leaving, slot):
    blocks, size = arrived.shape[0], arrived.shape[1] // PARTS[part]
    at = part_at(part)
    rows = blocks * size
    fixed = lambda *dims: pl.BlockSpec(dims, lambda i: (0,) * len(dims), pipeline_mode=pl.Buffered(1))
    spec = lambda block: pl.BlockSpec(
        (blocks, size, D), lambda i: (0, block, 0), pipeline_mode=pl.Buffered(1)
    )
    before = [] if leaving is None else [leaving]
    body = self_part_backward
    if leaving is None:
        body = lambda *refs: self_part_backward(*refs[:10], None, *refs[10:])
    return pl.pallas_call(
        body,
        name="self_part_backward",
        grid=(1,),
        in_specs=[in_smem()]
        + [fixed(*a.shape) for a in (dq, grad_cross, after, qkv, mix, lse)]
        + [spec(at), fixed(*one.shape), fixed(8, D)]
        + [anywhere()] * len(before),
        out_specs=[fixed(rows, D), fixed(rows, 3 * D), spec(slot), fixed(8, D)],
        out_shape=[
            in_hbm(rows, D),
            in_hbm(rows, 3 * D),
            in_hbm(blocks, 2 * size, D),
            in_hbm(8, D, dtype=f32),
        ],
        input_output_aliases={10: 2} if before else {},
        scratch_shapes=[
            pltpu.VMEM((rows, D), f32),
            pltpu.VMEM((rows, D), bf16),
            pltpu.VMEM((SOME, PAIR, rows), bf16),
            pltpu.VMEM((SOME, rows, PAIR), f32),
            pltpu.VMEM((SOME, rows, PAIR), f32),
        ],
        compiler_params=pltpu.CompilerParams(vmem_limit_bytes=40 * MIB),
        cost_estimate=COST,
    )(seq_len, dq, grad_cross, after, qkv, mix, lse, arrived, one, norm_rows, *before)


def anywhere():
    return pl.BlockSpec(memory_space=pl.ANY)


def copy_kernel(plan, n_in, n_out, scalar_ref, *refs):
    ins, outs, sem = refs[:n_in], refs[n_in : n_in + n_out], refs[-1]
    for which, src, dst in plan(scalar_ref, ins, outs):
        pltpu.make_async_copy(src, dst, sem.at[which]).start()
    for which, out in enumerate(outs):
        pltpu.make_async_copy(out, out, sem.at[which]).wait()


def run_copies(name, plan, scalars, ins, out_shapes, stage="in"):
    vmem = pl.BlockSpec(memory_space=pltpu.VMEM)
    return pl.pallas_call(
        functools.partial(copy_kernel, plan, len(ins), len(out_shapes)),
        name=name,
        in_specs=[in_smem()] + [vmem if stage == "in" else pl.BlockSpec(memory_space=pltpu.HBM)] * len(ins),
        out_specs=[vmem if stage == "out" else anywhere()] * len(out_shapes),
        out_shape=out_shapes,
        scratch_shapes=[pltpu.SemaphoreType.DMA((len(out_shapes),))],
        compiler_params=pltpu.CompilerParams(vmem_limit_bytes=16 * MIB),
        cost_estimate=pl.CostEstimate(flops=0, bytes_accessed=1000, transcendentals=0),
    )(scalars, *ins)


def device_bits():
    return [
        (axis, b)
        for axis in ("grp", "fsdp")
        for b in reversed(range(lax.axis_size(axis).bit_length() - 1))
    ]


def swap(array, axis, b):
    return lax.ppermute(array, axis, [(i, i ^ (1 << b)) for i in range(lax.axis_size(axis))])


def bit_mask(axis, b):
    return (1 << b) if axis == "fsdp" else lax.axis_size("fsdp") << b


def my_bit(axis, b):
    return (lax.axis_index(axis) >> b) & 1


class Gather:
    def __init__(self, name, shard, me, outs, pieces):
        self.name = name
        bits = device_bits()
        self.left = [p for p in bits if p[0] == "fsdp"] + [p for p in bits if p[0] == "grp"]
        self.masks = [0]
        self.value = shard[None]
        self.me = me
        self.outs = outs
        self.pieces = pieces
        self.got = None

    def send(self):
        self.got = swap(self.value, *self.left[0])

    def take(self):
        mask = bit_mask(*self.left.pop(0))
        masks = self.masks
        self.masks = masks + [mask ^ m for m in masks]
        k = len(masks)
        if self.left:

            def plan(_, ins, outs):
                return [(0, ins[0], outs[0].at[:k]), (0, ins[1], outs[0].at[k:])]

            shape = (2 * k,) + self.value.shape[1:]
            (self.value,) = run_copies(
                self.name + "_join", plan, self.me, [self.value, self.got], [in_hbm(*shape)]
            )
            return self.value

        def plan(me_ref, ins, outs):
            me = me_ref[0]
            return [
                (which, src, dst)
                for i in range(k)
                for half, src_ref in ((0, ins[0]), (k, ins[1]))
                for which, src, dst in self.pieces(src_ref.at[i], outs, me ^ self.masks[half + i])
            ]

        self.value = run_copies(
            self.name + "_order", plan, self.me, [self.value, self.got], self.outs
        )
        return self.value

    def step(self):
        self.send()
        return self.take()


def pack_shards(me, self_in, self_out, cross_q, norms, cross_kv, cross_out):
    rows = self_in.shape[0]

    def plan(_, ins, outs):
        w_in, w_out, w_q, w_norm, w_kv, w_cross = ins
        one, two = outs
        copies = []
        for pair in range(PAIRS):
            for o, w, parts in ((0, w_in, 3), (1, w_kv, 2)):
                for part in range(parts):
                    src = w.at[:, part * D + pair * PAIR : part * D + (pair + 1) * PAIR]
                    at = (parts * pair + part) * PAIR
                    copies.append((o, src, outs[o].at[:, at : at + PAIR]))
        copies.append((0, w_out, one.at[:, ONE_OUT:ONE_Q]))
        copies.append((0, w_q, one.at[:, ONE_Q:ONE_NORM]))
        copies.append((0, w_norm, one.at[:, ONE_NORM:]))
        copies.append((1, w_cross, two.at[:, TWO_OUT:]))
        return copies

    ins = [self_in, self_out, cross_q, norms, cross_kv, cross_out]
    shapes = [in_hbm(rows, ONE_COLS), in_hbm(rows, 3 * D)]
    return run_copies("pack_shards", plan, me, ins, shapes, "out")


def gather_rows(shard):
    return lax.all_gather(shard, ("grp", "fsdp"), axis=0, tiled=True)


def grad_kernel(
    full, len0_ref, len1_ref, bit_ref, left0_ref, right0_ref, left1_ref, right1_ref, *refs
):
    keep_ref, send_ref, flip_ref, acc_ref = refs[-4:]
    half, count = keep_ref.shape[1], right0_ref.shape[0]
    sides = (
        (len0_ref[0], left0_ref, right0_ref, 0),
        (len1_ref[0], left1_ref, right1_ref, count),
    )
    tiles = [slice(k, k + ROWS) for k in range(0, count, ROWS)]

    @pl.when(pl.program_id(0) == 0)
    def _():
        for seq_len, left_ref, _, at in sides:
            for tile in tiles:

                @pl.when(jnp.logical_or(full or tile.start == 0, tile.start < seq_len))
                def _():
                    if len(left_ref.shape) == 3:
                        size = left_ref.shape[1]
                        left = left_ref[tile.start // size : (tile.stop + size - 1) // size]
                        skip = tile.start % size
                        left = left.reshape(-1, D)[skip : skip + ROWS]
                    else:
                        left = left_ref[tile, :]
                    flip_ref[:, at + tile.start : at + tile.stop] = left.T

    if full:
        acc_ref[...] = nn(flip_ref[:, :count], right0_ref[...]) + nn(
            flip_ref[:, count:], right1_ref[...]
        )
    else:
        acc_ref[...] = nn(flip_ref[:, :ROWS], right0_ref[:ROWS, :]) + nn(
            flip_ref[:, count : count + ROWS], right1_ref[:ROWS, :]
        )
        for seq_len, _, right_ref, at in sides:
            for tile in tiles[1:]:

                @pl.when(tile.start < seq_len)
                def _():
                    acc_ref[...] += nn(flip_ref[:, at + tile.start : at + tile.stop], right_ref[tile, :])

    for i in range(keep_ref.shape[0]):
        for out_ref, bit in ((keep_ref, bit_ref[0]), (send_ref, 1 - bit_ref[0])):
            at = pl.multiple_of((2 * i + bit) * half, half)
            out_ref[i] = acc_ref[pl.ds(at, half), :].astype(bf16)


def fc_grad_kernel(
    len0_ref, len1_ref, normed0_ref, pre0_ref, hid0_ref, branch0_ref, normed1_ref, pre1_ref, hid1_ref, branch1_ref,
    out_ref, flip_ref, acc_ref,
):
    step = pl.program_id(0)
    count = normed0_ref.shape[0]
    tiles = [slice(k, k + ROWS) for k in range(0, count, ROWS)]
    sides = (
        (len0_ref[0], normed0_ref, pre0_ref, hid0_ref, branch0_ref, 0),
        (len1_ref[0], normed1_ref, pre1_ref, hid1_ref, branch1_ref, count),
    )

    def flip(pick):
        for side in sides:
            for tile in tiles:

                @pl.when(jnp.logical_or(tile.start == 0, tile.start < side[0]))
                def _():
                    flip_ref[:, side[5] + tile.start : side[5] + tile.stop] = side[pick][tile, :].T

    def multiply(pick):
        acc_ref[...] = nn(flip_ref[:, :ROWS], sides[0][pick][:ROWS, :]) + nn(
            flip_ref[:, count : count + ROWS], sides[1][pick][:ROWS, :]
        )
        for side in sides:
            for tile in tiles[1:]:

                @pl.when(tile.start < side[0])
                def _():
                    at = side[5]
                    acc_ref[...] += nn(flip_ref[:, at + tile.start : at + tile.stop], side[pick][tile, :])

        out_ref[...] = acc_ref[...].astype(bf16)

    @pl.when(step == 0)
    def _():
        flip(1)

    @pl.when(step < FF_PARTS)
    def _():
        multiply(2)

    @pl.when(step >= FF_PARTS)
    def _():
        flip(3)
        multiply(4)


def norm_grad_kernel(bit_ref, norm_ref, _, __, keep_ref, send_ref, flip_ref):
    flip_ref[...] = jnp.concatenate([norm_ref[...], jnp.zeros((PAIR - 8, D), f32)], axis=0).T
    size = keep_ref.shape[1]
    for i in range(keep_ref.shape[0]):
        for out_ref, bit in ((keep_ref, bit_ref[0]), (send_ref, 1 - bit_ref[0])):
            at = pl.multiple_of((2 * i + bit) * size, size)
            out_ref[i] = flip_ref[pl.ds(at, size), :].astype(bf16)


def put_norm_grad(norm_sum, halves):
    count, size, cols = halves[0].shape
    spec = pl.BlockSpec((count, size, PAIR), lambda i: (0, 0, cols // PAIR - 1))
    return pl.pallas_call(
        norm_grad_kernel,
        name="put_norm_grad",
        grid=(1,),
        in_specs=[in_smem(), pl.BlockSpec((8, D), lambda i: (0, 0)), anywhere(), anywhere()],
        out_specs=[spec, spec],
        out_shape=[in_hbm(*h.shape) for h in halves],
        input_output_aliases={2: 0, 3: 1},
        scratch_shapes=[pltpu.VMEM((D, PAIR), f32)],
        compiler_params=pltpu.CompilerParams(vmem_limit_bytes=8 * MIB),
        cost_estimate=COST,
    )(my_bit("grp", 0).reshape(1), norm_sum, *halves)


def run_fc_grad(lens, side0, side1):
    count = side0[0].shape[0]
    whole_spec = pl.BlockSpec((count, D), lambda i: (0, 0), pipeline_mode=pl.Buffered(1))
    pre_spec = pl.BlockSpec((count, D), lambda i: (0, jnp.minimum(i, FF_PARTS - 1)))
    hid_spec = pl.BlockSpec((count, D), lambda i: (0, jnp.maximum(i - FF_PARTS, 0)))
    return pl.pallas_call(
        fc_grad_kernel,
        name="grad_fc",
        grid=(2 * FF_PARTS,),
        in_specs=[in_smem()] * 2 + [whole_spec, pre_spec, hid_spec, whole_spec] * 2,
        out_specs=pl.BlockSpec((D, D), lambda i: (0, i)),
        out_shape=in_hbm(D, 2 * FF),
        scratch_shapes=[pltpu.VMEM((D, 2 * count), bf16), pltpu.VMEM((D, D), f32)],
        compiler_params=pltpu.CompilerParams(vmem_limit_bytes=32 * MIB),
        cost_estimate=COST,
    )(*lens, *side0, *side1)


def run_grad(name, lens, pairs, cols, at, before=(), full=False):
    (left0, right0), (left1, right1) = pairs
    count, wide = right0.shape
    tall = D
    n_grp = lax.axis_size("grp")
    def left_spec(left):
        if left.ndim == 3:
            block = (left.shape[0], frame_rows(left), D)
            return pl.BlockSpec(block, lambda n: (0, 0, 0), pipeline_mode=pl.Buffered(1))
        return pl.BlockSpec((count, tall), lambda n: (0, 0), pipeline_mode=pl.Buffered(1))

    right_spec = pl.BlockSpec((count, D), lambda n: (0, n))
    out_spec = pl.BlockSpec((n_grp // 2, tall // n_grp, D), lambda n: (0, 0, n + at))
    shape = in_hbm(n_grp // 2, tall // n_grp, cols)
    bit = my_bit("grp", 0).reshape(1)
    return pl.pallas_call(
        functools.partial(grad_kernel, full),
        name=name,
        grid=(wide // D,),
        in_specs=[in_smem()] * 3
        + [left_spec(left0), right_spec, left_spec(left1), right_spec]
        + [anywhere()] * len(before),
        out_specs=[out_spec, out_spec],
        out_shape=[shape, shape],
        input_output_aliases={7: 0, 8: 1} if before else {},
        scratch_shapes=[pltpu.VMEM((tall, 2 * count), bf16), pltpu.VMEM((tall, D), f32)],
        compiler_params=pltpu.CompilerParams(vmem_limit_bytes=48 * MIB),
        cost_estimate=COST,
    )(*lens, bit, left0, right0, left1, right1, *before)


def add_split_kernel(me_ref, kept_ref, got_ref, keep_ref, send_ref):
    for out_ref, half in ((keep_ref, me_ref[0]), (send_ref, 1 - me_ref[0])):
        total = kept_ref[0, half].astype(f32) + got_ref[0, half].astype(f32)
        out_ref[0] = total.astype(out_ref.dtype)


def add_kernel(kept_ref, got_ref, out_ref):
    out_ref[...] = kept_ref[...].astype(f32) + got_ref[...].astype(f32)


class Scatter:
    def __init__(self, name, keep, send):
        self.name = name
        self.held = device_bits()
        self.order = [p for p in reversed(self.held) if p[0] == "grp"]
        self.order += [p for p in reversed(self.held) if p[0] == "fsdp"]
        self.split()
        blocks = 1 << len(self.held)
        self.keep, self.send = (a.reshape(blocks, -1, a.shape[-1]) for a in (keep, send))
        self.block = self.keep.shape[1:]

    def split(self):
        self.bit = self.order.pop(0)
        dim = self.held.index(self.bit)
        self.held.remove(self.bit)
        return 1 << dim, 1 << (len(self.held) - dim)

    def move(self):
        self.got = swap(self.send, *self.bit)

    def step(self):
        self.move()
        return self.take()

    def take(self):
        got = self.got
        if not self.order:
            spec = pl.BlockSpec((1,) + self.block, lambda i: (0, 0, 0))
            return pl.pallas_call(
                add_kernel,
                name=self.name + "_sum",
                grid=(1,),
                in_specs=[spec, spec],
                out_specs=spec,
                out_shape=shape_of(1, *self.block, dtype=f32),
                compiler_params=pltpu.CompilerParams(vmem_limit_bytes=8 * MIB),
                cost_estimate=COST,
            )(self.keep, got).reshape(self.block)
        before, after = self.split()
        half = self.keep.shape[0] // 2
        view = (before, 2, after) + self.block
        some = min(after, 4)
        in_spec = pl.BlockSpec((1, 2, some) + self.block, lambda i, j, _: (i, 0, j, 0, 0))
        out_spec = pl.BlockSpec((1, some) + self.block, lambda i, j, _: (i, j, 0, 0))
        shape = shape_of(before, after, *self.block, dtype=self.keep.dtype)
        keep, send = pl.pallas_call(
            add_split_kernel,
            name=self.name + "_add",
            grid_spec=pltpu.PrefetchScalarGridSpec(
                num_scalar_prefetch=1,
                grid=(before, after // some),
                in_specs=[in_spec, in_spec],
                out_specs=[out_spec, out_spec],
            ),
            out_shape=[shape, shape],
            compiler_params=pltpu.CompilerParams(vmem_limit_bytes=16 * MIB),
            cost_estimate=COST,
        )(my_bit(*self.bit).reshape(1), self.keep.reshape(view), got.reshape(view))
        self.keep, self.send = (a.reshape((half,) + self.block) for a in (keep, send))

    def finish(self):
        while True:
            done = self.take()
            if done is not None:
                return done
            self.move()


def fence(*values):
    return lax.optimization_barrier(values)


def by_part(weight, parts):
    rows = weight.shape[0]
    return weight.reshape(rows, PAIRS, parts, PAIR).swapaxes(1, 2).reshape(rows, parts * D)


def rows_of(array):
    return array.reshape(-1, array.shape[-1])


def exchange(array):
    return lax.all_to_all(array, "fsdp", split_axis=0, concat_axis=0, tiled=True)


def shards(
    tokens,
    frames,
    lengths,
    cotangent,
    self_in,
    self_out,
    cross_q,
    cross_kv,
    cross_out,
    fc_in,
    fc_out,
    norm_gain,
    norm_bias,
):
    fsdp_count = lax.axis_size("fsdp")
    n_all = lax.axis_size("grp") * fsdp_count
    group_seqs, size = tokens.shape[:2]
    seq_ids = jnp.arange(group_seqs, dtype=jnp.int32)
    rank_order = jnp.argsort(-(lengths * group_seqs + (group_seqs - 1 - seq_ids)))
    sender = jnp.concatenate([rank_order[:fsdp_count], rank_order[fsdp_count:][::-1]])
    device = lax.axis_index("fsdp")
    len0, len1 = (
        lax.dynamic_slice_in_dim(lengths[sender], s * fsdp_count + device, 1) for s in range(2)
    )
    rows = self_in.shape[0]
    me = (lax.axis_index("grp") * fsdp_count + device).reshape(1)

    def pick(name, *parts):
        total = sum(array.shape[1] for array, _ in parts)

        def plan(seq_ref, ins, outs):
            copies, at = [], 0
            for src, (array, slot) in zip(ins, parts):
                span = slice(at, at + array.shape[1])
                at += array.shape[1]
                for j in range(fsdp_count):
                    seq = seq_ref[slot * fsdp_count + j]
                    copies.append((0, src.at[seq], outs[0].at[j, span]))
            return copies

        shape = in_hbm(fsdp_count, total, D)
        return run_copies(name, plan, sender, [array for array, _ in parts], [shape], "out")[0]

    def put_back(name, *parts):
        ins = []
        for first, _, second, _ in parts:
            ins += [a for a in (first, second) if not any(a is b for b in ins)]
        where = [[next(i for i, a in enumerate(ins) if a is p[k]) for k in (0, 2)] for p in parts]

        def plan(seq_ref, in_refs, outs):
            return [
                (o, in_refs[where[o][slot]].at[j, part[2 * slot + 1]], outs[o].at[seq_ref[slot * fsdp_count + j]])
                for o, part in enumerate(parts)
                for slot in range(2)
                for j in range(fsdp_count)
            ]

        shapes = [in_hbm(group_seqs, p[1].stop - p[1].start, D) for p in parts]
        return run_copies(name, plan, sender, ins, shapes)

    norms = jnp.pad(jnp.concatenate([norm_gain, norm_bias], axis=1), ((0, 0), (0, 120)))
    shard_one, shard_two = pack_shards(me, self_in, self_out, cross_q, norms, cross_kv, cross_out)
    w_two = gather_rows(shard_two)
    one = Gather(
        "one", shard_one, me, [in_hbm(n_all, rows, ONE_COLS)],
        lambda src, outs, b: [(0, src, outs[0].at[b])],
    )

    pick_t = pick("pick_tokens", (tokens, 0), (tokens, 1))
    far = sum(1 for axis, _ in device_bits() if axis == "fsdp")
    one.step()
    (one.value, pick_t, fc_in, fc_out) = fence(one.value, pick_t, fc_in, fc_out)
    fc_up = fc_in.reshape(rows, n_all, FF_PARTS, rows).swapaxes(1, 2).reshape(rows, FF)
    fc_down = fc_out.reshape(FF_PARTS, rows, D).swapaxes(0, 1).reshape(rows, FF)
    w_fc = gather_rows(jnp.concatenate([fc_up, fc_down], axis=1))
    for _ in range(far - 2):
        one.step()
        (one.value, pick_t) = fence(one.value, pick_t)
    in_t = exchange(pick_t)
    pick_a = pick("pick_frames", (frames, 0))
    one.step()
    (one.value, in_t, pick_a) = fence(one.value, in_t, pick_a)
    in_a = exchange(pick_a)
    while len(one.left) > 1:
        one.send()
        pick_b = pick("pick_cotangent", (cotangent, 0))
        pick_c = pick("pick_third", (frames, 1), (cotangent, 1))
        (one.value, one.got, pick_b, pick_c) = fence(one.value, one.got, pick_b, pick_c)
        one.take()
    (w_one,) = one.step()
    (w_one, in_t) = fence(w_one, in_t)
    w_one = rows_of(w_one)
    norm_rows = w_one[:, ONE_NORM : ONE_NORM + 8].T.astype(f32)

    fwd0 = run_self_forward(len0, in_t, "first", w_one, norm_rows)
    fwd1 = run_self_forward(len1, in_t, "second", w_one, norm_rows)
    (in_a, fwd0, fwd1, pick_b) = fence(in_a, fwd0, fwd1, pick_b)
    in_b = exchange(pick_b)
    crs0 = run_cross_forward(len0, in_a, w_two, fwd0[6])
    (in_b, fwd0, crs0, pick_c) = fence(in_b, fwd0, crs0, pick_c)

    in_c = exchange(pick_c)
    mid0 = run_middle(len0, crs0[0], fwd0[4], in_b, "all", w_two, w_fc, norm_rows)
    cb0 = run_cross_backward(len0, fwd0[6], crs0[2], crs0[0], mid0[7], crs0[1], w_two, mid0[0])
    mid0 = mid0[1:]
    (in_c, crs0, cb0, fwd1, mid0) = fence(in_c, crs0, cb0, fwd1, mid0)

    lens = (len0, len1)

    back_a = exchange(cb0[2])
    crs1 = run_cross_forward(len1, in_c, w_two, fwd1[6])
    mid1 = run_middle(len1, crs1[0], fwd1[4], in_c, "tokens", w_two, w_fc, norm_rows)
    leaving, mid1 = mid1[0], mid1[1:]
    fc_sides = [(mid[0], mid[2], mid[1], mid[3]) for mid in (mid0, mid1)]
    g_fc = run_fc_grad(lens, *fc_sides)
    (crs1, mid1, g_fc, leaving) = fence(crs1, mid1, g_fc, leaving)
    g_fc = lax.psum_scatter(g_fc, ("grp", "fsdp"), scatter_dimension=0, tiled=True)
    cb1 = run_cross_backward(len1, fwd1[6], crs1[2], crs1[0], mid1[6], crs1[1], w_two, leaving)
    (back_a, cb0, cb1, mid0, mid1) = fence(back_a, cb0, cb1, mid0, mid1)

    back_b = exchange(cb1[2])
    sb0 = run_self_backward(
        len0, cb0[0], mid0[5], fwd0[4], fwd0[0], fwd0[2], fwd0[3], in_t, "first", w_one, norm_rows, None, 0
    )
    sb1 = run_self_backward(
        len1, cb1[0], mid1[5], fwd1[4], fwd1[0], fwd1[2], fwd1[3], in_t, "second", w_one, norm_rows, sb0[2], 1
    )
    halves = run_grad("grad_self_in", lens, ((fwd0[1], sb0[1]), (fwd1[1], sb1[1])), 5 * D, 0)
    halves = run_grad("grad_self_out", lens, ((fwd0[2], sb0[0]), (fwd1[2], sb1[0])), 5 * D, 3, halves)
    halves = run_grad("grad_cross_q", lens, ((fwd0[5], cb0[0]), (fwd1[5], cb1[0])), 5 * D, 4, halves)
    g_one = Scatter("one", *halves)
    gtok, sb0, sb1 = sb1[2], (sb0[0], sb0[1], sb0[3]), (sb1[0], sb1[1], sb1[3])
    (sb0, sb1, g_one.keep, g_one.send, cb0, cb1, mid0, mid1) = fence(
        sb0, sb1, g_one.keep, g_one.send, cb0, cb1, mid0, mid1
    )
    g_one.step()
    halves = run_grad("grad_cross_kv", lens, ((in_a, cb0[1]), (in_c, cb1[1])), 3 * D + PAIR, 0, full=True)
    (g_one.keep, g_one.send, halves, cb0, cb1) = fence(g_one.keep, g_one.send, halves, cb0, cb1)
    g_one.move()
    halves = run_grad(
        "grad_cross_out", lens, ((crs0[0], mid0[4]), (crs1[0], mid1[4])), 3 * D + PAIR, 2, halves
    )
    ng_self = sb0[2] + sb1[2]
    ng_mid = mid0[7] + mid1[7]
    norm_sum = jnp.concatenate([ng_self[:2], ng_mid[:2], ng_self[2:4], ng_mid[2:4]], axis=0)
    g_two = Scatter("two", *put_norm_grad(norm_sum, halves))
    g_two.move()
    (back_b, g_two.got, gtok) = fence(back_b, g_two.got, gtok)

    back_c = exchange(gtok)
    grad_frames, output = put_back(
        "put_frames",
        (back_a, slice(0, 3 * size), back_b, slice(0, 3 * size)),
        (back_a, slice(3 * size, 4 * size), back_b, slice(3 * size, 4 * size)),
    )
    g_one = g_one.finish()
    g_two = g_two.finish()
    g_norm = g_two[:, 3 * D : 3 * D + 8]
    (grad_tokens,) = put_back("put_tokens", (back_c, slice(0, size), back_c, slice(size, 2 * size)))
    return (
        output,
        grad_tokens,
        grad_frames,
        by_part(g_one[:, :ONE_OUT], 3),
        g_one[:, ONE_OUT:ONE_Q],
        g_one[:, ONE_Q:],
        by_part(g_two[:, :TWO_OUT], 2),
        g_two[:, TWO_OUT : 3 * D],
        g_fc[:, :FF].astype(f32).reshape(rows, FF_PARTS, n_all, rows).swapaxes(1, 2).reshape(rows, FF),
        g_fc[:, FF:].astype(f32).reshape(rows, FF_PARTS, D).swapaxes(0, 1).reshape(FF_PARTS * rows, D),
        g_norm[:, :4],
        g_norm[:, 4:],
    )


def solution(mesh):
    rows = P(("grp", "fsdp"), None)
    seqs = P("grp", "fsdp", None)
    return jax.shard_map(
        shards,
        mesh=mesh,
        in_specs=(seqs, seqs, P("grp"), seqs) + (rows,) * 9,
        out_specs=(seqs,) * 3 + (rows,) * 9,
        check_vma=False,
    )
```

```python
import functools

import jax
import jax.numpy as jnp
import numpy as np
from jax import lax
from jax.experimental import pallas as pl
from jax.experimental.pallas import tpu as pltpu
from jax.sharding import PartitionSpec as P

D = 768
FF = 3072
HEAD_DIM = 64
FRAMES = 1500
FRAME_SLOTS = 1536
PAIR = 2 * HEAD_DIM
PAIRS = D // PAIR
TILE = 128
ROWS = 256
KEY_CHUNK = 256
SOME = 3
FF_PARTS = FF // D

eps_norm = 1e-05
neg_big = -1e30
head_scale = 0.125
bf16 = jnp.bfloat16
f32 = jnp.float32
MIB = 1024 * 1024
COST = pl.CostEstimate(flops=1000000, bytes_accessed=1000000, transcendentals=0)

ONE_OUT = 3 * D
ONE_Q = 4 * D
ONE_NORM = 5 * D
ONE_COLS = 5 * D + 128
TWO_OUT = 2 * D


def nt(left, right):
    return lax.dot_general(left, right, (((1,), (1,)), ((), ())), preferred_element_type=f32)


def nn(left, right):
    return lax.dot_general(left, right, (((1,), (0,)), ((), ())), preferred_element_type=f32)


def normalize(stream):
    centered = stream - jnp.mean(stream, axis=-1, keepdims=True)
    scale = lax.rsqrt(jnp.mean(centered * centered, axis=-1, keepdims=True) + eps_norm)
    return centered * scale, scale


def norm_backward(normed, scale, gain, grad):
    scaled = grad * gain
    mean_scaled = jnp.mean(scaled, axis=-1, keepdims=True)
    mean_along = jnp.mean(scaled * normed, axis=-1, keepdims=True)
    return scale * (scaled - mean_scaled - normed * mean_along)


def col_sum(values):
    return jnp.sum(values, axis=0, keepdims=True)


def split_heads(block):
    lanes = lax.broadcasted_iota(jnp.int32, block.shape, 1)
    zero = jnp.zeros_like(block)
    return jnp.concatenate(
        [jnp.where(lanes < HEAD_DIM, block, zero), jnp.where(lanes < HEAD_DIM, zero, block)], axis=0
    )


def join_heads(stacked):
    width = stacked.shape[1] // 2
    return jnp.concatenate([stacked[:HEAD_DIM, :width], stacked[HEAD_DIM:, width:]], axis=0).T


def row_dots(left, right):
    prod = (left.astype(f32) * right.astype(f32)).T
    return jnp.concatenate([col_sum(prod[:HEAD_DIM]), col_sum(prod[HEAD_DIM:])], axis=1)


def seen(shape, row_start, seq_len):
    keys = lax.broadcasted_iota(jnp.int32, shape, 0)
    rows = row_start + lax.rem(lax.broadcasted_iota(jnp.int32, shape, 1), TILE)
    return (keys <= rows) & (keys < seq_len)


def each_tile(count, size, body):
    def step(i, carry):
        body(pl.ds(pl.multiple_of(i * size, size), size), i)
        return carry

    lax.fori_loop(0, count, step, 0)


def each_wide_tile(seq_len, body):
    count = pl.cdiv(seq_len, TILE)
    each_tile(count // 4, 4 * TILE, lambda rows, i: body(rows, 4 * TILE))
    for some in (2, 1):

        @pl.when(count // some % 2 == 1)
        def _():
            start = count // (2 * some) * (2 * some) * TILE
            body(pl.ds(pl.multiple_of(start, TILE), some * TILE), some * TILE)


def lane_block(index):
    return pl.ds(pl.multiple_of(index * PAIR, PAIR), PAIR)


def token_rows(ref, tile):
    count = ROWS // ref.shape[1]
    return ref[pl.ds(tile * count, count)].reshape(ROWS, D).astype(f32)


def clear(*refs):
    for ref in refs:
        ref[...] = jnp.zeros_like(ref)


scale_of_heads = functools.partial(jnp.asarray, head_scale, bf16)


def self_part_forward(
    len_ref, tok_ref, one_ref, norm_ref,
    qkv_ref, normed_one_ref, mix_ref, lse_ref, after_ref, normed_two_ref, q_two_ref,
    vt_ref,
):
    seq_len = len_ref[0]
    row_tiles = pl.cdiv(seq_len, ROWS)
    clear(normed_one_ref, mix_ref, lse_ref, normed_two_ref)

    def project(rows, i):
        normed, _ = normalize(token_rows(tok_ref, i))
        normed = (normed * norm_ref[0:1, :] + norm_ref[4:5, :]).astype(bf16)
        normed_one_ref[rows, :] = normed
        qkv_ref[rows, :] = nn(normed, one_ref[:, :ONE_OUT]).astype(bf16)

    each_tile(row_tiles, ROWS, project)

    def per_pair(pair, vt_ref, rows, tile):
        q_lanes, k_lanes, v_lanes = (lane_block(3 * pair + i) for i in range(3))
        size = (tile + 1) * TILE
        vt_ref[:, rows] = qkv_ref[rows, v_lanes].T
        queries = split_heads(qkv_ref[rows, q_lanes] * scale_of_heads())
        scores = nt(qkv_ref[:size, k_lanes], queries)
        scores = jnp.where(seen(scores.shape, tile * TILE, seq_len), scores, neg_big)
        peak = jnp.max(scores, axis=0, keepdims=True)
        probs = jnp.exp(scores - peak)
        total = col_sum(probs)
        mixed = nn(vt_ref[:, :size], probs.astype(bf16))
        mix_ref[rows, lane_block(pair)] = join_heads(mixed / total).astype(bf16)
        lse_ref[pair, tile : tile + 1, :] = peak + jnp.log(total)

    def some_pairs(step, carry):
        for tile in range(qkv_ref.shape[0] // TILE):

            @pl.when(tile * TILE < seq_len)
            def _():
                for i in range(SOME):
                    per_pair(step * SOME + i, vt_ref.at[i], slice(tile * TILE, (tile + 1) * TILE), tile)

        return carry

    lax.fori_loop(0, PAIRS // SOME, some_pairs, 0)

    def finish(rows, i):
        after = token_rows(tok_ref, i) + nn(mix_ref[rows, :], one_ref[:, ONE_OUT:ONE_Q])
        after_ref[rows, :] = after
        normed, _ = normalize(after)
        normed = (normed * norm_ref[1:2, :] + norm_ref[5:6, :]).astype(bf16)
        normed_two_ref[rows, :] = normed
        q_two_ref[rows, :] = nn(normed, one_ref[:, ONE_Q:ONE_NORM]).astype(bf16)

    each_tile(row_tiles, ROWS, finish)


PARTS = {"frames": 4, "tokens": 4, "first": 2, "second": 2, "all": 1}


def part_at(part):
    return {"frames": 0, "tokens": 3, "first": 0, "second": 1, "all": 0}[part]


def whole():
    return pl.BlockSpec(memory_space=pltpu.VMEM)


def in_smem():
    return pl.BlockSpec(memory_space=pltpu.SMEM)


def shape_of(*dims, dtype=bf16):
    return jax.ShapeDtypeStruct(dims, dtype)


def in_hbm(*dims, dtype=bf16):
    return pltpu.HBM(dims, dtype)


def run_self_forward(seq_len, arrived, part, one, norm_rows):
    blocks, size = arrived.shape[0], arrived.shape[1] // PARTS[part]
    at = part_at(part)
    rows = blocks * size
    fixed = lambda *dims: pl.BlockSpec(dims, lambda i: (0,) * len(dims), pipeline_mode=pl.Buffered(1))
    shapes = [
        in_hbm(rows, 3 * D),
        in_hbm(rows, D),
        in_hbm(rows, D),
        in_hbm(PAIRS, rows // TILE, 2 * TILE, dtype=f32),
        in_hbm(rows, D, dtype=f32),
        in_hbm(rows, D),
        in_hbm(rows, D),
    ]
    return pl.pallas_call(
        self_part_forward,
        name="self_part_forward",
        grid=(1,),
        in_specs=[
            in_smem(),
            pl.BlockSpec((blocks, size, D), lambda i: (0, at, 0), pipeline_mode=pl.Buffered(1)),
            fixed(*one.shape),
            fixed(8, D),
        ],
        out_specs=[fixed(*s.shape) for s in shapes],
        out_shape=shapes,
        scratch_shapes=[pltpu.VMEM((SOME, PAIR, rows), bf16)],
        compiler_params=pltpu.CompilerParams(vmem_limit_bytes=36 * MIB),
        cost_estimate=COST,
    )(seq_len, arrived, one, norm_rows)


def cross_forward_kernel(len_ref, frm_ref, w_ref, q_ref, out_ref, lse_ref, kv_ref, vt_ref, s_ref):
    slots = kv_ref.shape[0]
    clear(out_ref, lse_ref)
    kv_ref[...] = nn(frm_ref[...].reshape(slots, D), w_ref[...]).astype(bf16)
    vt_ref[...] = kv_ref[:, PAIR:].T
    spans = [(k, min(KEY_CHUNK, slots - k)) for k in range(0, slots, KEY_CHUNK)]

    def per_tile(rows, width):
        queries = split_heads(q_ref[rows, :] * scale_of_heads())
        peak = jnp.full((1, 2 * width), neg_big, f32)
        for start, size in spans:
            scores = nt(kv_ref[start : start + size, :PAIR], queries)
            if start + size > FRAMES:
                keys = start + lax.broadcasted_iota(jnp.int32, scores.shape, 0)
                scores = jnp.where(keys < FRAMES, scores, neg_big)
            s_ref[start : start + size, : 2 * width] = scores
            peak = jnp.maximum(peak, jnp.max(scores, axis=0, keepdims=True))
        total = jnp.zeros((1, 2 * width), f32)
        mixed = jnp.zeros((PAIR, 2 * width), f32)
        for start, size in spans:
            probs = jnp.exp(s_ref[start : start + size, : 2 * width] - peak)
            total = total + col_sum(probs)
            mixed = mixed + nn(vt_ref[:, start : start + size], probs.astype(bf16))
        out_ref[rows, :] = join_heads(mixed / total).astype(bf16)
        log_sum = peak + jnp.log(total)
        lse_ref[0, 0:1, rows] = log_sum[:, :width]
        lse_ref[0, 1:2, rows] = log_sum[:, width:]

    each_wide_tile(len_ref[0], per_tile)


def frame_rows(arrived):
    return FRAME_SLOTS // arrived.shape[0]


def run_cross_forward(seq_len, arrived, two, q_two):
    blocks, size = arrived.shape[0], frame_rows(arrived)
    rows, slots = q_two.shape[0], blocks * size
    return pl.pallas_call(
        cross_forward_kernel,
        name="cross_forward",
        grid=(PAIRS,),
        in_specs=[
            in_smem(),
            pl.BlockSpec((blocks, size, D), lambda h: (0, 0, 0), pipeline_mode=pl.Buffered(1)),
            pl.BlockSpec((D, 2 * PAIR), lambda h: (0, h)),
            pl.BlockSpec((rows, PAIR), lambda h: (0, h)),
        ],
        out_specs=[
            pl.BlockSpec((rows, PAIR), lambda h: (0, h)),
            pl.BlockSpec((1, 2, rows), lambda h: (h, 0, 0)),
            pl.BlockSpec((slots, 2 * PAIR), lambda h: (0, h)),
        ],
        out_shape=[
            in_hbm(rows, D),
            in_hbm(PAIRS, 2, rows, dtype=f32),
            in_hbm(slots, 2 * D),
        ],
        scratch_shapes=[pltpu.VMEM((PAIR, slots), bf16), pltpu.VMEM((slots, 8 * TILE), f32)],
        compiler_params=pltpu.CompilerParams(vmem_limit_bytes=24 * MIB),
        cost_estimate=COST,
    )(seq_len, arrived, two, q_two)


def cross_backward_kernel(
    len_ref, q_ref, kv_ref, mix_ref, grad_ref, lse_ref, w_ref, _,
    dq_ref, dkv_ref, dfrm_ref,
    kt_ref, dk_ref, dv_ref, acc_ref,
):
    slots = kv_ref.shape[0]
    pair = pl.program_id(0)
    kt_ref[...] = kv_ref[:, :PAIR].T
    clear(dq_ref, dk_ref, dv_ref)
    spans = [(k, min(KEY_CHUNK, slots - k)) for k in range(0, slots, KEY_CHUNK)]

    def per_tile(rows, width):
        queries = split_heads(q_ref[rows, :] * scale_of_heads())
        grads = split_heads(grad_ref[rows, :])
        inner = row_dots(mix_ref[rows, :], grad_ref[rows, :])
        lse = jnp.concatenate([lse_ref[0, 0:1, rows], lse_ref[0, 1:2, rows]], axis=1)
        dq = jnp.zeros((PAIR, 2 * width), f32)
        for start, size in spans:
            span = slice(start, start + size)
            probs = jnp.exp(nt(kv_ref[span, :PAIR], queries) - lse)
            if start + size > FRAMES:
                keys = start + lax.broadcasted_iota(jnp.int32, probs.shape, 0)
                probs = jnp.where(keys < FRAMES, probs, 0.0)
            dscores = (probs * (nt(kv_ref[span, PAIR:], grads) - inner)).astype(bf16)
            dv_ref[span, :] += nn(probs.astype(bf16), grads)
            dk_ref[span, :] += nn(dscores, queries)
            dq = dq + nn(kt_ref[:, span], dscores)
        dq_ref[rows, :] = join_heads(dq).astype(bf16) * scale_of_heads()

    each_wide_tile(len_ref[0], per_tile)
    dkv_ref[:, :PAIR] = dk_ref[...].astype(bf16)
    dkv_ref[:, PAIR:] = dv_ref[...].astype(bf16)
    part = nt(dkv_ref[...], w_ref[...])

    @pl.when(pair == 0)
    def _():
        acc_ref[...] = part

    @pl.when((pair > 0) & (pair < PAIRS - 1))
    def _():
        acc_ref[...] += part

    @pl.when(pair == PAIRS - 1)
    def _():
        dfrm_ref[...] = (acc_ref[...] + part).astype(bf16).reshape(dfrm_ref.shape)


def run_cross_backward(seq_len, q_two, kv, mix, grad_mix, lse, two, leaving):
    rows, slots, blocks = q_two.shape[0], kv.shape[0], leaving.shape[0]
    row_spec = pl.BlockSpec((rows, PAIR), lambda h: (0, h))
    kv_spec = pl.BlockSpec((slots, 2 * PAIR), lambda h: (0, h))
    return pl.pallas_call(
        cross_backward_kernel,
        name="cross_backward",
        grid=(PAIRS,),
        in_specs=[
            in_smem(),
            row_spec,
            kv_spec,
            row_spec,
            row_spec,
            pl.BlockSpec((1, 2, rows), lambda h: (h, 0, 0)),
            pl.BlockSpec((D, 2 * PAIR), lambda h: (0, h)),
            pl.BlockSpec(memory_space=pl.ANY),
        ],
        out_specs=[
            row_spec,
            kv_spec,
            pl.BlockSpec((blocks, slots // blocks, D), lambda h: (0, 0, 0), pipeline_mode=pl.Buffered(1)),
        ],
        out_shape=[in_hbm(rows, D), in_hbm(slots, 2 * D), in_hbm(*leaving.shape)],
        input_output_aliases={7: 2},
        scratch_shapes=[
            pltpu.VMEM((PAIR, slots), bf16),
            pltpu.VMEM((slots, PAIR), f32),
            pltpu.VMEM((slots, PAIR), f32),
            pltpu.VMEM((slots, D), f32),
        ],
        compiler_params=pltpu.CompilerParams(vmem_limit_bytes=36 * MIB),
        cost_estimate=COST,
    )(seq_len, q_two, kv, mix, grad_mix, lse, two, leaving)


def middle_kernel(
    len_ref, mix_ref, after_ref, cot_ref, two_ref, fc_ref, norm_ref,
    out_ref, normed_ref, hidden_ref, grad_pre_ref, branch_three_ref, branch_two_ref,
    grad_cross_ref, grad_mix_ref, norm_grad_ref,
    slope_ref,
):
    seq_len = len_ref[0]
    step = pl.program_id(0)
    parts = [(slice(k, k + D), slice(FF + k, FF + k + D)) for k in range(0, FF, D)]

    @pl.when(step == 0)
    def _():
        clear(norm_grad_ref)

    @pl.when(step * ROWS >= seq_len)
    def _():
        clear(out_ref)

    @pl.when(step * ROWS < seq_len)
    def _():
        w_out = two_ref[:, TWO_OUT:]
        after_cross = after_ref[...] + nn(mix_ref[...], w_out)
        n_three, scale_three = normalize(after_cross)
        normed = (n_three * norm_ref[2:3, :] + norm_ref[6:7, :]).astype(bf16)
        normed_ref[...] = normed
        mlp = jnp.zeros((ROWS, D), f32)
        for span, rows_out in parts:
            pre = nn(normed, fc_ref[:, span])
            below = 0.5 * (1.0 + lax.erf(pre * np.float32(np.sqrt(0.5))))
            density = jnp.exp(-0.5 * pre * pre) * np.float32(1.0 / np.sqrt(2.0 * np.pi))
            slope_ref[:, span] = below + pre * density
            hidden = (pre * below).astype(bf16)
            hidden_ref[:, span] = hidden
            mlp = mlp + nn(hidden, fc_ref[:, rows_out])
        n_four, scale_four = normalize(after_cross + mlp)
        row_ids = step * ROWS + lax.broadcasted_iota(jnp.int32, (ROWS, 1), 0)
        valid = (row_ids < seq_len).astype(f32)
        output = ((n_four * norm_ref[3:4, :] + norm_ref[7:8, :]) * valid).astype(bf16)
        out_ref[...] = output.reshape(out_ref.shape)

        grad = cot_ref[...].reshape(ROWS, D).astype(f32) * valid
        norm_grad_ref[1:2, :] += col_sum(grad * n_four)
        norm_grad_ref[3:4, :] += col_sum(grad)
        grad_mlp = norm_backward(n_four, scale_four, norm_ref[3:4, :], grad)
        branch_three = grad_mlp.astype(bf16)
        branch_three_ref[...] = branch_three
        back = jnp.zeros((ROWS, D), f32)
        for span, rows_out in parts:
            grad_pre = (nt(branch_three, fc_ref[:, rows_out]) * slope_ref[:, span]).astype(bf16)
            grad_pre_ref[:, span] = grad_pre
            back = back + nt(grad_pre, fc_ref[:, span])
        norm_grad_ref[0:1, :] += col_sum(back * n_three)
        norm_grad_ref[2:3, :] += col_sum(back)
        grad_cross = grad_mlp + norm_backward(n_three, scale_three, norm_ref[2:3, :], back)
        grad_cross_ref[...] = grad_cross
        branch_two = grad_cross.astype(bf16)
        branch_two_ref[...] = branch_two
        grad_mix_ref[...] = nt(branch_two, w_out).astype(bf16)


def run_middle(seq_len, mix, after, arrived, part, two, fc, norm_rows):
    rows, blocks = mix.shape[0], arrived.shape[0]
    size = rows // blocks
    at = part_at(part)
    count = ROWS // size
    last = lambda i, n: jnp.minimum(i, (n[0] - 1) // ROWS)
    row_spec = pl.BlockSpec((ROWS, D), lambda i, n: (last(i, n), 0))
    wide_spec = pl.BlockSpec((ROWS, FF), lambda i, n: (last(i, n), 0))

    def fixed(*dims):
        return pl.BlockSpec(dims, lambda i, n: (0, 0), pipeline_mode=pl.Buffered(1))

    return pl.pallas_call(
        middle_kernel,
        name="mlp_and_back",
        grid_spec=pltpu.PrefetchScalarGridSpec(
            num_scalar_prefetch=1,
            grid=(rows // ROWS,),
            in_specs=[
                row_spec, row_spec, pl.BlockSpec((count, size, D), lambda i, n: (last(i, n), at, 0)),
                fixed(D, 3 * D), fixed(D, 2 * FF), fixed(8, D),
            ],
            out_specs=[pl.BlockSpec((count, size, D), lambda i, n: (i, 3, 0)), row_spec, wide_spec, wide_spec, row_spec, row_spec, row_spec, row_spec,
                   pl.BlockSpec((8, D), lambda i, n: (0, 0))],
            scratch_shapes=[pltpu.VMEM((ROWS, FF), f32)],
        ),
        out_shape=[
            in_hbm(blocks, 4 * size, D), in_hbm(rows, D), in_hbm(rows, FF), in_hbm(rows, FF),
            in_hbm(rows, D), in_hbm(rows, D), in_hbm(rows, D, dtype=f32), in_hbm(rows, D),
            in_hbm(8, D, dtype=f32),
        ],
        compiler_params=pltpu.CompilerParams(vmem_limit_bytes=48 * MIB),
        cost_estimate=COST,
    )(seq_len, mix, after, arrived, two, fc, norm_rows)


def self_part_backward(
    len_ref, dq_ref, grad_cross_ref, after_ref, qkv_ref, mix_ref, lse_ref, tok_ref, one_ref, norm_ref, _,
    branch_ref, dqkv_ref, grad_tok_ref, norm_grad_ref,
    attn_ref, grad_mix_ref, kt_ref, dk_ref, dv_ref,
):
    seq_len = len_ref[0]
    row_tiles = pl.cdiv(seq_len, ROWS)
    clear(branch_ref, dqkv_ref, grad_tok_ref, norm_grad_ref)

    def enter(rows, _):
        normed, scale = normalize(after_ref[rows, :])
        grad = nt(dq_ref[rows, :], one_ref[:, ONE_Q:ONE_NORM])
        norm_grad_ref[1:2, :] += col_sum(grad * normed)
        norm_grad_ref[3:4, :] += col_sum(grad)
        attn = grad_cross_ref[rows, :] + norm_backward(normed, scale, norm_ref[1:2, :], grad)
        attn_ref[rows, :] = attn
        branch = attn.astype(bf16)
        branch_ref[rows, :] = branch
        grad_mix_ref[rows, :] = nt(branch, one_ref[:, ONE_OUT:ONE_Q]).astype(bf16)

    each_tile(row_tiles, ROWS, enter)

    def per_pair(pair, kt_ref, dk_ref, dv_ref, rows, tile):
        q_lanes, k_lanes, v_lanes = (lane_block(3 * pair + i) for i in range(3))
        size = (tile + 1) * TILE
        kt_ref[:, rows] = qkv_ref[rows, k_lanes].T
        queries = split_heads(qkv_ref[rows, q_lanes] * scale_of_heads())
        grad_mix = grad_mix_ref[rows, lane_block(pair)]
        grads = split_heads(grad_mix)
        inner = row_dots(mix_ref[rows, lane_block(pair)], grad_mix)
        scores = nt(qkv_ref[:size, k_lanes], queries)
        scores = jnp.where(seen(scores.shape, tile * TILE, seq_len), scores, neg_big)
        probs = jnp.exp(scores - lse_ref[pair, tile : tile + 1, :])
        dscores = (probs * (nt(qkv_ref[:size, v_lanes], grads) - inner)).astype(bf16)
        dv_ref[:size, :] += nn(probs.astype(bf16), grads)
        dk_ref[:size, :] += nn(dscores, queries)
        dq = nn(kt_ref[:, :size], dscores)
        dqkv_ref[rows, q_lanes] = join_heads(dq).astype(bf16) * scale_of_heads()

    def some_pairs(step, carry):
        clear(dk_ref, dv_ref)
        for tile in range(qkv_ref.shape[0] // TILE):

            @pl.when(tile * TILE < seq_len)
            def _():
                for i in range(SOME):
                    rows = slice(tile * TILE, (tile + 1) * TILE)
                    per_pair(step * SOME + i, kt_ref.at[i], dk_ref.at[i], dv_ref.at[i], rows, tile)

        for i in range(SOME):
            pair = step * SOME + i
            dqkv_ref[:, lane_block(3 * pair + 1)] = dk_ref[i].astype(bf16)
            dqkv_ref[:, lane_block(3 * pair + 2)] = dv_ref[i].astype(bf16)
        return carry

    lax.fori_loop(0, PAIRS // SOME, some_pairs, 0)

    def leave(rows, i):
        normed, scale = normalize(token_rows(tok_ref, i))
        grad = nt(dqkv_ref[rows, :], one_ref[:, :ONE_OUT])
        norm_grad_ref[0:1, :] += col_sum(grad * normed)
        norm_grad_ref[2:3, :] += col_sum(grad)
        total = attn_ref[rows, :] + norm_backward(normed, scale, norm_ref[0:1, :], grad)
        count = ROWS // grad_tok_ref.shape[1]
        grad_tok_ref[pl.ds(i * count, count)] = total.astype(bf16).reshape(count, -1, D)

    each_tile(row_tiles, ROWS, leave)


def run_self_backward(seq_len, dq, grad_cross, after, qkv, mix, lse, arrived, part, one, norm_rows, leaving, slot):
    blocks, size = arrived.shape[0], arrived.shape[1] // PARTS[part]
    at = part_at(part)
    rows = blocks * size
    fixed = lambda *dims: pl.BlockSpec(dims, lambda i: (0,) * len(dims), pipeline_mode=pl.Buffered(1))
    spec = lambda block: pl.BlockSpec(
        (blocks, size, D), lambda i: (0, block, 0), pipeline_mode=pl.Buffered(1)
    )
    before = [] if leaving is None else [leaving]
    body = self_part_backward
    if leaving is None:
        body = lambda *refs: self_part_backward(*refs[:10], None, *refs[10:])
    return pl.pallas_call(
        body,
        name="self_part_backward",
        grid=(1,),
        in_specs=[in_smem()]
        + [fixed(*a.shape) for a in (dq, grad_cross, after, qkv, mix, lse)]
        + [spec(at), fixed(*one.shape), fixed(8, D)]
        + [anywhere()] * len(before),
        out_specs=[fixed(rows, D), fixed(rows, 3 * D), spec(slot), fixed(8, D)],
        out_shape=[
            in_hbm(rows, D),
            in_hbm(rows, 3 * D),
            in_hbm(blocks, 2 * size, D),
            in_hbm(8, D, dtype=f32),
        ],
        input_output_aliases={10: 2} if before else {},
        scratch_shapes=[
            pltpu.VMEM((rows, D), f32),
            pltpu.VMEM((rows, D), bf16),
            pltpu.VMEM((SOME, PAIR, rows), bf16),
            pltpu.VMEM((SOME, rows, PAIR), f32),
            pltpu.VMEM((SOME, rows, PAIR), f32),
        ],
        compiler_params=pltpu.CompilerParams(vmem_limit_bytes=40 * MIB),
        cost_estimate=COST,
    )(seq_len, dq, grad_cross, after, qkv, mix, lse, arrived, one, norm_rows, *before)


def anywhere():
    return pl.BlockSpec(memory_space=pl.ANY)


def copy_kernel(plan, n_in, n_out, scalar_ref, *refs):
    ins, outs, sem = refs[:n_in], refs[n_in : n_in + n_out], refs[-1]
    for which, src, dst in plan(scalar_ref, ins, outs):
        pltpu.make_async_copy(src, dst, sem.at[which]).start()
    for which, out in enumerate(outs):
        pltpu.make_async_copy(out, out, sem.at[which]).wait()


def run_copies(name, plan, scalars, ins, out_shapes, stage="in"):
    vmem = pl.BlockSpec(memory_space=pltpu.VMEM)
    return pl.pallas_call(
        functools.partial(copy_kernel, plan, len(ins), len(out_shapes)),
        name=name,
        in_specs=[in_smem()] + [vmem if stage == "in" else pl.BlockSpec(memory_space=pltpu.HBM)] * len(ins),
        out_specs=[vmem if stage == "out" else anywhere()] * len(out_shapes),
        out_shape=out_shapes,
        scratch_shapes=[pltpu.SemaphoreType.DMA((len(out_shapes),))],
        compiler_params=pltpu.CompilerParams(vmem_limit_bytes=16 * MIB),
        cost_estimate=pl.CostEstimate(flops=0, bytes_accessed=1000, transcendentals=0),
    )(scalars, *ins)


def device_bits():
    return [
        (axis, b)
        for axis in ("grp", "fsdp")
        for b in reversed(range(lax.axis_size(axis).bit_length() - 1))
    ]


def swap(array, axis, b):
    return lax.ppermute(array, axis, [(i, i ^ (1 << b)) for i in range(lax.axis_size(axis))])


def bit_mask(axis, b):
    return (1 << b) if axis == "fsdp" else lax.axis_size("fsdp") << b


def my_bit(axis, b):
    return (lax.axis_index(axis) >> b) & 1


class Gather:
    def __init__(self, name, shard, me, outs, pieces):
        self.name = name
        bits = device_bits()
        self.left = [p for p in bits if p[0] == "fsdp"] + [p for p in bits if p[0] == "grp"]
        self.masks = [0]
        self.value = shard[None]
        self.me = me
        self.outs = outs
        self.pieces = pieces
        self.got = None

    def send(self):
        self.got = swap(self.value, *self.left[0])

    def take(self):
        mask = bit_mask(*self.left.pop(0))
        masks = self.masks
        self.masks = masks + [mask ^ m for m in masks]
        k = len(masks)
        if self.left:

            def plan(_, ins, outs):
                return [(0, ins[0], outs[0].at[:k]), (0, ins[1], outs[0].at[k:])]

            shape = (2 * k,) + self.value.shape[1:]
            (self.value,) = run_copies(
                self.name + "_join", plan, self.me, [self.value, self.got], [in_hbm(*shape)]
            )
            return self.value

        def plan(me_ref, ins, outs):
            me = me_ref[0]
            return [
                (which, src, dst)
                for i in range(k)
                for half, src_ref in ((0, ins[0]), (k, ins[1]))
                for which, src, dst in self.pieces(src_ref.at[i], outs, me ^ self.masks[half + i])
            ]

        self.value = run_copies(
            self.name + "_order", plan, self.me, [self.value, self.got], self.outs
        )
        return self.value

    def step(self):
        self.send()
        return self.take()


def pack_shards(me, self_in, self_out, cross_q, norms, cross_kv, cross_out):
    rows = self_in.shape[0]

    def plan(_, ins, outs):
        w_in, w_out, w_q, w_norm, w_kv, w_cross = ins
        one, two = outs
        copies = []
        for pair in range(PAIRS):
            for o, w, parts in ((0, w_in, 3), (1, w_kv, 2)):
                for part in range(parts):
                    src = w.at[:, part * D + pair * PAIR : part * D + (pair + 1) * PAIR]
                    at = (parts * pair + part) * PAIR
                    copies.append((o, src, outs[o].at[:, at : at + PAIR]))
        copies.append((0, w_out, one.at[:, ONE_OUT:ONE_Q]))
        copies.append((0, w_q, one.at[:, ONE_Q:ONE_NORM]))
        copies.append((0, w_norm, one.at[:, ONE_NORM:]))
        copies.append((1, w_cross, two.at[:, TWO_OUT:]))
        return copies

    ins = [self_in, self_out, cross_q, norms, cross_kv, cross_out]
    shapes = [in_hbm(rows, ONE_COLS), in_hbm(rows, 3 * D)]
    return run_copies("pack_shards", plan, me, ins, shapes, "out")


def gather_rows(shard):
    return lax.all_gather(shard, ("grp", "fsdp"), axis=0, tiled=True)


def grad_kernel(
    full, len0_ref, len1_ref, bit_ref, left0_ref, right0_ref, left1_ref, right1_ref, *refs
):
    keep_ref, send_ref, flip_ref, acc_ref = refs[-4:]
    half, count = keep_ref.shape[1], right0_ref.shape[0]
    sides = (
        (len0_ref[0], left0_ref, right0_ref, 0),
        (len1_ref[0], left1_ref, right1_ref, count),
    )
    tiles = [slice(k, k + ROWS) for k in range(0, count, ROWS)]

    @pl.when(pl.program_id(0) == 0)
    def _():
        for seq_len, left_ref, _, at in sides:
            for tile in tiles:

                @pl.when(jnp.logical_or(full or tile.start == 0, tile.start < seq_len))
                def _():
                    if len(left_ref.shape) == 3:
                        size = left_ref.shape[1]
                        left = left_ref[tile.start // size : (tile.stop + size - 1) // size]
                        skip = tile.start % size
                        left = left.reshape(-1, D)[skip : skip + ROWS]
                    else:
                        left = left_ref[tile, :]
                    flip_ref[:, at + tile.start : at + tile.stop] = left.T

    if full:
        acc_ref[...] = nn(flip_ref[:, :count], right0_ref[...]) + nn(
            flip_ref[:, count:], right1_ref[...]
        )
    else:
        acc_ref[...] = nn(flip_ref[:, :ROWS], right0_ref[:ROWS, :]) + nn(
            flip_ref[:, count : count + ROWS], right1_ref[:ROWS, :]
        )
        for seq_len, _, right_ref, at in sides:
            for tile in tiles[1:]:

                @pl.when(tile.start < seq_len)
                def _():
                    acc_ref[...] += nn(flip_ref[:, at + tile.start : at + tile.stop], right_ref[tile, :])

    for i in range(keep_ref.shape[0]):
        for out_ref, bit in ((keep_ref, bit_ref[0]), (send_ref, 1 - bit_ref[0])):
            at = pl.multiple_of((2 * i + bit) * half, half)
            out_ref[i] = acc_ref[pl.ds(at, half), :].astype(bf16)


def fc_grad_kernel(
    len0_ref, len1_ref, normed0_ref, pre0_ref, hid0_ref, branch0_ref, normed1_ref, pre1_ref, hid1_ref, branch1_ref,
    out_ref, flip_ref, acc_ref,
):
    step = pl.program_id(0)
    count = normed0_ref.shape[0]
    tiles = [slice(k, k + ROWS) for k in range(0, count, ROWS)]
    sides = (
        (len0_ref[0], normed0_ref, pre0_ref, hid0_ref, branch0_ref, 0),
        (len1_ref[0], normed1_ref, pre1_ref, hid1_ref, branch1_ref, count),
    )

    def flip(pick):
        for side in sides:
            for tile in tiles:

                @pl.when(jnp.logical_or(tile.start == 0, tile.start < side[0]))
                def _():
                    flip_ref[:, side[5] + tile.start : side[5] + tile.stop] = side[pick][tile, :].T

    def multiply(pick):
        acc_ref[...] = nn(flip_ref[:, :ROWS], sides[0][pick][:ROWS, :]) + nn(
            flip_ref[:, count : count + ROWS], sides[1][pick][:ROWS, :]
        )
        for side in sides:
            for tile in tiles[1:]:

                @pl.when(tile.start < side[0])
                def _():
                    at = side[5]
                    acc_ref[...] += nn(flip_ref[:, at + tile.start : at + tile.stop], side[pick][tile, :])

        out_ref[...] = acc_ref[...].astype(bf16)

    @pl.when(step == 0)
    def _():
        flip(1)

    @pl.when(step < FF_PARTS)
    def _():
        multiply(2)

    @pl.when(step >= FF_PARTS)
    def _():
        flip(3)
        multiply(4)


def norm_grad_kernel(bit_ref, norm_ref, _, __, keep_ref, send_ref, flip_ref):
    flip_ref[...] = jnp.concatenate([norm_ref[...], jnp.zeros((PAIR - 8, D), f32)], axis=0).T
    size = keep_ref.shape[1]
    for i in range(keep_ref.shape[0]):
        for out_ref, bit in ((keep_ref, bit_ref[0]), (send_ref, 1 - bit_ref[0])):
            at = pl.multiple_of((2 * i + bit) * size, size)
            out_ref[i] = flip_ref[pl.ds(at, size), :].astype(bf16)


def put_norm_grad(norm_sum, halves):
    count, size, cols = halves[0].shape
    spec = pl.BlockSpec((count, size, PAIR), lambda i: (0, 0, cols // PAIR - 1))
    return pl.pallas_call(
        norm_grad_kernel,
        name="put_norm_grad",
        grid=(1,),
        in_specs=[in_smem(), pl.BlockSpec((8, D), lambda i: (0, 0)), anywhere(), anywhere()],
        out_specs=[spec, spec],
        out_shape=[in_hbm(*h.shape) for h in halves],
        input_output_aliases={2: 0, 3: 1},
        scratch_shapes=[pltpu.VMEM((D, PAIR), f32)],
        compiler_params=pltpu.CompilerParams(vmem_limit_bytes=8 * MIB),
        cost_estimate=COST,
    )(my_bit("grp", 0).reshape(1), norm_sum, *halves)


def run_fc_grad(lens, side0, side1):
    count = side0[0].shape[0]
    whole_spec = pl.BlockSpec((count, D), lambda i: (0, 0), pipeline_mode=pl.Buffered(1))
    pre_spec = pl.BlockSpec((count, D), lambda i: (0, jnp.minimum(i, FF_PARTS - 1)))
    hid_spec = pl.BlockSpec((count, D), lambda i: (0, jnp.maximum(i - FF_PARTS, 0)))
    return pl.pallas_call(
        fc_grad_kernel,
        name="grad_fc",
        grid=(2 * FF_PARTS,),
        in_specs=[in_smem()] * 2 + [whole_spec, pre_spec, hid_spec, whole_spec] * 2,
        out_specs=pl.BlockSpec((D, D), lambda i: (0, i)),
        out_shape=in_hbm(D, 2 * FF),
        scratch_shapes=[pltpu.VMEM((D, 2 * count), bf16), pltpu.VMEM((D, D), f32)],
        compiler_params=pltpu.CompilerParams(vmem_limit_bytes=32 * MIB),
        cost_estimate=COST,
    )(*lens, *side0, *side1)


def run_grad(name, lens, pairs, cols, at, before=(), full=False):
    (left0, right0), (left1, right1) = pairs
    count, wide = right0.shape
    tall = D
    n_grp = lax.axis_size("grp")
    def left_spec(left):
        if left.ndim == 3:
            block = (left.shape[0], frame_rows(left), D)
            return pl.BlockSpec(block, lambda n: (0, 0, 0), pipeline_mode=pl.Buffered(1))
        return pl.BlockSpec((count, tall), lambda n: (0, 0), pipeline_mode=pl.Buffered(1))

    right_spec = pl.BlockSpec((count, D), lambda n: (0, n))
    out_spec = pl.BlockSpec((n_grp // 2, tall // n_grp, D), lambda n: (0, 0, n + at))
    shape = in_hbm(n_grp // 2, tall // n_grp, cols)
    bit = my_bit("grp", 0).reshape(1)
    return pl.pallas_call(
        functools.partial(grad_kernel, full),
        name=name,
        grid=(wide // D,),
        in_specs=[in_smem()] * 3
        + [left_spec(left0), right_spec, left_spec(left1), right_spec]
        + [anywhere()] * len(before),
        out_specs=[out_spec, out_spec],
        out_shape=[shape, shape],
        input_output_aliases={7: 0, 8: 1} if before else {},
        scratch_shapes=[pltpu.VMEM((tall, 2 * count), bf16), pltpu.VMEM((tall, D), f32)],
        compiler_params=pltpu.CompilerParams(vmem_limit_bytes=48 * MIB),
        cost_estimate=COST,
    )(*lens, bit, left0, right0, left1, right1, *before)


def add_split_kernel(me_ref, kept_ref, got_ref, keep_ref, send_ref):
    for out_ref, half in ((keep_ref, me_ref[0]), (send_ref, 1 - me_ref[0])):
        total = kept_ref[0, half].astype(f32) + got_ref[0, half].astype(f32)
        out_ref[0] = total.astype(out_ref.dtype)


def add_kernel(kept_ref, got_ref, out_ref):
    out_ref[...] = kept_ref[...].astype(f32) + got_ref[...].astype(f32)


class Scatter:
    def __init__(self, name, keep, send):
        self.name = name
        self.held = device_bits()
        self.order = [p for p in reversed(self.held) if p[0] == "grp"]
        self.order += [p for p in reversed(self.held) if p[0] == "fsdp"]
        self.split()
        blocks = 1 << len(self.held)
        self.keep, self.send = (a.reshape(blocks, -1, a.shape[-1]) for a in (keep, send))
        self.block = self.keep.shape[1:]

    def split(self):
        self.bit = self.order.pop(0)
        dim = self.held.index(self.bit)
        self.held.remove(self.bit)
        return 1 << dim, 1 << (len(self.held) - dim)

    def move(self):
        self.got = swap(self.send, *self.bit)

    def step(self):
        self.move()
        return self.take()

    def take(self):
        got = self.got
        if not self.order:
            spec = pl.BlockSpec((1,) + self.block, lambda i: (0, 0, 0))
            return pl.pallas_call(
                add_kernel,
                name=self.name + "_sum",
                grid=(1,),
                in_specs=[spec, spec],
                out_specs=spec,
                out_shape=shape_of(1, *self.block, dtype=f32),
                compiler_params=pltpu.CompilerParams(vmem_limit_bytes=8 * MIB),
                cost_estimate=COST,
            )(self.keep, got).reshape(self.block)
        before, after = self.split()
        half = self.keep.shape[0] // 2
        view = (before, 2, after) + self.block
        some = min(after, 4)
        in_spec = pl.BlockSpec((1, 2, some) + self.block, lambda i, j, _: (i, 0, j, 0, 0))
        out_spec = pl.BlockSpec((1, some) + self.block, lambda i, j, _: (i, j, 0, 0))
        shape = shape_of(before, after, *self.block, dtype=self.keep.dtype)
        keep, send = pl.pallas_call(
            add_split_kernel,
            name=self.name + "_add",
            grid_spec=pltpu.PrefetchScalarGridSpec(
                num_scalar_prefetch=1,
                grid=(before, after // some),
                in_specs=[in_spec, in_spec],
                out_specs=[out_spec, out_spec],
            ),
            out_shape=[shape, shape],
            compiler_params=pltpu.CompilerParams(vmem_limit_bytes=16 * MIB),
            cost_estimate=COST,
        )(my_bit(*self.bit).reshape(1), self.keep.reshape(view), got.reshape(view))
        self.keep, self.send = (a.reshape((half,) + self.block) for a in (keep, send))

    def finish(self):
        while True:
            done = self.take()
            if done is not None:
                return done
            self.move()


def fence(*values):
    return lax.optimization_barrier(values)


def by_part(weight, parts):
    rows = weight.shape[0]
    return weight.reshape(rows, PAIRS, parts, PAIR).swapaxes(1, 2).reshape(rows, parts * D)


def rows_of(array):
    return array.reshape(-1, array.shape[-1])


def exchange(array):
    return lax.all_to_all(array, "fsdp", split_axis=0, concat_axis=0, tiled=True)


def shards(
    tokens,
    frames,
    lengths,
    cotangent,
    self_in,
    self_out,
    cross_q,
    cross_kv,
    cross_out,
    fc_in,
    fc_out,
    norm_gain,
    norm_bias,
):
    fsdp_count = lax.axis_size("fsdp")
    n_all = lax.axis_size("grp") * fsdp_count
    group_seqs, size = tokens.shape[:2]
    seq_ids = jnp.arange(group_seqs, dtype=jnp.int32)
    rank_order = jnp.argsort(-(lengths * group_seqs + (group_seqs - 1 - seq_ids)))
    sender = jnp.concatenate([rank_order[:fsdp_count], rank_order[fsdp_count:][::-1]])
    device = lax.axis_index("fsdp")
    len0, len1 = (
        lax.dynamic_slice_in_dim(lengths[sender], s * fsdp_count + device, 1) for s in range(2)
    )
    rows = self_in.shape[0]
    me = (lax.axis_index("grp") * fsdp_count + device).reshape(1)

    def pick(name, *parts):
        total = sum(array.shape[1] for array, _ in parts)

        def plan(seq_ref, ins, outs):
            copies, at = [], 0
            for src, (array, slot) in zip(ins, parts):
                span = slice(at, at + array.shape[1])
                at += array.shape[1]
                for j in range(fsdp_count):
                    seq = seq_ref[slot * fsdp_count + j]
                    copies.append((0, src.at[seq], outs[0].at[j, span]))
            return copies

        shape = in_hbm(fsdp_count, total, D)
        return run_copies(name, plan, sender, [array for array, _ in parts], [shape], "out")[0]

    def put_back(name, *parts):
        ins = []
        for first, _, second, _ in parts:
            ins += [a for a in (first, second) if not any(a is b for b in ins)]
        where = [[next(i for i, a in enumerate(ins) if a is p[k]) for k in (0, 2)] for p in parts]

        def plan(seq_ref, in_refs, outs):
            return [
                (o, in_refs[where[o][slot]].at[j, part[2 * slot + 1]], outs[o].at[seq_ref[slot * fsdp_count + j]])
                for o, part in enumerate(parts)
                for slot in range(2)
                for j in range(fsdp_count)
            ]

        shapes = [in_hbm(group_seqs, p[1].stop - p[1].start, D) for p in parts]
        return run_copies(name, plan, sender, ins, shapes)

    norms = jnp.pad(jnp.concatenate([norm_gain, norm_bias], axis=1), ((0, 0), (0, 120)))
    shard_one, shard_two = pack_shards(me, self_in, self_out, cross_q, norms, cross_kv, cross_out)
    w_two = gather_rows(shard_two)
    one = Gather(
        "one", shard_one, me, [in_hbm(n_all, rows, ONE_COLS)],
        lambda src, outs, b: [(0, src, outs[0].at[b])],
    )

    pick_t = pick("pick_tokens", (tokens, 0), (tokens, 1))
    far = sum(1 for axis, _ in device_bits() if axis == "fsdp")
    one.step()
    (one.value, pick_t, fc_in, fc_out) = fence(one.value, pick_t, fc_in, fc_out)
    fc_up = fc_in.reshape(rows, n_all, FF_PARTS, rows).swapaxes(1, 2).reshape(rows, FF)
    fc_down = fc_out.reshape(FF_PARTS, rows, D).swapaxes(0, 1).reshape(rows, FF)
    w_fc = gather_rows(jnp.concatenate([fc_up, fc_down], axis=1))
    for _ in range(far - 2):
        one.step()
        (one.value, pick_t) = fence(one.value, pick_t)
    in_t = exchange(pick_t)
    pick_a = pick("pick_frames", (frames, 0))
    one.step()
    (one.value, in_t, pick_a) = fence(one.value, in_t, pick_a)
    in_a = exchange(pick_a)
    while len(one.left) > 1:
        one.send()
        pick_b = pick("pick_cotangent", (cotangent, 0))
        pick_c = pick("pick_third", (frames, 1), (cotangent, 1))
        (one.value, one.got, pick_b, pick_c) = fence(one.value, one.got, pick_b, pick_c)
        one.take()
    (w_one,) = one.step()
    (w_one, in_t) = fence(w_one, in_t)
    w_one = rows_of(w_one)
    norm_rows = w_one[:, ONE_NORM : ONE_NORM + 8].T.astype(f32)

    fwd0 = run_self_forward(len0, in_t, "first", w_one, norm_rows)
    fwd1 = run_self_forward(len1, in_t, "second", w_one, norm_rows)
    (in_a, fwd0, fwd1, pick_b) = fence(in_a, fwd0, fwd1, pick_b)
    in_b = exchange(pick_b)
    crs0 = run_cross_forward(len0, in_a, w_two, fwd0[6])
    (in_b, fwd0, crs0, pick_c) = fence(in_b, fwd0, crs0, pick_c)

    in_c = exchange(pick_c)
    mid0 = run_middle(len0, crs0[0], fwd0[4], in_b, "all", w_two, w_fc, norm_rows)
    cb0 = run_cross_backward(len0, fwd0[6], crs0[2], crs0[0], mid0[7], crs0[1], w_two, mid0[0])
    mid0 = mid0[1:]
    (in_c, crs0, cb0, fwd1, mid0) = fence(in_c, crs0, cb0, fwd1, mid0)

    lens = (len0, len1)

    back_a = exchange(cb0[2])
    crs1 = run_cross_forward(len1, in_c, w_two, fwd1[6])
    mid1 = run_middle(len1, crs1[0], fwd1[4], in_c, "tokens", w_two, w_fc, norm_rows)
    leaving, mid1 = mid1[0], mid1[1:]
    fc_sides = [(mid[0], mid[2], mid[1], mid[3]) for mid in (mid0, mid1)]
    g_fc = run_fc_grad(lens, *fc_sides)
    (crs1, mid1, g_fc, leaving) = fence(crs1, mid1, g_fc, leaving)
    g_fc = lax.psum_scatter(g_fc, ("grp", "fsdp"), scatter_dimension=0, tiled=True)
    cb1 = run_cross_backward(len1, fwd1[6], crs1[2], crs1[0], mid1[6], crs1[1], w_two, leaving)
    (back_a, cb0, cb1, mid0, mid1) = fence(back_a, cb0, cb1, mid0, mid1)

    back_b = exchange(cb1[2])
    halves = run_grad("grad_cross_kv", lens, ((in_a, cb0[1]), (in_c, cb1[1])), 3 * D, 0, full=True)
    halves = run_grad(
        "grad_cross_out", lens, ((crs0[0], mid0[4]), (crs1[0], mid1[4])), 3 * D, 2, halves
    )
    g_two = Scatter("two", *halves)
    g_two.step()
    (g_two.keep, g_two.send, cb0, cb1) = fence(g_two.keep, g_two.send, cb0, cb1)
    g_two.move()
    sb0 = run_self_backward(
        len0, cb0[0], mid0[5], fwd0[4], fwd0[0], fwd0[2], fwd0[3], in_t, "first", w_one, norm_rows, None, 0
    )
    sb1 = run_self_backward(
        len1, cb1[0], mid1[5], fwd1[4], fwd1[0], fwd1[2], fwd1[3], in_t, "second", w_one, norm_rows, sb0[2], 1
    )
    sb0 = (sb0[0], sb0[1], sb1[2], sb0[3])
    (sb0, sb1, g_two.got) = fence(sb0, sb1, g_two.got)
    g_two.take()
    halves = run_grad("grad_self_in", lens, ((fwd0[1], sb0[1]), (fwd1[1], sb1[1])), 5 * D + PAIR, 0)
    halves = run_grad("grad_self_out", lens, ((fwd0[2], sb0[0]), (fwd1[2], sb1[0])), 5 * D + PAIR, 3, halves)
    halves = run_grad("grad_cross_q", lens, ((fwd0[5], cb0[0]), (fwd1[5], cb1[0])), 5 * D + PAIR, 4, halves)
    ng_self = sb0[3] + sb1[3]
    ng_mid = mid0[7] + mid1[7]
    norm_sum = jnp.concatenate([ng_self[:2], ng_mid[:2], ng_self[2:4], ng_mid[2:4]], axis=0)
    g_one = Scatter("one", *put_norm_grad(norm_sum, halves))
    gtok = sb1[2]
    g_one.step()
    (g_one.keep, g_one.send, back_b, gtok) = fence(g_one.keep, g_one.send, back_b, gtok)
    g_one.move()
    g_two.move()

    back_c = exchange(gtok)
    grad_frames, output = put_back(
        "put_frames",
        (back_a, slice(0, 3 * size), back_b, slice(0, 3 * size)),
        (back_a, slice(3 * size, 4 * size), back_b, slice(3 * size, 4 * size)),
    )
    g_one = g_one.finish()
    g_two = g_two.finish()
    g_norm = g_one[:, 5 * D : 5 * D + 8]
    (grad_tokens,) = put_back("put_tokens", (back_c, slice(0, size), back_c, slice(size, 2 * size)))
    return (
        output,
        grad_tokens,
        grad_frames,
        by_part(g_one[:, :ONE_OUT], 3),
        g_one[:, ONE_OUT:ONE_Q],
        g_one[:, ONE_Q:ONE_NORM],
        by_part(g_two[:, :TWO_OUT], 2),
        g_two[:, TWO_OUT:],
        g_fc[:, :FF].astype(f32).reshape(rows, FF_PARTS, n_all, rows).swapaxes(1, 2).reshape(rows, FF),
        g_fc[:, FF:].astype(f32).reshape(rows, FF_PARTS, D).swapaxes(0, 1).reshape(FF_PARTS * rows, D),
        g_norm[:, :4],
        g_norm[:, 4:],
    )


def solution(mesh):
    rows = P(("grp", "fsdp"), None)
    seqs = P("grp", "fsdp", None)
    return jax.shard_map(
        shards,
        mesh=mesh,
        in_specs=(seqs, seqs, P("grp"), seqs) + (rows,) * 9,
        out_specs=(seqs,) * 3 + (rows,) * 9,
        check_vma=False,
    )
```
